32 devices in a mesh: elem: 16 (over z, x, core), head: 2 (over y).
Axes of the slice: x: 2, y: 2, z: 4, core: 2. Of those that a mesh axis runs over, the one named last changes fastest.
Arguments:
- features: bfloat16 [16384, 512], P('elem'), may hold values from -6 to 6
- out_grad: bfloat16 [16384, 512], P('elem'), may hold values from -6 to 6
- bin_order: int32 [16384], P('elem'), may hold values from 0 to 16383, as said below
- key_lists: int32 [128, 12], P('elem'), may hold values from 0 to 127, as said below
- list_counts: int32 [128], P('elem'), may hold values from 1 to 12, as said below
- attn_gain: float32 [512], replicated, may hold values from 0.1 to 1.9
- query_weight: bfloat16 [512, 512], P(None, 'head')
- key_weight: bfloat16 [512, 512], P(None, 'head')
- value_weight: bfloat16 [512, 512], P(None, 'head'), may hold values from -0.25 to 0.25
- out_weight: bfloat16 [512, 512], P('head'), may hold values from -0.25 to 0.25
- ffn_gain: float32 [512], replicated, may hold values from 0.1 to 1.9
- ffn_in: bfloat16 [512, 2048], P(None, 'head'), may hold values from -0.25 to 0.25
- ffn_out: bfloat16 [2048, 512], P('head'), may hold values from -0.125 to 0.125
Outputs:
- output: bfloat16 [16384, 512], P('elem', 'head')
- input_grad: float32 [16384, 512], P('elem', 'head')
The draws below stay inside these ranges and needn't reach their ends.
Inputs may be any that keep to these rules, and one draw needn't show every extreme that they name: `bin_order`: the rows of region e, numbers e * 1024 to (e + 1) * 1024 - 1, hold a permutation of those same numbers. `key_lists`: slot 0 of row b is b; the other slots hold distinct blocks other than b, all of the regions r - 1, r and r + 1 modulo 16, where r = b // 8 and region r holds blocks r * 8 to (r + 1) * 8 - 1; in row r * 8 of every region, slot 1 is a block of region r - 1 and slot 2 a block of region r + 1. list_counts[r * 8] = 12 for every region r.
All inputs are finite; a program needn't handle non-finite values.
Results may differ from the reference program's by a relative error of at most 0.024.
Values may be sent and summed in bfloat16 or wider, within the bound.
No kernel may reach another device: no remote copies, remote signals or barrier semaphores. Data moves between devices by JAX's collectives and lax.ppermute only.
A program may use at most 128 MiB of HBM per device.

```python
import jax
import jax.numpy as jnp
from jax import lax

D = 512
HEADS = 8
HD = 64
FF = 2048
BLK = 128
LIST = 12
BLK_DEV = 8
ROWS_DEV = 1024
REGIONS = 16
NBLK = 128
ELEMENTS = 16384
N_HEAD = 2


def draw_query_weight(key, part):
    own_draw = jax.random.truncated_normal(jax.random.fold_in(key, 202), -6.0, 6.0, (D, D), jnp.float32)
    return (own_draw * D ** (-0.5)).astype(jnp.bfloat16)


def draw_key_weight(key, part):
    own_draw = jax.random.truncated_normal(jax.random.fold_in(key, 303), -6.0, 6.0, (D, D), jnp.float32)
    return (own_draw * D ** (-0.5)).astype(jnp.bfloat16)


def draw_bin_order(key, part):
    key_set = jax.random.split(jax.random.fold_in(key, 7), REGIONS)
    orders = jax.vmap(lambda subkey: jax.random.permutation(subkey, ROWS_DEV))(key_set).astype(jnp.int32)
    offsets = jnp.arange(REGIONS, dtype=jnp.int32)[:, None] * ROWS_DEV
    return (orders + offsets).reshape(-1)


def draw_key_lists(key, part):
    blocks = jnp.arange(NBLK, dtype=jnp.int32)
    region = blocks // BLK_DEV
    local_pos = blocks % BLK_DEV
    own_pos = BLK_DEV + local_pos
    candidates = 3 * BLK_DEV - 1
    key_set = jax.random.split(jax.random.fold_in(key, 11), NBLK)
    ranks = jax.vmap(lambda subkey: jax.random.permutation(subkey, candidates))(key_set).astype(jnp.int32)
    left_pick = jax.random.randint(jax.random.fold_in(key, 19), (NBLK,), 0, BLK_DEV).astype(jnp.int32)
    right_pick = jax.random.randint(jax.random.fold_in(key, 23), (NBLK,), 2 * BLK_DEV - 1, candidates).astype(jnp.int32)
    forced = (local_pos == 0)[:, None]
    slots_idx = jnp.arange(candidates, dtype=jnp.int32)[None, :]
    ranks = jnp.where(forced & (slots_idx == left_pick[:, None]), -2, ranks)
    ranks = jnp.where(forced & (slots_idx == right_pick[:, None]), -1, ranks)
    picks = jnp.argsort(ranks, axis=1, stable=True)[:, :LIST - 1].astype(jnp.int32)
    shifted = picks + (picks >= own_pos[:, None]).astype(jnp.int32)
    owners = jnp.mod(region[:, None] - 1 + shifted // BLK_DEV, REGIONS)
    others = owners * BLK_DEV + shifted % BLK_DEV
    return jnp.concatenate([blocks[:, None], others], axis=1).astype(jnp.int32)


def draw_list_counts(key, part):
    region_most = jax.random.randint(jax.random.fold_in(key, 13), (REGIONS,), 2, LIST + 1).astype(jnp.int32)
    region_most = region_most.at[0].set(LIST)
    per_block = jnp.repeat(region_most, BLK_DEV)
    raw_draw = jax.random.randint(jax.random.fold_in(key, 17), (NBLK,), 0, 1 << 20).astype(jnp.int32)
    counts = raw_draw % per_block + 1
    local_pos = jnp.arange(NBLK, dtype=jnp.int32) % BLK_DEV
    counts = jnp.where(local_pos == 0, LIST, counts)
    counts = counts.at[1].set(1)
    return counts.astype(jnp.int32)


def block_scale(key, shape, pieces, least, largest):
    def one(axis_at, parts):
        heights = jax.random.uniform(jax.random.fold_in(jax.random.fold_in(key, 6), axis_at), (parts,), jnp.float32, least / len(pieces), largest / len(pieces))
        return jnp.repeat(jnp.exp(heights), shape[axis_at] // parts).reshape((-1,) + (1,) * (len(shape) - axis_at - 1))

    loudness = one(*pieces[0])
    for cut in pieces[1:]:
        loudness = loudness * one(*cut)
    return loudness


def centred(stream_key, dims, spread, bound, cuts=(), kind=jnp.bfloat16):
    drawn = jax.random.normal(stream_key, dims, jnp.float32) * spread
    if len(cuts) > 0:
        drawn = block_scale(stream_key, dims, cuts, -0.22, 0.18) * drawn
    return jnp.clip(drawn, min=-bound, max=bound).astype(kind)


def setup_inputs(seed: int = 0) -> dict:
    key_of = jax.random.split(jax.random.key(seed), 14)
    return {
        "features": centred(key_of[0], (ELEMENTS, D), 1.0, 6.0, ((0, 16),)),
        "out_grad": centred(key_of[1], (ELEMENTS, D), 1.0, 6.0, ((0, 16),)),
        "bin_order": draw_bin_order(jax.random.fold_in(key_of[13], 71), 0),
        "key_lists": draw_key_lists(jax.random.fold_in(key_of[13], 71), 0),
        "list_counts": draw_list_counts(jax.random.fold_in(key_of[13], 71), 0),
        "attn_gain": jnp.clip(1.0 + 0.18 * jax.random.normal(key_of[5], (D,), jnp.float32), 0.1, 1.9),
        "query_weight": draw_query_weight(jax.random.fold_in(key_of[13], 71), 0),
        "key_weight": draw_key_weight(jax.random.fold_in(key_of[13], 71), 0),
        "value_weight": centred(key_of[8], (D, D), D ** -0.5, 0.25, ((1, 2),)),
        "out_weight": centred(key_of[9], (D, D), D ** -0.5, 0.25, ((0, 2),)),
        "ffn_gain": jnp.clip(1.0 + 0.18 * jax.random.normal(key_of[10], (D,), jnp.float32), 0.1, 1.9),
        "ffn_in": centred(key_of[11], (D, FF), D ** -0.5, 0.25, ((1, 2),)),
        "ffn_out": centred(key_of[12], (FF, D), FF ** -0.5, 0.125, ((0, 2),)),
    }


EPSILON = 1e-05

def row_scale(values):
    return lax.rsqrt(lax.optimization_barrier(jnp.mean(values * values, axis=-1, keepdims=True)) + EPSILON)

def rounded_values(values):
    narrow = lax.optimization_barrier(values.astype(jnp.bfloat16))
    return narrow.astype(jnp.float32)

def reference(features, out_grad, bin_order, key_lists, list_counts, attn_gain, query_weight, key_weight, value_weight, out_weight, ffn_gain, ffn_in, ffn_out):
    col_share = D // N_HEAD
    hidden_share = FF // N_HEAD
    scale_for_scores = HD ** (-0.5)
    highest_precision = lax.Precision.HIGHEST
    live_slots = jnp.arange(LIST, dtype=jnp.int32)[None, :] < list_counts[:, None]
    ordered = features[bin_order]
    ordered_rows = ordered.astype(jnp.float32)
    first_scale = row_scale(ordered_rows)
    first_norm = ordered_rows * first_scale
    normed = (first_norm * attn_gain).astype(jnp.bfloat16)
    queries = jnp.dot(normed, query_weight, preferred_element_type=jnp.float32).astype(jnp.bfloat16)
    key_rows = jnp.dot(normed, key_weight, preferred_element_type=jnp.float32).astype(jnp.bfloat16)
    value_rows = jnp.dot(normed, value_weight, preferred_element_type=jnp.float32).astype(jnp.bfloat16)

    def by_head(packed):
        return packed.reshape(NBLK, BLK, HEADS, HD).transpose(2, 0, 1, 3)

    def from_heads(packed):
        return packed.transpose(1, 2, 0, 3).reshape(ELEMENTS, D)

    def head_scores(head_query, key_head):
        key_tile_blocks = key_head[key_lists].astype(jnp.float32)
        attention_scores = jnp.einsum('puf,piaf->puia', head_query.astype(jnp.float32), key_tile_blocks, precision=highest_precision) * scale_for_scores
        return (jnp.where(live_slots[:, None, :, None], attention_scores, -jnp.inf), key_tile_blocks)

    def head_forward(operands):
        head_query, key_head, value_head = operands
        attention_scores, key_tile_blocks = head_scores(head_query, key_head)
        row_peak = lax.optimization_barrier(jnp.max(attention_scores, axis=(2, 3), keepdims=True))
        log_total = row_peak + jnp.log(lax.optimization_barrier(jnp.sum(jnp.exp(attention_scores - row_peak), axis=(2, 3), keepdims=True)))
        probabilities = rounded_values(jnp.exp(attention_scores - log_total))
        value_tile_blocks = value_head[key_lists].astype(jnp.float32)
        attended_output = jnp.einsum('ochv,ohvj->ocj', probabilities, value_tile_blocks, precision=highest_precision)
        return (attended_output.astype(jnp.bfloat16), log_total)
    q_heads = by_head(queries)
    k_heads = by_head(key_rows)
    v_heads = by_head(value_rows)
    attended_heads, log_totals = lax.map(head_forward, (q_heads, k_heads, v_heads))
    attended_output = from_heads(attended_heads)
    mixed_heads = jnp.zeros((ELEMENTS, D), jnp.float32)
    for group_pos in range(N_HEAD):
        columns = slice(group_pos * col_share, (group_pos + 1) * col_share)
        mixed_heads = mixed_heads + rounded_values(jnp.dot(attended_output[:, columns], out_weight[columns, :], preferred_element_type=jnp.float32))
    hidden_in = ordered_rows + mixed_heads
    second_scale = row_scale(hidden_in)
    second_norm = hidden_in * second_scale
    normed_two = (second_norm * ffn_gain).astype(jnp.bfloat16)
    pre_act = jnp.dot(normed_two, ffn_in, preferred_element_type=jnp.float32)
    activated = jax.nn.gelu(pre_act).astype(jnp.bfloat16)
    ffn_total = jnp.zeros((ELEMENTS, D), jnp.float32)
    for group_pos in range(N_HEAD):
        columns = slice(group_pos * hidden_share, (group_pos + 1) * hidden_share)
        ffn_total = ffn_total + rounded_values(jnp.dot(activated[:, columns], ffn_out[columns, :], preferred_element_type=jnp.float32))
    out_sorted = (hidden_in + ffn_total).astype(jnp.bfloat16)
    output = jnp.zeros((ELEMENTS, D), jnp.bfloat16).at[bin_order].set(out_sorted)
    grad_ordered = out_grad[bin_order]
    grad_act = jnp.dot(grad_ordered, ffn_out.T, preferred_element_type=jnp.float32)
    gelu_value, gelu_pull = jax.vjp(jax.nn.gelu, pre_act)
    grad_pre = gelu_pull(grad_act)[0].astype(jnp.bfloat16)
    norm_grad = jnp.zeros((ELEMENTS, D), jnp.float32)
    for group_pos in range(N_HEAD):
        columns = slice(group_pos * hidden_share, (group_pos + 1) * hidden_share)
        norm_grad = norm_grad + rounded_values(jnp.dot(grad_pre[:, columns], ffn_in[:, columns].T, preferred_element_type=jnp.float32))
    scaled_grad = norm_grad * ffn_gain
    grad_hidden = grad_ordered.astype(jnp.float32) + second_scale * (scaled_grad - second_norm * lax.optimization_barrier(jnp.mean(scaled_grad * second_norm, axis=-1, keepdims=True)))
    grad_mixed = jnp.dot(grad_hidden.astype(jnp.bfloat16), out_weight.T, preferred_element_type=jnp.float32).astype(jnp.bfloat16)

    def head_backward(operands):
        head_query, key_head, value_head, attended_head, grad_head, log_total = operands
        attention_scores, key_tile_blocks = head_scores(head_query, key_head)
        complete_probabilities = jnp.exp(attention_scores - log_total)
        value_tile_blocks = value_head[key_lists].astype(jnp.float32)
        row_gradients = grad_head.astype(jnp.float32)
        deltas = lax.optimization_barrier(jnp.sum(row_gradients * attended_head.astype(jnp.float32), axis=-1))
        probability_gradient = jnp.einsum('puf,piaf->puia', row_gradients, value_tile_blocks, precision=highest_precision)
        score_gradient = rounded_values(complete_probabilities * (probability_gradient - deltas[:, :, None, None]))
        query_gradient = jnp.einsum('ochv,ohvj->ocj', score_gradient, key_tile_blocks, precision=highest_precision) * scale_for_scores
        key_portion = jnp.einsum('mjif,mje->mife', score_gradient, head_query.astype(jnp.float32), precision=highest_precision) * scale_for_scores
        value_portion = jnp.einsum('mjif,mje->mife', rounded_values(complete_probabilities), row_gradients, precision=highest_precision)
        grad_keys = jnp.zeros((NBLK, BLK, HD), jnp.float32).at[key_lists].add(key_portion)
        grad_values = jnp.zeros((NBLK, BLK, HD), jnp.float32).at[key_lists].add(value_portion)
        return (query_gradient, grad_keys, grad_values)
    grad_q_heads, grad_k_heads, grad_v_heads = lax.map(head_backward, (q_heads, k_heads, v_heads, attended_heads, by_head(grad_mixed), log_totals))
    grad_queries = from_heads(grad_q_heads)
    grad_keys = from_heads(grad_k_heads)
    grad_values = from_heads(grad_v_heads)
    norm_grad_one = jnp.zeros((ELEMENTS, D), jnp.float32)
    for group_pos in range(N_HEAD):
        columns = slice(group_pos * col_share, (group_pos + 1) * col_share)
        group_term = jnp.dot(grad_queries[:, columns], query_weight[:, columns].astype(jnp.float32).T, precision=highest_precision)
        group_term = group_term + jnp.dot(grad_keys[:, columns], key_weight[:, columns].astype(jnp.float32).T, precision=highest_precision)
        group_term = group_term + jnp.dot(grad_values[:, columns], value_weight[:, columns].astype(jnp.float32).T, precision=highest_precision)
        norm_grad_one = norm_grad_one + rounded_values(group_term)
    scaled_one = norm_grad_one * attn_gain
    grad_rows_all = grad_hidden + first_scale * (scaled_one - first_norm * lax.optimization_barrier(jnp.mean(scaled_one * first_norm, axis=-1, keepdims=True)))
    input_grad = jnp.zeros((ELEMENTS, D), jnp.float32).at[bin_order].set(grad_rows_all)
    return (output, input_grad)
```

```python
import functools

import jax
import jax.numpy as jnp
from jax import lax
from jax.experimental import pallas as pl
from jax.experimental.pallas import tpu as pltpu
from jax.sharding import PartitionSpec as P

HD = 64
PAIR = 2 * HD
EPSILON = 1e-05
F32 = jnp.float32
BF16 = jnp.bfloat16
VMEM = pl.BlockSpec(memory_space=pltpu.VMEM)
SMEM = pl.BlockSpec(memory_space=pltpu.SMEM)
COUNT_COL = 12
BLOCK_COL = 13
GROUP_COL = 14
OWN_COL = 15
COST = 1000


def dot_nn(a, b):
    return lax.dot_general(a, b, (((1,), (0,)), ((), ())), preferred_element_type=F32)


def dot_nt(a, b):
    return lax.dot_general(a, b, (((1,), (1,)), ((), ())), preferred_element_type=F32)


def row_scale(values):
    return lax.rsqrt(jnp.mean(values * values, axis=-1, keepdims=True) + EPSILON)


def call(kernel, out_shape, in_specs, scratch=(), vmem=16):
    out_specs = jax.tree.map(lambda _: VMEM, out_shape)
    return pl.pallas_call(
        kernel,
        out_shape=out_shape,
        in_specs=in_specs,
        out_specs=out_specs,
        scratch_shapes=list(scratch),
        compiler_params=pltpu.CompilerParams(vmem_limit_bytes=vmem << 20),
        cost_estimate=pl.CostEstimate(flops=COST, bytes_accessed=COST, transcendentals=0),
    )


def shaped(shape, dtype):
    return jax.ShapeDtypeStruct(shape, dtype)


def column_of(row, size):
    return jnp.broadcast_to(row, (size, size)).T


def sort_matrix(pos_ref, first, size, total):
    lanes = lax.broadcasted_iota(jnp.int32, (128, total), 1).astype(F32)
    parts = []
    for start in range(first, first + size, 128):
        column = column_of(places(pos_ref, start, 128).astype(F32), 128)
        wide = jnp.concatenate([column] * (total // 128), axis=1)
        parts.append(jnp.where(wide == lanes, 1.0, 0.0).astype(BF16))
    return jnp.concatenate(parts, axis=0)


def places(pos_ref, start, size):
    return lax.rem(pos_ref[:, start : start + size], pos_ref.shape[1])


def plan_kernel(head_groups, where_ref, lists_ref, counts_ref, meta_ref):
    blocks, slots = lists_ref.shape
    region, regions, group, heads = where_ref[0], where_ref[1], where_ref[2], head_groups
    counts = [counts_ref[i] for i in range(blocks)]
    for i in range(blocks):
        rank = jnp.int32(0)
        for j in range(blocks):
            if j != i:
                ahead = counts[j] >= counts[i] if j < i else counts[j] > counts[i]
                rank = rank + jnp.where(ahead, 1, 0)
        turn = rank // heads
        side = rank % heads
        side = jnp.where(turn % 2 == 1, heads - 1 - side, side)
        from_me = group - side
        from_me = jnp.where(from_me < 0, from_me + heads, from_me)
        row = from_me * (blocks // heads) + turn
        meta_ref[row, COUNT_COL] = counts[i]
        meta_ref[row, BLOCK_COL] = jnp.int32(i)
        meta_ref[row, GROUP_COL] = group
        entries = []
        own_total = jnp.int32(0)
        for s in range(slots):
            key = lists_ref[i, s]
            away = key // blocks - region + 1
            away = jnp.where(away < 0, away + regions, away)
            away = jnp.where(away >= regions, away - regions, away)
            own = (away == 1) & (s < counts[i])
            entries.append((key % blocks + jnp.where(away == 2, blocks, 0), away == 1))
            own_total = own_total + jnp.where(own, 1, 0)
        meta_ref[row, OWN_COL] = own_total
        own_next, other_next = jnp.int32(0), own_total
        for s in range(slots):
            index, own = entries[s]

            @pl.when(s < counts[i])
            def _(index=index, own=own, own_next=own_next, other_next=other_next):
                meta_ref[row, jnp.where(own, own_next, other_next)] = index

            own_next = own_next + jnp.where(own, 1, 0)
            other_next = other_next + jnp.where(own, 0, 1)


def prep_kernel(pos_ref, rows_ref, gain_ref, normed_ref):
    total = rows_ref.shape[0]
    for first in range(0, total, 512):
        picked = dot_nn(sort_matrix(pos_ref, first, 512, total), rows_ref[...])
        normed_ref[first : first + 512, :] = (picked * row_scale(picked) * gain_ref[...]).astype(BF16)


def sort_kernel(pos_ref, rows_ref, grads_ref, sorted_rows_ref, sorted_grads_ref):
    total = rows_ref.shape[0]
    for first in range(0, total, 512):
        matrix = sort_matrix(pos_ref, first, 512, total)
        sorted_rows_ref[first : first + 512, :] = dot_nn(matrix, rows_ref[...]).astype(BF16)
        sorted_grads_ref[first : first + 512, :] = dot_nn(matrix, grads_ref[...]).astype(BF16)


def chunk(values, who, share):
    out = values[:, :share]
    for start in range(share, values.shape[1], share):
        out = jnp.where(who == start // share, values[:, start : start + share], out)
    return out


def below(group, steps, count):
    who = group + steps
    return jnp.where(who >= count, who - count, who)


def both_heads(rows):
    lane = lax.broadcasted_iota(jnp.int32, rows.shape, 1)
    zero = jnp.zeros_like(rows)
    return jnp.concatenate([jnp.where(lane < HD, rows, zero), jnp.where(lane < HD, zero, rows)], axis=0)


def own_heads(wide):
    half = wide.shape[1] // 2
    return jnp.concatenate([wide[:HD, :half], wide[HD:, half:]], axis=0)


def groups_of_eight(tile, op):
    out = tile[:8]
    for start in range(8, tile.shape[0], 8):
        out = op(out, tile[start : start + 8])
    return out


def joined(mine_ref, packs, which):
    parts = [mine_ref[...]]
    for ref in packs:
        size = ref.shape[1] // 3
        parts.append(ref[:, which * size : (which + 1) * size])
    return jnp.concatenate(parts, axis=1)


def project_keys(rows_ref, wk, wv, keys_ref, values_ref, values_t_ref, base):
    for start in range(0, rows_ref.shape[0], 512):
        at = slice(base + start, base + start + 512)
        here = rows_ref[start : start + 512, :]
        keys_ref[at, :] = dot_nn(here, wk).astype(BF16)
        found = dot_nn(here, wv).astype(BF16)
        values_ref[at, :] = found
        for part in range(4):
            values_t_ref[(base + start) // 128 + part] = found[part * 128 : part * 128 + 128, :].T


def two_slots(meta_ref, b, first, count, step):
    one = first + 2 * step
    two = jnp.minimum(one + 1, first + count - 1)
    return meta_ref[b, one], meta_ref[b, two], 2 * step + 1 < count


def block_rows(ref, index, cols):
    return ref[pl.ds(pl.multiple_of(index * 128, 128), 128), cols]


def both_rows(ref, one, two, cols):
    return jnp.concatenate([block_rows(ref, one, cols), block_rows(ref, two, cols)], axis=0)


def both_cols(ref, one, two, cols):
    return jnp.concatenate([ref[one, cols, :], ref[two, cols, :]], axis=1)


def attend(meta_ref, b, first, count, keys_ref, values_t_ref, query_t_ref, keep_ref, acc_ref, old):
    pairs = query_t_ref.shape[0]
    wide = query_t_ref.shape[2]
    steps = (count + 1) // 2

    def peak_step(i, peaks):
        one, two, _ = two_slots(meta_ref, b, first, count, i)
        out = []
        for p in range(pairs):
            cols = slice(p * PAIR, (p + 1) * PAIR)
            tile = dot_nn(both_rows(keys_ref, one, two, cols), query_t_ref[p])
            keep_ref[i, p] = tile
            out.append(jnp.maximum(peaks[p], groups_of_eight(tile, jnp.maximum)))
        return tuple(out)

    if old is None:
        start = (jnp.full((8, wide), -3.0e38, F32),) * pairs
    else:
        start = tuple(jnp.broadcast_to(peak, (8, wide)) for peak, _ in old)
    peaks = lax.fori_loop(0, steps, peak_step, start)
    peaks = tuple(jnp.max(peak, axis=0, keepdims=True) for peak in peaks)
    totals = []
    for p in range(pairs):
        if old is None:
            acc_ref[p] = jnp.zeros(acc_ref.shape[1:], F32)
            totals.append(jnp.zeros((1, wide), F32))
        else:
            shrink = jnp.exp(old[p][0] - peaks[p])
            acc_ref[p] = acc_ref[p] * shrink
            totals.append(old[p][1] * shrink)

    def sum_step(i, sums):
        one, two, live = two_slots(meta_ref, b, first, count, i)
        out = []
        for p in range(pairs):
            cols = slice(p * PAIR, (p + 1) * PAIR)
            upper = jnp.exp(keep_ref[i, p, :128] - peaks[p])
            lower = jnp.exp(keep_ref[i, p, 128:] - jnp.where(live, peaks[p], 3.0e38))
            out.append(sums[p] + groups_of_eight(upper + lower, jnp.add))
            probs = jnp.concatenate([upper, lower], axis=0).astype(BF16)
            acc_ref[p] += dot_nn(both_cols(values_t_ref, one, two, cols), probs)
        return tuple(out)

    sums = lax.fori_loop(0, steps, sum_step, (jnp.zeros((8, wide), F32),) * pairs)
    return [
        (peaks[p], totals[p] + jnp.sum(sums[p], axis=0, keepdims=True)) for p in range(pairs)
    ]


def own_kernel(
    meta_ref,
    own_ref,
    wq_ref,
    wk_ref,
    wv_ref,
    pack_a,
    pack_b,
    keys_ref,
    values_ref,
    queries_ref,
    acc_ref,
    peaks_ref,
    sums_ref,
    keep_ref,
    values_t_ref,
    query_t_ref,
):
    block = 128
    pairs = queries_ref.shape[1] // PAIR
    packs = (pack_a, pack_b)
    project_keys(own_ref, joined(wk_ref, packs, 1), joined(wv_ref, packs, 2), keys_ref, values_ref, values_t_ref, 0)
    wq = joined(wq_ref, packs, 0)

    @pl.loop(0, queries_ref.shape[0] // block)
    def _(b):
        first = pl.multiple_of(meta_ref[b, BLOCK_COL] * block, block)
        query = dot_nn(own_ref[pl.ds(first, block), :], wq).astype(BF16)
        query = (query.astype(F32) * (HD ** (-0.5))).astype(BF16)
        queries_ref[pl.ds(pl.multiple_of(b * block, block), block), :] = query
        for p in range(pairs):
            query_t_ref[p] = both_heads(query[:, p * PAIR : (p + 1) * PAIR]).T
        found = attend(
            meta_ref,
            b,
            0,
            meta_ref[b, OWN_COL],
            keys_ref,
            values_t_ref,
            query_t_ref,
            keep_ref,
            acc_ref.at[b],
            None,
        )
        for p in range(pairs):
            at = slice(p * 2 * block, (p + 1) * 2 * block)
            peaks_ref[pl.ds(b, 1), at] = found[p][0]
            sums_ref[pl.ds(b, 1), at] = found[p][1]


def halo_kernel(
    meta_ref,
    low_ref,
    high_ref,
    wk_ref,
    wv_ref,
    pack_a,
    pack_b,
    queries_ref,
    old_acc_ref,
    peaks_ref,
    sums_ref,
    keys_ref,
    values_ref,
    attended_ref,
    attended_t_ref,
    log_total_ref,
    keep_ref,
    values_t_ref,
    query_t_ref,
    acc_ref,
):
    block = 128
    pairs = queries_ref.shape[1] // PAIR
    wk = joined(wk_ref, (pack_a, pack_b), 1)
    wv = joined(wv_ref, (pack_a, pack_b), 2)
    project_keys(low_ref, wk, wv, keys_ref, values_ref, values_t_ref, 0)
    project_keys(high_ref, wk, wv, keys_ref, values_ref, values_t_ref, low_ref.shape[0])

    @pl.loop(0, queries_ref.shape[0] // block)
    def _(b):
        here = pl.ds(pl.multiple_of(b * block, block), block)
        old = []
        for p in range(pairs):
            at = slice(p * 2 * block, (p + 1) * 2 * block)
            query_t_ref[p] = both_heads(queries_ref[here, p * PAIR : (p + 1) * PAIR]).T
            acc_ref[p] = old_acc_ref[b, p]
            old.append((peaks_ref[pl.ds(b, 1), at], sums_ref[pl.ds(b, 1), at]))
        own = meta_ref[b, OWN_COL]
        found = attend(
            meta_ref,
            b,
            own,
            meta_ref[b, COUNT_COL] - own,
            keys_ref,
            values_t_ref,
            query_t_ref,
            keep_ref,
            acc_ref,
            old,
        )
        for p in range(pairs):
            peak, total = found[p]
            log_total_ref[pl.ds(b, 1), p * 2 * block : (p + 1) * 2 * block] = peak + jnp.log(total)
            rows = own_heads(acc_ref[p] * (1.0 / total)).astype(BF16)
            attended_t_ref[b, p * PAIR : (p + 1) * PAIR, :] = rows
            attended_ref[here, p * PAIR : (p + 1) * PAIR] = rows.T


GELU_A = 0.044715
GELU_B = 0.7978845608028654


def mix_rows(wo_ref, rows_a, rows_b):
    half = (rows_a.shape[1] - wo_ref.shape[0]) // 2
    return jnp.concatenate([wo_ref[...], rows_a[:half, :], rows_b[:half, :]], axis=0)


def ffn_step(norm_ref, grad_ref, up, down):
    pre = dot_nn(norm_ref[...], up)
    square = pre * pre
    inner = jnp.tanh(GELU_B * pre * (1.0 + GELU_A * square))
    gate = 0.5 * (1.0 + inner)
    active = (pre * gate).astype(BF16)
    slope = gate + (0.5 * GELU_B) * pre * (1.0 - inner * inner) * (1.0 + (3.0 * GELU_A) * square)
    grad_pre = (dot_nt(grad_ref[...], down) * slope).astype(BF16)
    return dot_nn(active, down), dot_nt(grad_pre, up)


def ffn_kernel(
    meta_ref,
    ordered_ref,
    grad_ref,
    attended_ref,
    gain_ref,
    wo_ref,
    rows_a,
    rows_b,
    in_ref,
    out_ref,
    hidden_ref,
    grad_rows,
    norm_ref,
    total_ref,
    back_ref,
):
    block = 128
    size = attended_ref.shape[0]
    for b in range(size // block):
        first = pl.multiple_of(meta_ref[b, BLOCK_COL] * block, block)
        hidden_ref[b * block : (b + 1) * block, :] = ordered_ref[pl.ds(first, block), :].astype(F32)
        grad_rows[b * block : (b + 1) * block, :] = grad_ref[pl.ds(first, block), :]
    mixing = mix_rows(wo_ref, rows_a, rows_b)
    hidden_in = hidden_ref[...] + dot_nn(attended_ref[...], mixing)
    hidden_ref[...] = hidden_in
    norm_ref[...] = (hidden_in * row_scale(hidden_in) * gain_ref[...]).astype(BF16)
    for start in range(0, in_ref.shape[1], 512):
        at = slice(start, start + 512)
        forward, backward = ffn_step(norm_ref, grad_rows, in_ref[:, at], out_ref[at, :])
        if start == 0:
            total_ref[...] = forward
            back_ref[...] = backward
        else:
            total_ref[...] += forward
            back_ref[...] += backward


def rest_kernel(
    meta_ref,
    hidden_ref,
    grad_rows,
    norm_ref,
    old_total_ref,
    old_back_ref,
    gain_ref,
    wo_ref,
    rows_a,
    rows_b,
    in_a,
    in_b,
    mixed_grad_ref,
    out_own_ref,
    hidden_own_ref,
    *refs,
):
    heads = (len(refs) - 2) // 2 + 1
    total_ref, back_ref = refs[-2:]
    forward, backward = ffn_step(norm_ref, grad_rows, in_a[...], rows_a[-in_a.shape[1] :, :])
    total_ref[...] = old_total_ref[...] + forward
    back_ref[...] = old_back_ref[...] + backward
    forward, backward = ffn_step(norm_ref, grad_rows, in_b[...], rows_b[-in_b.shape[1] :, :])
    hidden_in = hidden_ref[...]
    result = (hidden_in + (total_ref[...] + forward)).astype(BF16)
    group = meta_ref[0, GROUP_COL]
    share = out_own_ref.shape[1]
    out_own_ref[...] = chunk(result, group, share)
    for k in range(1, heads):
        refs[k - 1][...] = chunk(result, below(group, k, heads), share)
    scale = row_scale(hidden_in)
    second_norm = hidden_in * scale
    scaled = (back_ref[...] + backward) * gain_ref[...]
    hidden_grad = grad_rows[...].astype(F32) + scale * (
        scaled - second_norm * jnp.mean(scaled * second_norm, axis=-1, keepdims=True)
    )
    hidden_own_ref[...] = chunk(hidden_grad, group, share)
    for k in range(1, heads):
        refs[heads + k - 2][...] = chunk(hidden_grad, below(group, k, heads), share)
    narrow = hidden_grad.astype(BF16)
    mixed_grad_ref[...] = dot_nt(narrow, mix_rows(wo_ref, rows_a, rows_b)).astype(BF16)


def scores_back(
    meta_ref,
    b,
    first,
    count,
    keys_ref,
    values_ref,
    keys_t_ref,
    queries_ref,
    mixed_grad_ref,
    attended_t_ref,
    log_total_ref,
    grad_keys,
    grad_values,
    rows_ref,
    rows_t_ref,
    acc_ref,
):
    block = 128
    pairs = queries_ref.shape[1] // PAIR
    here = pl.ds(pl.multiple_of(b * block, block), block)
    deltas = []
    logs = []
    for p in range(pairs):
        cols = slice(p * PAIR, (p + 1) * PAIR)
        query = both_heads(queries_ref[here, cols])
        grad = both_heads(mixed_grad_ref[here, cols])
        grad_t = grad.T
        rows_ref[0, p] = query
        rows_ref[1, p] = grad
        rows_t_ref[0, p] = query.T
        rows_t_ref[1, p] = grad_t
        attended = attended_t_ref[b, cols, :].astype(F32)
        product = grad_t.astype(F32) * jnp.concatenate([attended, attended], axis=1)
        deltas.append(jnp.sum(product, axis=0, keepdims=True))
        logs.append(log_total_ref[pl.ds(b, 1), p * 2 * block : (p + 1) * 2 * block])

    @pl.loop(0, (count + 1) // 2)
    def _(i):
        one, two, live = two_slots(meta_ref, b, first, count, i)
        at_one = pl.ds(pl.multiple_of(one * block, block), block)
        at_two = pl.ds(pl.multiple_of(two * block, block), block)
        for p in range(pairs):
            cols = slice(p * PAIR, (p + 1) * PAIR)
            scores = dot_nn(both_rows(keys_ref, one, two, cols), rows_t_ref[0, p])
            upper = jnp.exp(scores[:block] - logs[p])
            lower = jnp.exp(scores[block:] - jnp.where(live, logs[p], 3.0e38))
            probs = jnp.concatenate([upper, lower], axis=0)
            prob_grad = dot_nn(both_rows(values_ref, one, two, cols), rows_t_ref[1, p])
            score_grad = (probs * (prob_grad - deltas[p])).astype(BF16)
            to_values = dot_nn(probs.astype(BF16), rows_ref[1, p])
            to_keys = dot_nn(score_grad, rows_ref[0, p])
            acc_ref[p] += dot_nn(both_cols(keys_t_ref, one, two, cols), score_grad)
            grad_values[at_one, cols] += to_values[:block]
            grad_keys[at_one, cols] += to_keys[:block]
            grad_values[at_two, cols] += to_values[block:]
            grad_keys[at_two, cols] += to_keys[block:]


def clear_back(keys_ref, keys_t_ref, grad_keys, grad_values):
    @pl.loop(0, keys_ref.shape[0] // 128)
    def _(kb):
        at = pl.ds(pl.multiple_of(kb * 128, 128), 128)
        grad_keys[at, :] = jnp.zeros((128, grad_keys.shape[1]), F32)
        grad_values[at, :] = jnp.zeros((128, grad_keys.shape[1]), F32)
        keys_t_ref[kb] = keys_ref[at, :].T


def project_back(grad_keys, grad_values, wk, wv, start, size):
    at = slice(start, start + size)
    keys_part = dot_nt(grad_keys[at, :].astype(BF16), wk)
    return keys_part + dot_nt(grad_values[at, :].astype(BF16), wv)


def halo_back_kernel(
    meta_ref,
    keys_ref,
    values_ref,
    queries_ref,
    mixed_grad_ref,
    attended_t_ref,
    log_total_ref,
    wk_ref,
    wv_ref,
    pack_a,
    pack_b,
    low_ref,
    high_ref,
    acc_ref,
    grad_keys,
    grad_values,
    keys_t_ref,
    rows_ref,
    rows_t_ref,
):
    rows = low_ref.shape[0]
    clear_back(keys_ref, keys_t_ref, grad_keys, grad_values)

    @pl.loop(0, queries_ref.shape[0] // 128)
    def _(b):
        own = meta_ref[b, OWN_COL]
        acc_ref[b] = jnp.zeros(acc_ref.shape[1:], F32)
        scores_back(
            meta_ref,
            b,
            own,
            meta_ref[b, COUNT_COL] - own,
            keys_ref,
            values_ref,
            keys_t_ref,
            queries_ref,
            mixed_grad_ref,
            attended_t_ref,
            log_total_ref,
            grad_keys,
            grad_values,
            rows_ref,
            rows_t_ref,
            acc_ref.at[b],
        )

    packs = (pack_a, pack_b)
    weights = joined(wk_ref, packs, 1), joined(wv_ref, packs, 2)
    for start in range(0, rows, 512):
        at = slice(start, start + 512)
        low_ref[at, :] = project_back(grad_keys, grad_values, *weights, start, 512).astype(BF16)
        high_ref[at, :] = project_back(grad_keys, grad_values, *weights, rows + start, 512).astype(BF16)


def own_back_kernel(
    meta_ref,
    keys_ref,
    values_ref,
    queries_ref,
    mixed_grad_ref,
    attended_t_ref,
    log_total_ref,
    old_acc_ref,
    wq_ref,
    wk_ref,
    wv_ref,
    pack_a,
    pack_b,
    own_ref,
    grad_keys,
    grad_values,
    keys_t_ref,
    rows_ref,
    rows_t_ref,
    acc_ref,
    query_grad,
):
    block = 128
    rows = own_ref.shape[0]
    pairs = queries_ref.shape[1] // PAIR
    blocks = queries_ref.shape[0] // block
    clear_back(keys_ref, keys_t_ref, grad_keys, grad_values)

    @pl.loop(0, blocks)
    def _(b):
        acc_ref[...] = old_acc_ref[b]
        scores_back(
            meta_ref,
            b,
            0,
            meta_ref[b, OWN_COL],
            keys_ref,
            values_ref,
            keys_t_ref,
            queries_ref,
            mixed_grad_ref,
            attended_t_ref,
            log_total_ref,
            grad_keys,
            grad_values,
            rows_ref,
            rows_t_ref,
            acc_ref,
        )
        for p in range(pairs):
            found = own_heads(acc_ref[p]) * (HD ** (-0.5))
            query_grad[pl.ds(pl.multiple_of(b * block, block), block), p * PAIR : (p + 1) * PAIR] = found.T.astype(BF16)

    packs = (pack_a, pack_b)
    weights = joined(wk_ref, packs, 1), joined(wv_ref, packs, 2)
    for start in range(0, rows, 512):
        own_ref[start : start + 512, :] = project_back(grad_keys, grad_values, *weights, start, 512)
    parts = dot_nt(query_grad[...], joined(wq_ref, packs, 0))
    for b in range(blocks):
        first = pl.multiple_of(meta_ref[b, BLOCK_COL] * block, block)
        own_ref[pl.ds(first, block), :] += parts[b * block : (b + 1) * block]


def term_kernel(meta_ref, own_ref, low_ref, high_ref, ordered_ref, gain_ref, term_ref, dots_ref, *send_refs):
    rows = own_ref.shape[0]
    share = term_ref.shape[1]
    heads = len(send_refs) + 1
    group = meta_ref[0, GROUP_COL]
    dot_rows = []
    for start in range(0, rows, 128):
        at = slice(start, start + 128)
        term = own_ref[at, :] + low_ref[at, :].astype(F32) + high_ref[at, :].astype(F32)
        ordered = ordered_ref[at, :].astype(F32)
        norm = ordered * row_scale(ordered)
        dots = jnp.sum(term * gain_ref[...] * norm, axis=-1, keepdims=True)
        dot_rows.append(jnp.broadcast_to(dots, (128, 128)).T[:1])
        term_ref[at, :] = chunk(term, group, share)
        for k in range(1, heads):
            send_refs[k - 1][at, :] = chunk(term, below(group, k, heads), share).astype(BF16)
    dots = jnp.concatenate(dot_rows, axis=0)
    dots_ref[...] = dots
    high = dots.astype(BF16)
    low = (dots - high.astype(F32)).astype(BF16)
    wide = min(share, 128)
    tail = jnp.concatenate(
        [half[:, start : start + wide] for half in (high, low) for start in range(0, 128, wide)], axis=0
    )
    if share > wide:
        tail = jnp.concatenate([tail] * (share // wide), axis=1)
    for ref in send_refs:
        ref[rows:, :] = tail


def dots_of(tail):
    wide = min(tail.shape[1], 128)
    count = 128 // wide
    size = tail.shape[0] // (2 * count)
    parts = [tail[i * size : (i + 1) * size, :wide].astype(F32) for i in range(2 * count)]
    sums = [parts[i] + parts[count + i] for i in range(count)]
    return sums[0] if count == 1 else jnp.concatenate(sums, axis=1)


def back_matrix(pos_ref, first, size, total):
    place = lax.broadcasted_iota(jnp.int32, (size, total), 0) + first
    return jnp.where(jnp.broadcast_to(places(pos_ref, 0, total), (size, total)) == place, 1.0, 0.0).astype(BF16)


def place_blocks(meta_ref, refs, all_ref):
    block = 128
    blocks = refs[0].shape[0] // block
    for k, ref in enumerate(refs):
        for b in range(blocks):
            first = pl.multiple_of(meta_ref[k * blocks + b, BLOCK_COL] * block, block)
            all_ref[pl.ds(first, block), :] = ref[b * block : (b + 1) * block, :]


def output_kernel(meta_ref, pos_ref, *refs):
    out_ref, all_ref = refs[-2:]
    place_blocks(meta_ref, refs[:-2], all_ref)
    total = all_ref.shape[0]
    for first in range(0, total, 512):
        out_ref[first : first + 512, :] = dot_nn(
            back_matrix(pos_ref, first, 512, total), all_ref[...]
        ).astype(BF16)


def final_kernel(meta_ref, pos_ref, term_ref, dots_ref, ordered_ref, gain_ref, *refs):
    out_ref, all_ref, split_ref = refs[-3:]
    heads = (len(refs) - 3 + 1) // 2
    place_blocks(meta_ref, refs[:heads], all_ref)
    got_refs = refs[heads:-3]
    total, share = out_ref.shape
    group = meta_ref[0, GROUP_COL]
    gain = chunk(gain_ref[...], group, share)
    dots = dots_ref[...]
    for ref in got_refs:
        dots = dots + dots_of(ref[total:, :])
    dots = dots * (1.0 / ordered_ref.shape[1])
    for start in range(0, total, 128):
        at = slice(start, start + 128)
        ordered = ordered_ref[at, :].astype(F32)
        scale = row_scale(ordered)
        part = chunk(ordered, group, share) * scale
        mean = column_of(dots[start // 128 : start // 128 + 1], 128)[:, :1]
        term = term_ref[at, :]
        for ref in got_refs:
            term = term + ref[at, :].astype(F32)
        value = all_ref[at, :] + scale * (term * gain - part * mean)
        high = value.astype(BF16)
        split_ref[at, :share] = high
        split_ref[at, share:] = (value - high.astype(F32)).astype(BF16)
    for first in range(0, total, 512):
        found = dot_nn(back_matrix(pos_ref, first, 512, total), split_ref[...])
        out_ref[first : first + 512, :] = found[:, :share] + found[:, share:]


def local(
    features,
    out_grad,
    bin_order,
    key_lists,
    list_counts,
    attn_gain,
    query_weight,
    key_weight,
    value_weight,
    out_weight,
    ffn_gain,
    ffn_in,
    ffn_out,
):
    rows, width = features.shape
    block_count, slots = key_lists.shape
    block = rows // block_count
    share = query_weight.shape[1]
    hidden = ffn_in.shape[1]
    region = lax.axis_index("elem")
    regions = lax.axis_size("elem")
    group = lax.axis_index("head")
    head_groups = lax.axis_size("head")
    half_count = block_count // head_groups
    mine_rows = rows // head_groups
    forward = [(i, (i + 1) % regions) for i in range(regions)]
    backward = [(target, source) for source, target in forward]
    sibling = [(i, i ^ 1) for i in range(regions)]

    def exchanged(pieces):
        return [
            lax.ppermute(piece, "head", [(i, (i + k) % head_groups) for i in range(head_groups)])
            for k, piece in enumerate(pieces, 1)
        ]

    positions = bin_order.reshape(1, rows)
    gain_one = attn_gain.reshape(1, width)
    gain_two = ffn_gain.reshape(1, width)

    normed = call(prep_kernel, shaped((rows, width), BF16), [VMEM] * 3)(positions, features, gain_one)
    low = lax.ppermute(normed, "elem", forward)
    high = lax.ppermute(normed, "elem", backward)
    projections = (query_weight, key_weight, value_weight)
    if head_groups == 2:

        def my_piece(weight, core, dim):
            size = weight.shape[dim] // 2
            return lax.dynamic_slice_in_dim(weight, core * size, size, dim)

        core, normed = lax.optimization_barrier((region % 2, normed))
        pack = jnp.concatenate([my_piece(w, core, 1) for w in projections], axis=1)
        core, pack = lax.optimization_barrier((core, pack))
        (pack_a,) = exchanged([pack])
        pack_b = lax.ppermute(pack_a, "elem", sibling)
        pack = jnp.concatenate([my_piece(out_weight, core, 0), my_piece(ffn_out, core, 0)], axis=0)
        core, pack = lax.optimization_barrier((core, pack))
        (rows_a,) = exchanged([pack])
        (up_a,) = exchanged([my_piece(ffn_in, core, 1)])
    else:

        def pieces(weight, dim):
            size = weight.shape[dim] * head_groups // 4
            whole = lax.all_gather(weight, "head", axis=dim, tiled=True)
            return jnp.split(whole, (2 * size, 3 * size), axis=dim)

        split = [pieces(w, 1) for w in projections]
        projections = tuple(parts[0] for parts in split)
        pack_a, pack_b = (jnp.concatenate([parts[i] for parts in split], axis=1) for i in (1, 2))
        mix_parts, out_parts = pieces(out_weight, 0), pieces(ffn_out, 0)
        out_weight, ffn_out = mix_parts[0], out_parts[0]
        rows_a, rows_b = (jnp.concatenate([mix_parts[i], out_parts[i]], axis=0) for i in (1, 2))
        ffn_in, up_a, up_b = pieces(ffn_in, 1)

    meta = pl.pallas_call(
        functools.partial(plan_kernel, head_groups),
        out_shape=shaped((block_count, 16), jnp.int32),
        in_specs=[SMEM] * 3,
        out_specs=SMEM,
    )(jnp.stack([region, jnp.int32(regions), group, group]), key_lists, list_counts)

    ordered, grad_sorted = call(
        sort_kernel, (shaped((rows, width), BF16), shaped((rows, width), BF16)), [VMEM] * 3
    )(positions, features, out_grad)

    heads_width = head_groups * share
    key_value = (*projections[1:], pack_a, pack_b)
    pairs = heads_width // PAIR
    pair_tile = (pairs, PAIR, 2 * block)
    keep = pltpu.VMEM(((slots + 1) // 2, pairs, 2 * block, 2 * block), F32)
    stats = shaped((half_count, 2 * heads_width), F32)
    keys, values, queries, part_acc, part_peaks, part_sums = call(
        own_kernel,
        (
            shaped((rows, heads_width), BF16),
            shaped((rows, heads_width), BF16),
            shaped((mine_rows, heads_width), BF16),
            shaped((half_count,) + pair_tile, F32),
            stats,
            stats,
        ),
        [SMEM] + [VMEM] * 6,
        scratch=(
            keep,
            pltpu.VMEM((block_count, heads_width, block), BF16),
            pltpu.VMEM(pair_tile, BF16),
        ),
        vmem=26,
    )(meta, normed, *projections, pack_a, pack_b)
    if head_groups == 2:
        queries, rows_a = lax.optimization_barrier((queries, rows_a))
        rows_b = lax.ppermute(rows_a, "elem", sibling)
    halo_keys, halo_values, attended, attended_t, log_total = call(
        halo_kernel,
        (
            shaped((2 * rows, heads_width), BF16),
            shaped((2 * rows, heads_width), BF16),
            shaped((mine_rows, heads_width), BF16),
            shaped((half_count, heads_width, block), BF16),
            stats,
        ),
        [SMEM] + [VMEM] * 10,
        scratch=(
            keep,
            pltpu.VMEM((2 * block_count, heads_width, block), BF16),
            pltpu.VMEM(pair_tile, BF16),
            pltpu.VMEM(pair_tile, F32),
        ),
        vmem=30,
    )(meta, low, high, *key_value, queries, part_acc, part_peaks, part_sums)

    square = shaped((mine_rows, width), F32)
    narrow = shaped((mine_rows, width), BF16)
    if head_groups == 2:
        attended, up_a = lax.optimization_barrier((attended, up_a))
        up_b = lax.ppermute(up_a, "elem", sibling)
    hidden_in, grad_rows, norm_two, part_total, part_back = call(
        ffn_kernel,
        (square, narrow, narrow, square, square),
        [SMEM] + [VMEM] * 9,
    )(meta, ordered, grad_sorted, attended, gain_two, out_weight, rows_a, rows_b, ffn_in, ffn_out)
    others = head_groups - 1
    mixed_grad, out_own, hidden_own, *sends = call(
        rest_kernel,
        (
            narrow,
            shaped((mine_rows, share), BF16),
            shaped((mine_rows, share), F32),
            *[shaped((mine_rows, share), BF16)] * others,
            *[shaped((mine_rows, share), F32)] * others,
        ),
        [SMEM] + [VMEM] * 11,
        scratch=(pltpu.VMEM((mine_rows, width), F32), pltpu.VMEM((mine_rows, width), F32)),
    )(
        meta,
        hidden_in,
        grad_rows,
        norm_two,
        part_total,
        part_back,
        gain_two,
        out_weight,
        rows_a,
        rows_b,
        up_a,
        up_b,
    )
    out_got = exchanged(sends[:others])
    hidden_got = exchanged(sends[others:])

    rows_pair = pltpu.VMEM((2, pairs, 2 * block, PAIR), BF16)
    cols_pair = pltpu.VMEM((2,) + pair_tile, BF16)
    grad_low, grad_high, part_grad = call(
        halo_back_kernel,
        (
            shaped((rows, width), BF16),
            shaped((rows, width), BF16),
            shaped((half_count,) + pair_tile, F32),
        ),
        [SMEM] + [VMEM] * 10,
        scratch=(
            pltpu.VMEM((2 * rows, heads_width), F32),
            pltpu.VMEM((2 * rows, heads_width), F32),
            pltpu.VMEM((2 * block_count, heads_width, block), BF16),
            rows_pair,
            cols_pair,
        ),
        vmem=36,
    )(meta, halo_keys, halo_values, queries, mixed_grad, attended_t, log_total, *key_value)
    from_right = lax.ppermute(grad_low, "elem", backward)
    from_left = lax.ppermute(grad_high, "elem", forward)
    grad_own = call(
        own_back_kernel,
        shaped((rows, width), F32),
        [SMEM] + [VMEM] * 12,
        scratch=(
            pltpu.VMEM((rows, heads_width), F32),
            pltpu.VMEM((rows, heads_width), F32),
            pltpu.VMEM((block_count, heads_width, block), BF16),
            rows_pair,
            cols_pair,
            pltpu.VMEM(pair_tile, F32),
            pltpu.VMEM((mine_rows, heads_width), BF16),
        ),
        vmem=30,
    )(
        meta,
        keys,
        values,
        queries,
        mixed_grad,
        attended_t,
        log_total,
        part_grad,
        *projections,
        pack_a,
        pack_b,
    )
    from_right, from_left, out_got, hidden_got = lax.optimization_barrier(
        (from_right, from_left, out_got, hidden_got)
    )
    tail = 2 * (rows // 128) * (128 // min(share, 128))
    term, dots, *sends = call(
        term_kernel,
        (
            shaped((rows, share), F32),
            shaped((rows // 128, 128), F32),
            *[shaped((rows + tail, share), BF16)] * others,
        ),
        [SMEM] + [VMEM] * 5,
    )(meta, grad_own, from_right, from_left, ordered, gain_one)
    got = exchanged(sends)
    output = call(
        output_kernel,
        shaped((rows, share), BF16),
        [SMEM] + [VMEM] * (1 + head_groups),
        scratch=(pltpu.VMEM((rows, share), BF16),),
    )(meta, positions, out_own, *out_got)
    input_grad = call(
        final_kernel,
        shaped((rows, share), F32),
        [SMEM] + [VMEM] * (4 + 2 * head_groups),
        scratch=(pltpu.VMEM((rows, share), F32), pltpu.VMEM((rows, 2 * share), BF16)),
    )(meta, positions, term, dots, ordered, gain_one, hidden_own, *hidden_got, *got)
    return (output, input_grad)


def solution(mesh):
    in_specs = (
        P("elem", None),
        P("elem", None),
        P("elem"),
        P("elem", None),
        P("elem"),
        P(),
        P(None, "head"),
        P(None, "head"),
        P(None, "head"),
        P("head", None),
        P(),
        P(None, "head"),
        P("head", None),
    )
    out_specs = (P("elem", "head"), P("elem", "head"))
    return jax.shard_map(local, mesh=mesh, in_specs=in_specs, out_specs=out_specs, check_vma=False)
```

```python
import functools

import jax
import jax.numpy as jnp
from jax import lax
from jax.experimental import pallas as pl
from jax.experimental.pallas import tpu as pltpu
from jax.sharding import PartitionSpec as P

HD = 64
PAIR = 2 * HD
EPSILON = 1e-05
F32 = jnp.float32
BF16 = jnp.bfloat16
VMEM = pl.BlockSpec(memory_space=pltpu.VMEM)
SMEM = pl.BlockSpec(memory_space=pltpu.SMEM)
COUNT_COL = 12
BLOCK_COL = 13
GROUP_COL = 14
OWN_COL = 15
LOW_COL = 16
META_COLS = 128
COST = 1000


def dot_nn(a, b):
    return lax.dot_general(a, b, (((1,), (0,)), ((), ())), preferred_element_type=F32)


def dot_nt(a, b):
    return lax.dot_general(a, b, (((1,), (1,)), ((), ())), preferred_element_type=F32)


def row_scale(values):
    return lax.rsqrt(jnp.mean(values * values, axis=-1, keepdims=True) + EPSILON)


def call(kernel, out_shape, in_specs, scratch=(), vmem=16):
    out_specs = jax.tree.map(lambda _: VMEM, out_shape)
    return pl.pallas_call(
        kernel,
        out_shape=out_shape,
        in_specs=in_specs,
        out_specs=out_specs,
        scratch_shapes=list(scratch),
        compiler_params=pltpu.CompilerParams(vmem_limit_bytes=vmem << 20),
        cost_estimate=pl.CostEstimate(flops=COST, bytes_accessed=COST, transcendentals=0),
    )


def shaped(shape, dtype):
    return jax.ShapeDtypeStruct(shape, dtype)


def column_of(row, size):
    return jnp.broadcast_to(row, (size, size)).T


def sort_matrix(pos_ref, first, size, total):
    lanes = lax.broadcasted_iota(jnp.int32, (128, total), 1).astype(F32)
    parts = []
    for start in range(first, first + size, 128):
        column = column_of(places(pos_ref, start, 128).astype(F32), 128)
        wide = jnp.concatenate([column] * (total // 128), axis=1)
        parts.append(jnp.where(wide == lanes, 1.0, 0.0).astype(BF16))
    return jnp.concatenate(parts, axis=0)


def places(pos_ref, start, size):
    return lax.rem(pos_ref[:, start : start + size], pos_ref.shape[1])


def plan_kernel(head_groups, where_ref, lists_ref, counts_ref, meta_ref):
    blocks, slots = lists_ref.shape
    region, regions, group, heads = where_ref[0], where_ref[1], where_ref[2], head_groups
    counts = [counts_ref[i] for i in range(blocks)]
    for i in range(blocks):
        rank = jnp.int32(0)
        for j in range(blocks):
            if j != i:
                ahead = counts[j] >= counts[i] if j < i else counts[j] > counts[i]
                rank = rank + jnp.where(ahead, 1, 0)
        turn = rank // heads
        side = rank % heads
        side = jnp.where(turn % 2 == 1, heads - 1 - side, side)
        from_me = group - side
        from_me = jnp.where(from_me < 0, from_me + heads, from_me)
        row = from_me * (blocks // heads) + turn
        meta_ref[row, COUNT_COL] = counts[i]
        meta_ref[row, BLOCK_COL] = jnp.int32(i)
        meta_ref[row, GROUP_COL] = group
        entries = []
        own_total = low_total = jnp.int32(0)
        for s in range(slots):
            key = lists_ref[i, s]
            away = key // blocks - region + 1
            away = jnp.where(away < 0, away + regions, away)
            away = jnp.where(away >= regions, away - regions, away)
            entries.append((key % blocks + jnp.where(away == 2, blocks, 0), away))
            live = s < counts[i]
            own_total = own_total + jnp.where((away == 1) & live, 1, 0)
            low_total = low_total + jnp.where((away == 0) & live, 1, 0)
        meta_ref[row, OWN_COL] = own_total
        meta_ref[row, LOW_COL] = low_total
        own_next, low_next, high_next = jnp.int32(0), own_total, own_total + low_total
        for s in range(slots):
            index, away = entries[s]
            to = jnp.where(away == 1, own_next, jnp.where(away == 0, low_next, high_next))

            @pl.when(s < counts[i])
            def _(index=index, to=to):
                meta_ref[row, to] = index

            own_next = own_next + jnp.where(away == 1, 1, 0)
            low_next = low_next + jnp.where(away == 0, 1, 0)
            high_next = high_next + jnp.where(away == 2, 1, 0)


def prep_kernel(pos_ref, rows_ref, gain_ref, normed_ref):
    total = rows_ref.shape[0]
    for first in range(0, total, 512):
        picked = dot_nn(sort_matrix(pos_ref, first, 512, total), rows_ref[...])
        normed_ref[first : first + 512, :] = (picked * row_scale(picked) * gain_ref[...]).astype(BF16)


def sort_kernel(pos_ref, rows_ref, grads_ref, sorted_rows_ref, sorted_grads_ref):
    total = rows_ref.shape[0]
    for first in range(0, total, 512):
        matrix = sort_matrix(pos_ref, first, 512, total)
        sorted_rows_ref[first : first + 512, :] = dot_nn(matrix, rows_ref[...]).astype(BF16)
        sorted_grads_ref[first : first + 512, :] = dot_nn(matrix, grads_ref[...]).astype(BF16)


def chunk(values, who, share):
    out = values[:, :share]
    for start in range(share, values.shape[1], share):
        out = jnp.where(who == start // share, values[:, start : start + share], out)
    return out


def below(group, steps, count):
    who = group + steps
    return jnp.where(who >= count, who - count, who)


def both_heads(rows):
    lane = lax.broadcasted_iota(jnp.int32, rows.shape, 1)
    zero = jnp.zeros_like(rows)
    return jnp.concatenate([jnp.where(lane < HD, rows, zero), jnp.where(lane < HD, zero, rows)], axis=0)


def both_heads_t(rows):
    flipped = rows.T
    row = lax.broadcasted_iota(jnp.int32, flipped.shape, 0)
    zero = jnp.zeros_like(flipped)
    return jnp.concatenate([jnp.where(row < HD, flipped, zero), jnp.where(row < HD, zero, flipped)], axis=1)


def own_heads(wide):
    half = wide.shape[1] // 2
    return jnp.concatenate([wide[:HD, :half], wide[HD:, half:]], axis=0)


def groups_of_eight(tile, op):
    out = tile[:8]
    for start in range(8, tile.shape[0], 8):
        out = op(out, tile[start : start + 8])
    return out


def packed(packs, which):
    size = packs[0].shape[1] // 4
    return jnp.concatenate([ref[:, which * size : (which + 1) * size] for ref in packs], axis=1)


def joined(mine_ref, packs, which):
    return jnp.concatenate([mine_ref[...], packed(packs, which)], axis=1)


def project_keys(rows_ref, wk, wv, keys_ref, values_ref, values_t_ref, base):
    for start in range(0, rows_ref.shape[0], 512):
        at = slice(base + start, base + start + 512)
        here = rows_ref[start : start + 512, :]
        keys_ref[at, :] = dot_nn(here, wk).astype(BF16)
        found = dot_nn(here, wv).astype(BF16)
        values_ref[at, :] = found
        for part in range(4):
            values_t_ref[(base + start) // 128 + part] = found[part * 128 : part * 128 + 128, :].T


def block_rows(ref, indices, cols):
    return jnp.concatenate(
        [ref[pl.ds(pl.multiple_of(index * 128, 128), 128), cols] for index in indices], axis=0
    )


def block_cols(ref, indices, cols):
    return jnp.concatenate([ref[index, cols, :] for index in indices], axis=1)


def by_two(count, step, carried):
    carried = lax.fori_loop(0, count // 2, lambda i, c: step(2 * i, 2, c), carried)
    return lax.fori_loop(0, count % 2, lambda i, c: step(count - 1, 1, c), carried)


def attend(meta_ref, b, first, count, keys_ref, values_t_ref, query_t_ref, keep_ref, acc_ref, old):
    pairs = query_t_ref.shape[0]
    wide = query_t_ref.shape[2]

    def peak_step(slot, size, peaks):
        indices = [meta_ref[b, first + slot + j] for j in range(size)]
        out = []
        for p in range(pairs):
            cols = slice(p * PAIR, (p + 1) * PAIR)
            tile = dot_nn(block_rows(keys_ref, indices, cols), query_t_ref[p])
            for j in range(size):
                keep_ref[slot + j, p] = tile[j * 128 : (j + 1) * 128]
            out.append(jnp.maximum(peaks[p], groups_of_eight(tile, jnp.maximum)))
        return tuple(out)

    if old is None:
        start = (jnp.full((8, wide), -3.0e38, F32),) * pairs
    else:
        start = tuple(jnp.broadcast_to(peak, (8, wide)) for peak, _ in old)
    peaks = by_two(count, peak_step, start)
    peaks = tuple(jnp.max(peak, axis=0, keepdims=True) for peak in peaks)
    totals = []
    for p in range(pairs):
        if old is None:
            acc_ref[p] = jnp.zeros(acc_ref.shape[1:], F32)
            totals.append(jnp.zeros((1, wide), F32))
        else:
            shrink = jnp.exp(old[p][0] - peaks[p])
            acc_ref[p] = acc_ref[p] * shrink
            totals.append(old[p][1] * shrink)

    def sum_step(slot, size, sums):
        indices = [meta_ref[b, first + slot + j] for j in range(size)]
        out = []
        for p in range(pairs):
            cols = slice(p * PAIR, (p + 1) * PAIR)
            tile = jnp.concatenate([jnp.exp(keep_ref[slot + j, p] - peaks[p]) for j in range(size)], axis=0)
            out.append(sums[p] + groups_of_eight(tile, jnp.add))
            acc_ref[p] += dot_nn(block_cols(values_t_ref, indices, cols), tile.astype(BF16))
        return tuple(out)

    sums = by_two(count, sum_step, (jnp.zeros((8, wide), F32),) * pairs)
    return [
        (peaks[p], totals[p] + jnp.sum(sums[p], axis=0, keepdims=True)) for p in range(pairs)
    ]


def own_kernel(
    meta_ref,
    own_ref,
    wq_ref,
    wk_ref,
    wv_ref,
    pack_a,
    pack_b,
    keys_ref,
    values_ref,
    queries_ref,
    query_t_ref,
    acc_ref,
    peaks_ref,
    sums_ref,
    keep_ref,
    values_t_ref,
):
    block = 128
    pairs = queries_ref.shape[1] // PAIR
    packs = (pack_a, pack_b)
    project_keys(own_ref, joined(wk_ref, packs, 1), joined(wv_ref, packs, 2), keys_ref, values_ref, values_t_ref, 0)
    wq = joined(wq_ref, packs, 0)

    @pl.loop(0, queries_ref.shape[0] // block)
    def _(b):
        first = pl.multiple_of(meta_ref[b, BLOCK_COL] * block, block)
        query = dot_nn(own_ref[pl.ds(first, block), :], wq).astype(BF16)
        query = (query.astype(F32) * (HD ** (-0.5))).astype(BF16)
        queries_ref[pl.ds(pl.multiple_of(b * block, block), block), :] = query
        for p in range(pairs):
            query_t_ref[b, p] = both_heads_t(query[:, p * PAIR : (p + 1) * PAIR])
        found = attend(
            meta_ref,
            b,
            0,
            meta_ref[b, OWN_COL],
            keys_ref,
            values_t_ref,
            query_t_ref.at[b],
            keep_ref,
            acc_ref.at[b],
            None,
        )
        for p in range(pairs):
            at = slice(p * 2 * block, (p + 1) * 2 * block)
            peaks_ref[pl.ds(b, 1), at] = found[p][0]
            sums_ref[pl.ds(b, 1), at] = found[p][1]


def halo_kernel(
    meta_ref,
    low_ref,
    high_ref,
    wk_ref,
    wv_ref,
    pack_a,
    pack_b,
    query_t_ref,
    old_acc_ref,
    peaks_ref,
    sums_ref,
    keys_ref,
    values_ref,
    attended_ref,
    attended_t_ref,
    log_total_ref,
    keep_ref,
    values_t_ref,
    acc_ref,
):
    block = 128
    pairs = query_t_ref.shape[1]
    wk = joined(wk_ref, (pack_a, pack_b), 1)
    wv = joined(wv_ref, (pack_a, pack_b), 2)
    project_keys(low_ref, wk, wv, keys_ref, values_ref, values_t_ref, 0)
    project_keys(high_ref, wk, wv, keys_ref, values_ref, values_t_ref, low_ref.shape[0])

    @pl.loop(0, query_t_ref.shape[0])
    def _(b):
        here = pl.ds(pl.multiple_of(b * block, block), block)
        old = []
        for p in range(pairs):
            at = slice(p * 2 * block, (p + 1) * 2 * block)
            acc_ref[p] = old_acc_ref[b, p]
            old.append((peaks_ref[pl.ds(b, 1), at], sums_ref[pl.ds(b, 1), at]))
        own = meta_ref[b, OWN_COL]
        found = attend(
            meta_ref,
            b,
            own,
            meta_ref[b, COUNT_COL] - own,
            keys_ref,
            values_t_ref,
            query_t_ref.at[b],
            keep_ref,
            acc_ref,
            old,
        )
        for p in range(pairs):
            peak, total = found[p]
            log_total_ref[pl.ds(b, 1), p * 2 * block : (p + 1) * 2 * block] = peak + jnp.log(total)
            rows = own_heads(acc_ref[p] * (1.0 / total)).astype(BF16)
            attended_t_ref[b, p * PAIR : (p + 1) * PAIR, :] = rows
            attended_ref[here, p * PAIR : (p + 1) * PAIR] = rows.T


GELU_A = 0.044715
GELU_B = 0.7978845608028654


def ffn_step(norm_ref, grad_ref, up, down):
    pre = dot_nn(norm_ref[...], up)
    square = pre * pre
    inner = jnp.tanh(GELU_B * pre * (1.0 + GELU_A * square))
    gate = 0.5 * (1.0 + inner)
    active = (pre * gate).astype(BF16)
    slope = gate + (0.5 * GELU_B) * pre * (1.0 - inner * inner) * (1.0 + (3.0 * GELU_A) * square)
    grad_pre = (dot_nt(grad_ref[...], down) * slope).astype(BF16)
    return dot_nn(active, down), dot_nt(grad_pre, up)


def ffn_kernel(
    meta_ref,
    ordered_ref,
    grad_ref,
    attended_ref,
    gain_ref,
    wo_ref,
    pack_a,
    pack_b,
    in_ref,
    out_ref,
    hidden_ref,
    grad_rows,
    norm_ref,
    total_ref,
    back_ref,
):
    block = 128
    size = attended_ref.shape[0]
    for b in range(size // block):
        first = pl.multiple_of(meta_ref[b, BLOCK_COL] * block, block)
        hidden_ref[b * block : (b + 1) * block, :] = ordered_ref[pl.ds(first, block), :].astype(F32)
        grad_rows[b * block : (b + 1) * block, :] = grad_ref[pl.ds(first, block), :]
    share = wo_ref.shape[0]
    hidden_in = hidden_ref[...] + dot_nn(attended_ref[:, :share], wo_ref[...])
    hidden_in = hidden_in + dot_nt(attended_ref[:, share:], packed((pack_a, pack_b), 3))
    hidden_ref[...] = hidden_in
    norm_ref[...] = (hidden_in * row_scale(hidden_in) * gain_ref[...]).astype(BF16)
    for start in range(0, in_ref.shape[1], 512):
        at = slice(start, start + 512)
        forward, backward = ffn_step(norm_ref, grad_rows, in_ref[:, at], out_ref[at, :])
        if start == 0:
            total_ref[...] = forward
            back_ref[...] = backward
        else:
            total_ref[...] += forward
            back_ref[...] += backward


def rest_kernel(
    meta_ref,
    hidden_ref,
    grad_rows,
    norm_ref,
    old_total_ref,
    old_back_ref,
    gain_ref,
    wo_ref,
    pack_a,
    pack_b,
    hidden_a,
    hidden_b,
    mixed_grad_ref,
    out_own_ref,
    hidden_own_ref,
    *refs,
):
    heads = (len(refs) - 2) // 2 + 1
    total_ref, back_ref = refs[-2:]
    width = norm_ref.shape[1]
    forward, backward = ffn_step(norm_ref, grad_rows, hidden_a[:width, :], hidden_a[width:, :])
    total_ref[...] = old_total_ref[...] + forward
    back_ref[...] = old_back_ref[...] + backward
    forward, backward = ffn_step(norm_ref, grad_rows, hidden_b[:width, :], hidden_b[width:, :])
    hidden_in = hidden_ref[...]
    result = (hidden_in + (total_ref[...] + forward)).astype(BF16)
    group = meta_ref[0, GROUP_COL]
    share = out_own_ref.shape[1]
    out_own_ref[...] = chunk(result, group, share)
    for k in range(1, heads):
        refs[k - 1][...] = chunk(result, below(group, k, heads), share)
    scale = row_scale(hidden_in)
    second_norm = hidden_in * scale
    scaled = (back_ref[...] + backward) * gain_ref[...]
    hidden_grad = grad_rows[...].astype(F32) + scale * (
        scaled - second_norm * jnp.mean(scaled * second_norm, axis=-1, keepdims=True)
    )
    hidden_own_ref[...] = chunk(hidden_grad, group, share)
    for k in range(1, heads):
        refs[heads + k - 2][...] = chunk(hidden_grad, below(group, k, heads), share)
    narrow = hidden_grad.astype(BF16)
    half = wo_ref.shape[0]
    mixed_grad_ref[:, :half] = dot_nt(narrow, wo_ref[...]).astype(BF16)
    mixed_grad_ref[:, half:] = dot_nn(narrow, packed((pack_a, pack_b), 3)).astype(BF16)


def back_operands(queries_ref, mixed_grad_ref, attended_t_ref, grad_t_ref, deltas_ref):
    block = 128
    pairs = queries_ref.shape[1] // PAIR

    @pl.loop(0, queries_ref.shape[0] // block)
    def _(b):
        here = pl.ds(pl.multiple_of(b * block, block), block)
        for p in range(pairs):
            cols = slice(p * PAIR, (p + 1) * PAIR)
            grad_t = both_heads_t(mixed_grad_ref[here, cols])
            grad_t_ref[b, p] = grad_t
            attended = attended_t_ref[b, cols, :].astype(F32)
            product = grad_t.astype(F32) * jnp.concatenate([attended, attended], axis=1)
            deltas_ref[pl.ds(b, 1), p * 2 * block : (p + 1) * 2 * block] = jnp.sum(product, axis=0, keepdims=True)


def scores_back(
    meta_ref,
    b,
    first,
    count,
    base,
    keys_ref,
    values_ref,
    keys_t_ref,
    operands,
    grad_keys,
    grad_values,
    rows_ref,
    acc_ref,
):
    queries_ref, query_t_ref, mixed_grad_ref, grad_t_ref, deltas_ref, log_total_ref = operands
    block = 128
    pairs = queries_ref.shape[1] // PAIR
    here = pl.ds(pl.multiple_of(b * block, block), block)
    deltas = []
    logs = []
    for p in range(pairs):
        cols = slice(p * PAIR, (p + 1) * PAIR)
        wide = slice(p * 2 * block, (p + 1) * 2 * block)
        rows_ref[0, p] = both_heads(queries_ref[here, cols])
        rows_ref[1, p] = both_heads(mixed_grad_ref[here, cols])
        deltas.append(deltas_ref[pl.ds(b, 1), wide])
        logs.append(log_total_ref[pl.ds(b, 1), wide])

    def step(slot, size, carried):
        indices = [meta_ref[b, first + slot + j] for j in range(size)]
        for p in range(pairs):
            cols = slice(p * PAIR, (p + 1) * PAIR)
            scores = dot_nn(block_rows(keys_ref, indices, cols), query_t_ref[b, p])
            probs = jnp.exp(scores - logs[p])
            prob_grad = dot_nn(block_rows(values_ref, indices, cols), grad_t_ref[b, p])
            score_grad = (probs * (prob_grad - deltas[p])).astype(BF16)
            to_values = dot_nn(probs.astype(BF16), rows_ref[1, p])
            to_keys = dot_nn(score_grad, rows_ref[0, p])
            here = [index - base for index in indices]
            acc_ref[p] += dot_nn(block_cols(keys_t_ref, here, cols), score_grad)
            for j in range(size):
                at = pl.ds(pl.multiple_of(here[j] * block, block), block)
                grad_values[at, cols] += to_values[j * block : (j + 1) * block]
                grad_keys[at, cols] += to_keys[j * block : (j + 1) * block]
        return carried

    by_two(count, step, 0)


def clear_back(keys_ref, keys_t_ref, grad_keys, grad_values, base):
    @pl.loop(0, grad_keys.shape[0] // 128)
    def _(kb):
        at = pl.ds(pl.multiple_of(kb * 128, 128), 128)
        grad_keys[at, :] = jnp.zeros((128, grad_keys.shape[1]), F32)
        grad_values[at, :] = jnp.zeros((128, grad_keys.shape[1]), F32)
        keys_t_ref[kb] = keys_ref[pl.ds(pl.multiple_of((kb + base) * 128, 128), 128), :].T


def project_back(grad_keys, grad_values, wk, wv, start, size):
    at = slice(start, start + size)
    keys_part = dot_nt(grad_keys[at, :].astype(BF16), wk)
    return keys_part + dot_nt(grad_values[at, :].astype(BF16), wv)


def side_back_kernel(
    side,
    meta_ref,
    keys_ref,
    values_ref,
    queries_ref,
    query_t_ref,
    mixed_grad_ref,
    log_total_ref,
    wk_ref,
    wv_ref,
    pack_a,
    pack_b,
    *refs,
):
    acc_ref, grad_keys, grad_values, keys_t_ref, rows_ref = refs[-5:]
    if side == 0:
        attended_t_ref, *grads, grad_t_ref, deltas_ref = refs[:-5]
        back_operands(queries_ref, mixed_grad_ref, attended_t_ref, grad_t_ref, deltas_ref)
    else:
        grad_t_ref, deltas_ref, old_acc_ref, *grads = refs[:-5]
    operands = queries_ref, query_t_ref, mixed_grad_ref, grad_t_ref, deltas_ref, log_total_ref
    base = side * keys_t_ref.shape[0]
    clear_back(keys_ref, keys_t_ref, grad_keys, grad_values, base)

    @pl.loop(0, queries_ref.shape[0] // 128)
    def _(b):
        own, low = meta_ref[b, OWN_COL], meta_ref[b, LOW_COL]
        acc_ref[b] = jnp.zeros(acc_ref.shape[1:], F32) if side == 0 else old_acc_ref[b]
        scores_back(
            meta_ref,
            b,
            own if side == 0 else own + low,
            low if side == 0 else meta_ref[b, COUNT_COL] - own - low,
            base,
            keys_ref,
            values_ref,
            keys_t_ref,
            operands,
            grad_keys,
            grad_values,
            rows_ref,
            acc_ref.at[b],
        )

    packs = (pack_a, pack_b)
    weights = joined(wk_ref, packs, 1), joined(wv_ref, packs, 2)
    start = 0
    for ref in grads:
        for part in range(0, ref.shape[0], 512):
            ref[part : part + 512, :] = project_back(
                grad_keys, grad_values, *weights, start + part, 512
            ).astype(BF16)
        start += ref.shape[0]


def own_back_kernel(
    meta_ref,
    keys_ref,
    values_ref,
    queries_ref,
    query_t_ref,
    mixed_grad_ref,
    grad_t_ref,
    deltas_ref,
    log_total_ref,
    old_acc_ref,
    wq_ref,
    wk_ref,
    wv_ref,
    pack_a,
    pack_b,
    own_ref,
    grad_keys,
    grad_values,
    keys_t_ref,
    rows_ref,
    acc_ref,
    query_grad,
):
    operands = queries_ref, query_t_ref, mixed_grad_ref, grad_t_ref, deltas_ref, log_total_ref
    block = 128
    rows = own_ref.shape[0]
    pairs = queries_ref.shape[1] // PAIR
    blocks = queries_ref.shape[0] // block
    clear_back(keys_ref, keys_t_ref, grad_keys, grad_values, 0)

    @pl.loop(0, blocks)
    def _(b):
        acc_ref[...] = old_acc_ref[b]
        scores_back(
            meta_ref,
            b,
            0,
            meta_ref[b, OWN_COL],
            0,
            keys_ref,
            values_ref,
            keys_t_ref,
            operands,
            grad_keys,
            grad_values,
            rows_ref,
            acc_ref,
        )
        for p in range(pairs):
            found = own_heads(acc_ref[p]) * (HD ** (-0.5))
            query_grad[pl.ds(pl.multiple_of(b * block, block), block), p * PAIR : (p + 1) * PAIR] = found.T.astype(BF16)

    packs = (pack_a, pack_b)
    weights = joined(wk_ref, packs, 1), joined(wv_ref, packs, 2)
    for start in range(0, rows, 512):
        own_ref[start : start + 512, :] = project_back(grad_keys, grad_values, *weights, start, 512)
    parts = dot_nt(query_grad[...], joined(wq_ref, packs, 0))
    for b in range(blocks):
        first = pl.multiple_of(meta_ref[b, BLOCK_COL] * block, block)
        own_ref[pl.ds(first, block), :] += parts[b * block : (b + 1) * block]


def term_kernel(offset, meta_ref, own_ref, low_ref, high_ref, ordered_ref, gain_ref, term_ref, dots_ref, *send_refs):
    rows, share = term_ref.shape
    heads = len(send_refs) + 1
    group = meta_ref[0, GROUP_COL]
    dot_rows = []
    for start in range(0, rows, 128):
        at = slice(start, start + 128)
        whole = slice(offset + start, offset + start + 128)
        term = own_ref[whole, :] + low_ref[whole, :].astype(F32) + high_ref[at, :].astype(F32)
        ordered = ordered_ref[whole, :].astype(F32)
        norm = ordered * row_scale(ordered)
        dots = jnp.sum(term * gain_ref[...] * norm, axis=-1, keepdims=True)
        dot_rows.append(jnp.broadcast_to(dots, (128, 128)).T[:1])
        term_ref[at, :] = chunk(term, group, share)
        for k in range(1, heads):
            send_refs[k - 1][at, :] = chunk(term, below(group, k, heads), share).astype(BF16)
    dots = jnp.concatenate(dot_rows, axis=0)
    dots_ref[...] = dots
    high = dots.astype(BF16)
    low = (dots - high.astype(F32)).astype(BF16)
    wide = min(share, 128)
    tail = jnp.concatenate(
        [half[:, start : start + wide] for half in (high, low) for start in range(0, 128, wide)], axis=0
    )
    if share > wide:
        tail = jnp.concatenate([tail] * (share // wide), axis=1)
    for ref in send_refs:
        ref[rows:, :] = tail


def dots_of(tail):
    wide = min(tail.shape[1], 128)
    count = 128 // wide
    size = tail.shape[0] // (2 * count)
    parts = [tail[i * size : (i + 1) * size, :wide].astype(F32) for i in range(2 * count)]
    sums = [parts[i] + parts[count + i] for i in range(count)]
    return sums[0] if count == 1 else jnp.concatenate(sums, axis=1)


def back_matrix(pos_ref, first, size, total):
    place = lax.broadcasted_iota(jnp.int32, (size, total), 0) + first
    return jnp.where(jnp.broadcast_to(places(pos_ref, 0, total), (size, total)) == place, 1.0, 0.0).astype(BF16)


def place_blocks(meta_ref, refs, all_ref):
    block = 128
    blocks = refs[0].shape[0] // block
    for k, ref in enumerate(refs):
        for b in range(blocks):
            first = pl.multiple_of(meta_ref[k * blocks + b, BLOCK_COL] * block, block)
            all_ref[pl.ds(first, block), :] = ref[b * block : (b + 1) * block, :]


def output_kernel(meta_ref, pos_ref, *refs):
    out_ref, matrix_ref, all_ref = refs[-3:]
    place_blocks(meta_ref, refs[:-3], all_ref)
    total = all_ref.shape[0]
    for first in range(0, total, 512):
        matrix = back_matrix(pos_ref, first, 512, total)
        matrix_ref[first : first + 512, :] = matrix
        out_ref[first : first + 512, :] = dot_nn(matrix, all_ref[...]).astype(BF16)


def final_kernel(meta_ref, matrix_ref, term_a, dots_a, term_b, dots_b, ordered_ref, gain_ref, *refs):
    out_ref, all_ref, split_ref = refs[-3:]
    heads = (len(refs) - 3 + 2) // 3
    place_blocks(meta_ref, refs[:heads], all_ref)
    total, share = out_ref.shape
    half = total // 2
    group = meta_ref[0, GROUP_COL]
    gain = chunk(gain_ref[...], group, share)
    for i, (term_ref, dots_ref) in enumerate(((term_a, dots_a), (term_b, dots_b))):
        got_refs = refs[heads + i * (heads - 1) : heads + (i + 1) * (heads - 1)]
        dots = dots_ref[...]
        for ref in got_refs:
            dots = dots + dots_of(ref[half:, :])
        dots = dots * (1.0 / ordered_ref.shape[1])
        for start in range(0, half, 128):
            at = slice(start, start + 128)
            whole = slice(i * half + start, i * half + start + 128)
            ordered = ordered_ref[whole, :].astype(F32)
            scale = row_scale(ordered)
            part = chunk(ordered, group, share) * scale
            mean = column_of(dots[start // 128 : start // 128 + 1], 128)[:, :1]
            term = term_ref[at, :]
            for ref in got_refs:
                term = term + ref[at, :].astype(F32)
            value = all_ref[whole, :] + scale * (term * gain - part * mean)
            high = value.astype(BF16)
            split_ref[whole, :share] = high
            split_ref[whole, share:] = (value - high.astype(F32)).astype(BF16)
    for first in range(0, total, 512):
        found = dot_nn(matrix_ref[first : first + 512, :], split_ref[...])
        out_ref[first : first + 512, :] = found[:, :share] + found[:, share:]


def local(
    features,
    out_grad,
    bin_order,
    key_lists,
    list_counts,
    attn_gain,
    query_weight,
    key_weight,
    value_weight,
    out_weight,
    ffn_gain,
    ffn_in,
    ffn_out,
):
    rows, width = features.shape
    block_count, slots = key_lists.shape
    block = rows // block_count
    share = query_weight.shape[1]
    hidden = ffn_in.shape[1]
    region = lax.axis_index("elem")
    regions = lax.axis_size("elem")
    group = lax.axis_index("head")
    head_groups = lax.axis_size("head")
    half_count = block_count // head_groups
    mine_rows = rows // head_groups
    forward = [(i, (i + 1) % regions) for i in range(regions)]
    backward = [(target, source) for source, target in forward]
    sibling = [(i, i ^ 1) for i in range(regions)]

    def exchanged(pieces):
        return [
            lax.ppermute(piece, "head", [(i, (i + k) % head_groups) for i in range(head_groups)])
            for k, piece in enumerate(pieces, 1)
        ]

    positions = bin_order.reshape(1, rows)
    gain_one = attn_gain.reshape(1, width)
    gain_two = ffn_gain.reshape(1, width)

    normed = call(prep_kernel, shaped((rows, width), BF16), [VMEM] * 3, vmem=60)(positions, features, gain_one)
    low = lax.ppermute(normed, "elem", forward)
    high = lax.ppermute(normed, "elem", backward)
    meta = pl.pallas_call(
        functools.partial(plan_kernel, head_groups),
        out_shape=shaped((block_count, META_COLS), jnp.int32),
        in_specs=[SMEM] * 3,
        out_specs=SMEM,
    )(jnp.stack([region, jnp.int32(regions), group, group]), key_lists, list_counts)

    ordered, grad_sorted = call(
        sort_kernel, (shaped((rows, width), BF16), shaped((rows, width), BF16)), [VMEM] * 3
    )(positions, features, out_grad)

    projections = (query_weight, key_weight, value_weight)
    if head_groups == 2:

        def my_piece(weight, core, dim):
            size = weight.shape[dim] // 2
            return lax.dynamic_slice_in_dim(weight, core * size, size, dim)

        core, normed = lax.optimization_barrier((region % 2, normed))
        mix = my_piece(out_weight, core, 0).T
        pack = jnp.concatenate([*[my_piece(w, core, 1) for w in projections], mix], axis=1)
        core, pack = lax.optimization_barrier((core, pack))
        (pack_a,) = exchanged([pack])
        hidden_pack = jnp.concatenate([my_piece(ffn_in, core, 1), my_piece(ffn_out, core, 0)], axis=0)
        (hidden_a,) = exchanged([hidden_pack])
        pack_a, meta, ordered, grad_sorted, hidden_pack = lax.optimization_barrier(
            (pack_a, meta, ordered, grad_sorted, hidden_pack)
        )
        pack_b = lax.ppermute(pack_a, "elem", sibling)
    else:

        def pieces(weight, dim):
            size = weight.shape[dim] * head_groups // 4
            whole = lax.all_gather(weight, "head", axis=dim, tiled=True)
            return jnp.split(whole, (2 * size, 3 * size), axis=dim)

        split = [pieces(w, 1) for w in projections]
        mixing = pieces(out_weight, 0)
        projections = tuple(parts[0] for parts in split)
        pack_a, pack_b = (
            jnp.concatenate([*[parts[i] for parts in split], mixing[i].T], axis=1) for i in (1, 2)
        )
        out_weight = mixing[0]
        ffn_in, *up_parts = pieces(ffn_in, 1)
        ffn_out, *down_parts = pieces(ffn_out, 0)
        hidden_a, hidden_b = (jnp.concatenate(parts, axis=0) for parts in zip(up_parts, down_parts))

    heads_width = head_groups * share
    key_value = (*projections[1:], pack_a, pack_b)
    pairs = heads_width // PAIR
    pair_tile = (pairs, PAIR, 2 * block)
    keep = pltpu.VMEM((slots, pairs, block, 2 * block), F32)
    stats = shaped((half_count, 2 * heads_width), F32)
    keys, values, queries, query_t, part_acc, part_peaks, part_sums = call(
        own_kernel,
        (
            shaped((rows, heads_width), BF16),
            shaped((rows, heads_width), BF16),
            shaped((mine_rows, heads_width), BF16),
            shaped((half_count,) + pair_tile, BF16),
            shaped((half_count,) + pair_tile, F32),
            stats,
            stats,
        ),
        [SMEM] + [VMEM] * 6,
        scratch=(
            keep,
            pltpu.VMEM((block_count, heads_width, block), BF16),
        ),
        vmem=26,
    )(meta, normed, *projections, pack_a, pack_b)
    halo_keys, halo_values, attended, attended_t, log_total = call(
        halo_kernel,
        (
            shaped((2 * rows, heads_width), BF16),
            shaped((2 * rows, heads_width), BF16),
            shaped((mine_rows, heads_width), BF16),
            shaped((half_count, heads_width, block), BF16),
            stats,
        ),
        [SMEM] + [VMEM] * 10,
        scratch=(
            keep,
            pltpu.VMEM((2 * block_count, heads_width, block), BF16),
            pltpu.VMEM(pair_tile, F32),
        ),
        vmem=30,
    )(meta, low, high, *key_value, query_t, part_acc, part_peaks, part_sums)

    square = shaped((mine_rows, width), F32)
    narrow = shaped((mine_rows, width), BF16)
    if head_groups == 2:
        attended, hidden_a = lax.optimization_barrier((attended, hidden_a))
        hidden_b = lax.ppermute(hidden_a, "elem", sibling)
    hidden_in, grad_rows, norm_two, part_total, part_back = call(
        ffn_kernel,
        (square, narrow, narrow, square, square),
        [SMEM] + [VMEM] * 9,
    )(meta, ordered, grad_sorted, attended, gain_two, out_weight, pack_a, pack_b, ffn_in, ffn_out)
    others = head_groups - 1
    mixed_grad, out_own, hidden_own, *sends = call(
        rest_kernel,
        (
            narrow,
            shaped((mine_rows, share), BF16),
            shaped((mine_rows, share), F32),
            *[shaped((mine_rows, share), BF16)] * others,
            *[shaped((mine_rows, share), F32)] * others,
        ),
        [SMEM] + [VMEM] * 11,
        scratch=(pltpu.VMEM((mine_rows, width), F32), pltpu.VMEM((mine_rows, width), F32)),
    )(
        meta,
        hidden_in,
        grad_rows,
        norm_two,
        part_total,
        part_back,
        gain_two,
        out_weight,
        pack_a,
        pack_b,
        hidden_a,
        hidden_b,
    )
    out_got = exchanged(sends[:others])
    hidden_got = exchanged(sends[others:])

    rows_pair = pltpu.VMEM((2, pairs, 2 * block, PAIR), BF16)
    half = rows // 2

    def side_back(side, grads, more, *extra):
        return call(
            functools.partial(side_back_kernel, side),
            (*[shaped((size, width), BF16) for size in grads], *more, shaped((half_count,) + pair_tile, F32)),
            [SMEM] + [VMEM] * (10 + len(extra)),
            scratch=(
                pltpu.VMEM((rows, heads_width), F32),
                pltpu.VMEM((rows, heads_width), F32),
                pltpu.VMEM((block_count, heads_width, block), BF16),
                rows_pair,
            ),
            vmem=24,
        )(meta, halo_keys, halo_values, queries, query_t, mixed_grad, log_total, *key_value, *extra)

    grad_low, grad_t, deltas, part_grad = side_back(
        0, (rows,), (shaped((half_count,) + pair_tile, BF16), stats), attended_t
    )
    from_right = lax.ppermute(grad_low, "elem", backward)
    grad_high_a, grad_high_b, part_grad = side_back(1, (half, half), (), grad_t, deltas, part_grad)
    from_left = [lax.ppermute(grad, "elem", forward) for grad in (grad_high_a, grad_high_b)]
    grad_own = call(
        own_back_kernel,
        shaped((rows, width), F32),
        [SMEM] + [VMEM] * 14,
        scratch=(
            pltpu.VMEM((rows, heads_width), F32),
            pltpu.VMEM((rows, heads_width), F32),
            pltpu.VMEM((block_count, heads_width, block), BF16),
            rows_pair,
            pltpu.VMEM(pair_tile, F32),
            pltpu.VMEM((mine_rows, heads_width), BF16),
        ),
        vmem=30,
    )(
        meta,
        keys,
        values,
        queries,
        query_t,
        mixed_grad,
        grad_t,
        deltas,
        log_total,
        part_grad,
        *projections,
        pack_a,
        pack_b,
    )
    from_right, out_got, hidden_got = lax.optimization_barrier((from_right, out_got, hidden_got))
    tail = 2 * (half // 128) * (128 // min(share, 128))
    terms, got = [], []
    for i in range(2):
        term, dots, *sends = call(
            functools.partial(term_kernel, i * half),
            (
                shaped((half, share), F32),
                shaped((half // 128, 128), F32),
                *[shaped((half + tail, share), BF16)] * others,
            ),
            [SMEM] + [VMEM] * 5,
        )(meta, grad_own, from_right, from_left[i], ordered, gain_one)
        terms += [term, dots]
        got += exchanged(sends)
    output, matrix = call(
        output_kernel,
        (shaped((rows, share), BF16), shaped((rows, rows), BF16)),
        [SMEM] + [VMEM] * (1 + head_groups),
        scratch=(pltpu.VMEM((rows, share), BF16),),
    )(meta, positions, out_own, *out_got)
    input_grad = call(
        final_kernel,
        shaped((rows, share), F32),
        [SMEM] + [VMEM] * (7 + head_groups + 2 * others),
        scratch=(pltpu.VMEM((rows, share), F32), pltpu.VMEM((rows, 2 * share), BF16)),
    )(meta, matrix, *terms, ordered, gain_one, hidden_own, *hidden_got, *got)
    return (output, input_grad)


def solution(mesh):
    in_specs = (
        P("elem", None),
        P("elem", None),
        P("elem"),
        P("elem", None),
        P("elem"),
        P(),
        P(None, "head"),
        P(None, "head"),
        P(None, "head"),
        P("head", None),
        P(),
        P(None, "head"),
        P("head", None),
    )
    out_specs = (P("elem", "head"), P("elem", "head"))
    return jax.shard_map(local, mesh=mesh, in_specs=in_specs, out_specs=out_specs, check_vma=False)
```

```python
import functools

import jax
import jax.numpy as jnp
from jax import lax
from jax.experimental import pallas as pl
from jax.experimental.pallas import tpu as pltpu
from jax.sharding import PartitionSpec as P

HD = 64
PAIR = 2 * HD
EPSILON = 1e-05
F32 = jnp.float32
BF16 = jnp.bfloat16
VMEM = pl.BlockSpec(memory_space=pltpu.VMEM)
SMEM = pl.BlockSpec(memory_space=pltpu.SMEM)
COUNT_COL = 12
BLOCK_COL = 13
GROUP_COL = 14
OWN_COL = 15
LOW_COL = 16
META_COLS = 128
COST = 1000


def dot_nn(a, b):
    return lax.dot_general(a, b, (((1,), (0,)), ((), ())), preferred_element_type=F32)


def dot_nt(a, b):
    return lax.dot_general(a, b, (((1,), (1,)), ((), ())), preferred_element_type=F32)


def row_scale(values):
    return lax.rsqrt(jnp.mean(values * values, axis=-1, keepdims=True) + EPSILON)


def call(kernel, out_shape, in_specs, scratch=(), vmem=16):
    out_specs = jax.tree.map(lambda _: VMEM, out_shape)
    return pl.pallas_call(
        kernel,
        out_shape=out_shape,
        in_specs=in_specs,
        out_specs=out_specs,
        scratch_shapes=list(scratch),
        compiler_params=pltpu.CompilerParams(vmem_limit_bytes=vmem << 20),
        cost_estimate=pl.CostEstimate(flops=COST, bytes_accessed=COST, transcendentals=0),
    )


def shaped(shape, dtype):
    return jax.ShapeDtypeStruct(shape, dtype)


def column_of(row, size):
    return jnp.broadcast_to(row, (size, size)).T


def sort_matrix(pos_ref, first, size, total):
    lanes = lax.broadcasted_iota(jnp.int32, (128, total), 1).astype(F32)
    parts = []
    for start in range(first, first + size, 128):
        column = column_of(places(pos_ref, start, 128).astype(F32), 128)
        wide = jnp.concatenate([column] * (total // 128), axis=1)
        parts.append(jnp.where(wide == lanes, 1.0, 0.0).astype(BF16))
    return jnp.concatenate(parts, axis=0)


def places(pos_ref, start, size):
    return lax.rem(pos_ref[:, start : start + size], pos_ref.shape[1])


def plan_kernel(head_groups, where_ref, lists_ref, counts_ref, meta_ref):
    blocks, slots = lists_ref.shape
    region, regions, group, heads = where_ref[0], where_ref[1], where_ref[2], head_groups
    counts = [counts_ref[i] for i in range(blocks)]
    for i in range(blocks):
        rank = jnp.int32(0)
        for j in range(blocks):
            if j != i:
                ahead = counts[j] >= counts[i] if j < i else counts[j] > counts[i]
                rank = rank + jnp.where(ahead, 1, 0)
        turn = rank // heads
        side = rank % heads
        side = jnp.where(turn % 2 == 1, heads - 1 - side, side)
        from_me = group - side
        from_me = jnp.where(from_me < 0, from_me + heads, from_me)
        row = from_me * (blocks // heads) + turn
        meta_ref[row, COUNT_COL] = counts[i]
        meta_ref[row, BLOCK_COL] = jnp.int32(i)
        meta_ref[row, GROUP_COL] = group
        entries = []
        own_total = low_total = jnp.int32(0)
        for s in range(slots):
            key = lists_ref[i, s]
            away = key // blocks - region + 1
            away = jnp.where(away < 0, away + regions, away)
            away = jnp.where(away >= regions, away - regions, away)
            entries.append((key % blocks + jnp.where(away == 2, blocks, 0), away))
            live = s < counts[i]
            own_total = own_total + jnp.where((away == 1) & live, 1, 0)
            low_total = low_total + jnp.where((away == 0) & live, 1, 0)
        meta_ref[row, OWN_COL] = own_total
        meta_ref[row, LOW_COL] = low_total
        own_next, low_next, high_next = jnp.int32(0), own_total, own_total + low_total
        for s in range(slots):
            index, away = entries[s]
            to = jnp.where(away == 1, own_next, jnp.where(away == 0, low_next, high_next))

            @pl.when(s < counts[i])
            def _(index=index, to=to):
                meta_ref[row, to] = index

            own_next = own_next + jnp.where(away == 1, 1, 0)
            low_next = low_next + jnp.where(away == 0, 1, 0)
            high_next = high_next + jnp.where(away == 2, 1, 0)


def prep_kernel(pos_ref, rows_ref, gain_ref, normed_ref):
    total = rows_ref.shape[0]
    for first in range(0, total, 512):
        picked = dot_nn(sort_matrix(pos_ref, first, 512, total), rows_ref[...])
        normed_ref[first : first + 512, :] = (picked * row_scale(picked) * gain_ref[...]).astype(BF16)


def sort_kernel(pos_ref, rows_ref, grads_ref, sorted_rows_ref, sorted_grads_ref):
    total = rows_ref.shape[0]
    for first in range(0, total, 512):
        matrix = sort_matrix(pos_ref, first, 512, total)
        sorted_rows_ref[first : first + 512, :] = dot_nn(matrix, rows_ref[...]).astype(BF16)
        sorted_grads_ref[first : first + 512, :] = dot_nn(matrix, grads_ref[...]).astype(BF16)


def chunk(values, who, share):
    out = values[:, :share]
    for start in range(share, values.shape[1], share):
        out = jnp.where(who == start // share, values[:, start : start + share], out)
    return out


def below(group, steps, count):
    who = group + steps
    return jnp.where(who >= count, who - count, who)


def both_heads(rows):
    lane = lax.broadcasted_iota(jnp.int32, rows.shape, 1)
    zero = jnp.zeros_like(rows)
    return jnp.concatenate([jnp.where(lane < HD, rows, zero), jnp.where(lane < HD, zero, rows)], axis=0)


def both_heads_t(rows):
    flipped = rows.T
    row = lax.broadcasted_iota(jnp.int32, flipped.shape, 0)
    zero = jnp.zeros_like(flipped)
    return jnp.concatenate([jnp.where(row < HD, flipped, zero), jnp.where(row < HD, zero, flipped)], axis=1)


def own_heads(wide):
    half = wide.shape[1] // 2
    return jnp.concatenate([wide[:HD, :half], wide[HD:, half:]], axis=0)


def groups_of_eight(tile, op):
    out = tile[:8]
    for start in range(8, tile.shape[0], 8):
        out = op(out, tile[start : start + 8])
    return out


def packed(packs, which):
    size = packs[0].shape[1] // 4
    return jnp.concatenate([ref[:, which * size : (which + 1) * size] for ref in packs], axis=1)


def joined(mine_ref, packs, which):
    return jnp.concatenate([mine_ref[...], packed(packs, which)], axis=1)


def project_keys(rows_ref, wk, wv, keys_ref, values_ref, values_t_ref, base):
    for start in range(0, rows_ref.shape[0], 512):
        at = slice(base + start, base + start + 512)
        here = rows_ref[start : start + 512, :]
        keys_ref[at, :] = dot_nn(here, wk).astype(BF16)
        found = dot_nn(here, wv).astype(BF16)
        values_ref[at, :] = found
        for part in range(4):
            values_t_ref[(base + start) // 128 + part] = found[part * 128 : part * 128 + 128, :].T


def block_rows(ref, indices, cols):
    return jnp.concatenate(
        [ref[pl.ds(pl.multiple_of(index * 128, 128), 128), cols] for index in indices], axis=0
    )


def block_cols(ref, indices, cols):
    return jnp.concatenate([ref[index, cols, :] for index in indices], axis=1)


def by_two(count, step, carried):
    carried = lax.fori_loop(0, count // 2, lambda i, c: step(2 * i, 2, c), carried)
    return lax.fori_loop(0, count % 2, lambda i, c: step(count - 1, 1, c), carried)


def attend(meta_ref, b, first, count, keys_ref, values_t_ref, query_t_ref, keep_ref, acc_ref, old):
    pairs = query_t_ref.shape[0]
    wide = query_t_ref.shape[2]

    def peak_step(slot, size, peaks):
        indices = [meta_ref[b, first + slot + j] for j in range(size)]
        out = []
        for p in range(pairs):
            cols = slice(p * PAIR, (p + 1) * PAIR)
            tile = dot_nn(block_rows(keys_ref, indices, cols), query_t_ref[p])
            for j in range(size):
                keep_ref[slot + j, p] = tile[j * 128 : (j + 1) * 128]
            out.append(jnp.maximum(peaks[p], groups_of_eight(tile, jnp.maximum)))
        return tuple(out)

    if old is None:
        start = (jnp.full((8, wide), -3.0e38, F32),) * pairs
    else:
        start = tuple(jnp.broadcast_to(peak, (8, wide)) for peak, _ in old)
    peaks = by_two(count, peak_step, start)
    peaks = tuple(jnp.max(peak, axis=0, keepdims=True) for peak in peaks)
    totals = []
    for p in range(pairs):
        if old is None:
            acc_ref[p] = jnp.zeros(acc_ref.shape[1:], F32)
            totals.append(jnp.zeros((1, wide), F32))
        else:
            shrink = jnp.exp(old[p][0] - peaks[p])
            acc_ref[p] = acc_ref[p] * shrink
            totals.append(old[p][1] * shrink)

    def sum_step(slot, size, sums):
        indices = [meta_ref[b, first + slot + j] for j in range(size)]
        out = []
        for p in range(pairs):
            cols = slice(p * PAIR, (p + 1) * PAIR)
            tile = jnp.concatenate([jnp.exp(keep_ref[slot + j, p] - peaks[p]) for j in range(size)], axis=0)
            out.append(sums[p] + groups_of_eight(tile, jnp.add))
            acc_ref[p] += dot_nn(block_cols(values_t_ref, indices, cols), tile.astype(BF16))
        return tuple(out)

    sums = by_two(count, sum_step, (jnp.zeros((8, wide), F32),) * pairs)
    return [
        (peaks[p], totals[p] + jnp.sum(sums[p], axis=0, keepdims=True)) for p in range(pairs)
    ]


def own_kernel(
    meta_ref,
    own_ref,
    wq_ref,
    wk_ref,
    wv_ref,
    pack_a,
    pack_b,
    keys_ref,
    values_ref,
    keys_t_ref,
    queries_ref,
    query_t_ref,
    acc_ref,
    peaks_ref,
    sums_ref,
    keep_ref,
    values_t_ref,
):
    block = 128
    pairs = queries_ref.shape[1] // PAIR
    packs = (pack_a, pack_b)
    project_keys(own_ref, joined(wk_ref, packs, 1), joined(wv_ref, packs, 2), keys_ref, values_ref, values_t_ref, 0)
    wq = joined(wq_ref, packs, 0)
    for kb in range(keys_t_ref.shape[0]):
        keys_t_ref[kb] = keys_ref[kb * block : (kb + 1) * block, :].T

    @pl.loop(0, queries_ref.shape[0] // block)
    def _(b):
        first = pl.multiple_of(meta_ref[b, BLOCK_COL] * block, block)
        query = dot_nn(own_ref[pl.ds(first, block), :], wq).astype(BF16)
        query = (query.astype(F32) * (HD ** (-0.5))).astype(BF16)
        queries_ref[pl.ds(pl.multiple_of(b * block, block), block), :] = query
        for p in range(pairs):
            query_t_ref[b, p] = both_heads_t(query[:, p * PAIR : (p + 1) * PAIR])
        found = attend(
            meta_ref,
            b,
            0,
            meta_ref[b, OWN_COL],
            keys_ref,
            values_t_ref,
            query_t_ref.at[b],
            keep_ref,
            acc_ref.at[b],
            None,
        )
        for p in range(pairs):
            at = slice(p * 2 * block, (p + 1) * 2 * block)
            peaks_ref[pl.ds(b, 1), at] = found[p][0]
            sums_ref[pl.ds(b, 1), at] = found[p][1]


def halo_kernel(
    meta_ref,
    low_ref,
    high_ref,
    wk_ref,
    wv_ref,
    pack_a,
    pack_b,
    query_t_ref,
    old_acc_ref,
    peaks_ref,
    sums_ref,
    keys_ref,
    values_ref,
    attended_ref,
    attended_t_ref,
    log_total_ref,
    keep_ref,
    values_t_ref,
    acc_ref,
):
    block = 128
    pairs = query_t_ref.shape[1]
    wk = joined(wk_ref, (pack_a, pack_b), 1)
    wv = joined(wv_ref, (pack_a, pack_b), 2)
    project_keys(low_ref, wk, wv, keys_ref, values_ref, values_t_ref, 0)
    project_keys(high_ref, wk, wv, keys_ref, values_ref, values_t_ref, low_ref.shape[0])

    @pl.loop(0, query_t_ref.shape[0])
    def _(b):
        here = pl.ds(pl.multiple_of(b * block, block), block)
        old = []
        for p in range(pairs):
            at = slice(p * 2 * block, (p + 1) * 2 * block)
            acc_ref[p] = old_acc_ref[b, p]
            old.append((peaks_ref[pl.ds(b, 1), at], sums_ref[pl.ds(b, 1), at]))
        own = meta_ref[b, OWN_COL]
        found = attend(
            meta_ref,
            b,
            own,
            meta_ref[b, COUNT_COL] - own,
            keys_ref,
            values_t_ref,
            query_t_ref.at[b],
            keep_ref,
            acc_ref,
            old,
        )
        for p in range(pairs):
            peak, total = found[p]
            log_total_ref[pl.ds(b, 1), p * 2 * block : (p + 1) * 2 * block] = peak + jnp.log(total)
            rows = own_heads(acc_ref[p] * (1.0 / total)).astype(BF16)
            attended_t_ref[b, p * PAIR : (p + 1) * PAIR, :] = rows
            attended_ref[here, p * PAIR : (p + 1) * PAIR] = rows.T


GELU_A = 0.044715
GELU_B = 0.7978845608028654


def ffn_step(norm_ref, grad_ref, up, down):
    pre = dot_nn(norm_ref[...], up)
    square = pre * pre
    inner = jnp.tanh(GELU_B * pre * (1.0 + GELU_A * square))
    gate = 0.5 * (1.0 + inner)
    active = (pre * gate).astype(BF16)
    slope = gate + (0.5 * GELU_B) * pre * (1.0 - inner * inner) * (1.0 + (3.0 * GELU_A) * square)
    grad_pre = (dot_nt(grad_ref[...], down) * slope).astype(BF16)
    return dot_nn(active, down), dot_nt(grad_pre, up)


def ffn_kernel(
    meta_ref,
    ordered_ref,
    grad_ref,
    attended_ref,
    gain_ref,
    wo_ref,
    pack_a,
    pack_b,
    in_ref,
    out_ref,
    hidden_ref,
    grad_rows,
    norm_ref,
    total_ref,
    back_ref,
):
    block = 128
    size = attended_ref.shape[0]
    for b in range(size // block):
        first = pl.multiple_of(meta_ref[b, BLOCK_COL] * block, block)
        hidden_ref[b * block : (b + 1) * block, :] = ordered_ref[pl.ds(first, block), :].astype(F32)
        grad_rows[b * block : (b + 1) * block, :] = grad_ref[pl.ds(first, block), :]
    share = wo_ref.shape[0]
    hidden_in = hidden_ref[...] + dot_nn(attended_ref[:, :share], wo_ref[...])
    hidden_in = hidden_in + dot_nt(attended_ref[:, share:], packed((pack_a, pack_b), 3))
    hidden_ref[...] = hidden_in
    norm_ref[...] = (hidden_in * row_scale(hidden_in) * gain_ref[...]).astype(BF16)
    for start in range(0, in_ref.shape[1], 512):
        at = slice(start, start + 512)
        forward, backward = ffn_step(norm_ref, grad_rows, in_ref[:, at], out_ref[at, :])
        if start == 0:
            total_ref[...] = forward
            back_ref[...] = backward
        else:
            total_ref[...] += forward
            back_ref[...] += backward


def rest_kernel(
    meta_ref,
    hidden_ref,
    grad_rows,
    norm_ref,
    old_total_ref,
    old_back_ref,
    gain_ref,
    wo_ref,
    pack_a,
    pack_b,
    hidden_a,
    hidden_b,
    mixed_grad_ref,
    out_own_ref,
    hidden_own_ref,
    *refs,
):
    heads = len(refs) - 1
    total_ref, back_ref = refs[-2:]
    width = norm_ref.shape[1]
    forward, backward = ffn_step(norm_ref, grad_rows, hidden_a[:width, :], hidden_a[width:, :])
    total_ref[...] = old_total_ref[...] + forward
    back_ref[...] = old_back_ref[...] + backward
    forward, backward = ffn_step(norm_ref, grad_rows, hidden_b[:width, :], hidden_b[width:, :])
    hidden_in = hidden_ref[...]
    result = (hidden_in + (total_ref[...] + forward)).astype(BF16)
    group = meta_ref[0, GROUP_COL]
    share = out_own_ref.shape[1]
    out_own_ref[...] = chunk(result, group, share)
    scale = row_scale(hidden_in)
    second_norm = hidden_in * scale
    scaled = (back_ref[...] + backward) * gain_ref[...]
    hidden_grad = grad_rows[...].astype(F32) + scale * (
        scaled - second_norm * jnp.mean(scaled * second_norm, axis=-1, keepdims=True)
    )
    hidden_own_ref[...] = chunk(hidden_grad, group, share)
    for k in range(1, heads):
        who = below(group, k, heads)
        refs[k - 1][:, :share] = chunk(result, who, share)
        refs[k - 1][:, share:] = chunk(hidden_grad, who, share).astype(BF16)
    narrow = hidden_grad.astype(BF16)
    half = wo_ref.shape[0]
    mixed_grad_ref[:, :half] = dot_nt(narrow, wo_ref[...]).astype(BF16)
    mixed_grad_ref[:, half:] = dot_nn(narrow, packed((pack_a, pack_b), 3)).astype(BF16)


def back_operands(queries_ref, mixed_grad_ref, attended_t_ref, grad_t_ref, deltas_ref):
    block = 128
    pairs = queries_ref.shape[1] // PAIR

    @pl.loop(0, queries_ref.shape[0] // block)
    def _(b):
        here = pl.ds(pl.multiple_of(b * block, block), block)
        for p in range(pairs):
            cols = slice(p * PAIR, (p + 1) * PAIR)
            grad_t = both_heads_t(mixed_grad_ref[here, cols])
            grad_t_ref[b, p] = grad_t
            attended = attended_t_ref[b, cols, :].astype(F32)
            product = grad_t.astype(F32) * jnp.concatenate([attended, attended], axis=1)
            deltas_ref[pl.ds(b, 1), p * 2 * block : (p + 1) * 2 * block] = jnp.sum(product, axis=0, keepdims=True)


def scores_back(
    meta_ref,
    b,
    first,
    count,
    base,
    keys_ref,
    values_ref,
    keys_t_ref,
    operands,
    grad_keys,
    grad_values,
    rows_ref,
    acc_ref,
):
    queries_ref, query_t_ref, mixed_grad_ref, grad_t_ref, deltas_ref, log_total_ref = operands
    block = 128
    pairs = queries_ref.shape[1] // PAIR
    here = pl.ds(pl.multiple_of(b * block, block), block)
    deltas = []
    logs = []
    for p in range(pairs):
        cols = slice(p * PAIR, (p + 1) * PAIR)
        wide = slice(p * 2 * block, (p + 1) * 2 * block)
        rows_ref[0, p] = both_heads(queries_ref[here, cols])
        rows_ref[1, p] = both_heads(mixed_grad_ref[here, cols])
        deltas.append(deltas_ref[pl.ds(b, 1), wide])
        logs.append(log_total_ref[pl.ds(b, 1), wide])

    def step(slot, size, carried):
        indices = [meta_ref[b, first + slot + j] for j in range(size)]
        for p in range(pairs):
            cols = slice(p * PAIR, (p + 1) * PAIR)
            scores = dot_nn(block_rows(keys_ref, indices, cols), query_t_ref[b, p])
            probs = jnp.exp(scores - logs[p])
            prob_grad = dot_nn(block_rows(values_ref, indices, cols), grad_t_ref[b, p])
            score_grad = (probs * (prob_grad - deltas[p])).astype(BF16)
            to_values = dot_nn(probs.astype(BF16), rows_ref[1, p])
            to_keys = dot_nn(score_grad, rows_ref[0, p])
            here = [index - base for index in indices]
            acc_ref[p] += dot_nn(block_cols(keys_t_ref, here, cols), score_grad)
            for j in range(size):
                at = pl.ds(pl.multiple_of(here[j] * block, block), block)
                grad_values[at, cols] += to_values[j * block : (j + 1) * block]
                grad_keys[at, cols] += to_keys[j * block : (j + 1) * block]
        return carried

    by_two(count, step, 0)


def clear_back(grad_keys, grad_values):
    @pl.loop(0, grad_keys.shape[0] // 128)
    def _(kb):
        at = pl.ds(pl.multiple_of(kb * 128, 128), 128)
        grad_keys[at, :] = jnp.zeros((128, grad_keys.shape[1]), F32)
        grad_values[at, :] = jnp.zeros((128, grad_keys.shape[1]), F32)


def project_back(grad_keys, grad_values, wk, wv, start, size):
    at = slice(start, start + size)
    keys_part = dot_nt(grad_keys[at, :].astype(BF16), wk)
    return keys_part + dot_nt(grad_values[at, :].astype(BF16), wv)


def side_back_kernel(
    side,
    meta_ref,
    keys_ref,
    values_ref,
    queries_ref,
    query_t_ref,
    mixed_grad_ref,
    log_total_ref,
    wk_ref,
    wv_ref,
    pack_a,
    pack_b,
    *refs,
):
    acc_ref, grad_keys, grad_values, keys_t_ref, rows_ref = refs[-5:]
    if side == 0:
        attended_t_ref, *grads, grad_t_ref, deltas_ref = refs[:-5]
        back_operands(queries_ref, mixed_grad_ref, attended_t_ref, grad_t_ref, deltas_ref)
    else:
        grad_t_ref, deltas_ref, old_acc_ref, *grads = refs[:-5]
    operands = queries_ref, query_t_ref, mixed_grad_ref, grad_t_ref, deltas_ref, log_total_ref
    base = side * keys_t_ref.shape[0]
    clear_back(grad_keys, grad_values)

    @pl.loop(0, keys_t_ref.shape[0])
    def _(kb):
        keys_t_ref[kb] = keys_ref[pl.ds(pl.multiple_of((kb + base) * 128, 128), 128), :].T

    @pl.loop(0, queries_ref.shape[0] // 128)
    def _(b):
        own, low = meta_ref[b, OWN_COL], meta_ref[b, LOW_COL]
        acc_ref[b] = jnp.zeros(acc_ref.shape[1:], F32) if side == 0 else old_acc_ref[b]
        scores_back(
            meta_ref,
            b,
            own if side == 0 else own + low,
            low if side == 0 else meta_ref[b, COUNT_COL] - own - low,
            base,
            keys_ref,
            values_ref,
            keys_t_ref,
            operands,
            grad_keys,
            grad_values,
            rows_ref,
            acc_ref.at[b],
        )

    packs = (pack_a, pack_b)
    weights = joined(wk_ref, packs, 1), joined(wv_ref, packs, 2)
    start = 0
    for ref in grads:
        for part in range(0, ref.shape[0], 512):
            ref[part : part + 512, :] = project_back(
                grad_keys, grad_values, *weights, start + part, 512
            ).astype(BF16)
        start += ref.shape[0]


def own_back_kernel(
    meta_ref,
    keys_ref,
    values_ref,
    keys_t_ref,
    queries_ref,
    query_t_ref,
    mixed_grad_ref,
    grad_t_ref,
    deltas_ref,
    log_total_ref,
    old_acc_ref,
    wq_ref,
    wk_ref,
    wv_ref,
    pack_a,
    pack_b,
    own_ref,
    grad_keys,
    grad_values,
    rows_ref,
    acc_ref,
    query_grad,
):
    operands = queries_ref, query_t_ref, mixed_grad_ref, grad_t_ref, deltas_ref, log_total_ref
    block = 128
    rows = own_ref.shape[0]
    pairs = queries_ref.shape[1] // PAIR
    blocks = queries_ref.shape[0] // block
    clear_back(grad_keys, grad_values)

    @pl.loop(0, blocks)
    def _(b):
        acc_ref[...] = old_acc_ref[b]
        scores_back(
            meta_ref,
            b,
            0,
            meta_ref[b, OWN_COL],
            0,
            keys_ref,
            values_ref,
            keys_t_ref,
            operands,
            grad_keys,
            grad_values,
            rows_ref,
            acc_ref,
        )
        for p in range(pairs):
            found = own_heads(acc_ref[p]) * (HD ** (-0.5))
            query_grad[pl.ds(pl.multiple_of(b * block, block), block), p * PAIR : (p + 1) * PAIR] = found.T.astype(BF16)

    packs = (pack_a, pack_b)
    weights = joined(wk_ref, packs, 1), joined(wv_ref, packs, 2)
    for start in range(0, rows, 512):
        own_ref[start : start + 512, :] = project_back(grad_keys, grad_values, *weights, start, 512)
    parts = dot_nt(query_grad[...], joined(wq_ref, packs, 0))
    for b in range(blocks):
        first = pl.multiple_of(meta_ref[b, BLOCK_COL] * block, block)
        own_ref[pl.ds(first, block), :] += parts[b * block : (b + 1) * block]


def term_kernel(offset, meta_ref, own_ref, low_ref, high_ref, normed_ref, term_ref, dots_ref, *send_refs):
    rows, share = term_ref.shape
    heads = len(send_refs) + 1
    group = meta_ref[0, GROUP_COL]
    dot_rows = []
    for start in range(0, rows, 128):
        at = slice(start, start + 128)
        whole = slice(offset + start, offset + start + 128)
        term = own_ref[whole, :] + low_ref[whole, :].astype(F32) + high_ref[at, :].astype(F32)
        dots = jnp.sum(term * normed_ref[whole, :].astype(F32), axis=-1, keepdims=True)
        dot_rows.append(jnp.broadcast_to(dots, (128, 128)).T[:1])
        term_ref[at, :] = chunk(term, group, share)
        for k in range(1, heads):
            send_refs[k - 1][at, :] = chunk(term, below(group, k, heads), share).astype(BF16)
    dots = jnp.concatenate(dot_rows, axis=0)
    dots_ref[...] = dots
    high = dots.astype(BF16)
    low = (dots - high.astype(F32)).astype(BF16)
    wide = min(share, 128)
    tail = jnp.concatenate(
        [half[:, start : start + wide] for half in (high, low) for start in range(0, 128, wide)], axis=0
    )
    if share > wide:
        tail = jnp.concatenate([tail] * (share // wide), axis=1)
    for ref in send_refs:
        ref[rows:, :] = tail


def dots_of(tail):
    wide = min(tail.shape[1], 128)
    count = 128 // wide
    size = tail.shape[0] // (2 * count)
    parts = [tail[i * size : (i + 1) * size, :wide].astype(F32) for i in range(2 * count)]
    sums = [parts[i] + parts[count + i] for i in range(count)]
    return sums[0] if count == 1 else jnp.concatenate(sums, axis=1)


def back_matrix(pos_ref, first, size, total):
    place = lax.broadcasted_iota(jnp.int32, (size, total), 0) + first
    return jnp.where(jnp.broadcast_to(places(pos_ref, 0, total), (size, total)) == place, 1.0, 0.0).astype(BF16)


def place_blocks(meta_ref, refs, all_ref, first_col):
    block = 128
    share = all_ref.shape[1]
    blocks = refs[0].shape[0] // block
    for k, ref in enumerate(refs):
        cols = slice(0, share) if k == 0 else slice(first_col, first_col + share)
        for b in range(blocks):
            first = pl.multiple_of(meta_ref[k * blocks + b, BLOCK_COL] * block, block)
            all_ref[pl.ds(first, block), :] = ref[b * block : (b + 1) * block, cols].astype(all_ref.dtype)


def output_kernel(meta_ref, pos_ref, ordered_ref, gain_ref, hidden_own_ref, *refs):
    out_ref, matrix_ref, base_ref, scale_ref, norm_ref, all_ref = refs[-6:]
    own_ref, *got_refs = refs[:-6]
    place_blocks(meta_ref, [own_ref, *got_refs], all_ref, 0)
    total, share = all_ref.shape
    place_blocks(meta_ref, [hidden_own_ref, *got_refs], base_ref, share)
    for first in range(0, total, 512):
        matrix = back_matrix(pos_ref, first, 512, total)
        matrix_ref[first : first + 512, :] = matrix
        out_ref[first : first + 512, :] = dot_nn(matrix, all_ref[...]).astype(BF16)
    group = meta_ref[0, GROUP_COL]
    gain = chunk(gain_ref[...], group, share)
    for start in range(0, total, 128):
        at = slice(start, start + 128)
        ordered = ordered_ref[at, :].astype(F32)
        scale = row_scale(ordered)
        scale_ref[at, :] = scale * gain
        norm_ref[at, :] = chunk(ordered, group, share) * (scale * scale)


def final_kernel(matrix_ref, base_ref, scale_ref, norm_ref, term_a, dots_a, term_b, dots_b, *refs):
    out_ref, split_ref = refs[-2:]
    total, share = out_ref.shape
    half = total // 2
    others = (len(refs) - 2) // 2
    for i, (term_ref, dots_ref) in enumerate(((term_a, dots_a), (term_b, dots_b))):
        got_refs = refs[i * others : (i + 1) * others]
        dots = dots_ref[...]
        for ref in got_refs:
            dots = dots + dots_of(ref[half:, :])
        dots = dots * (1.0 / (share * (others + 1)))
        for start in range(0, half, 128):
            at = slice(start, start + 128)
            whole = slice(i * half + start, i * half + start + 128)
            mean = column_of(dots[start // 128 : start // 128 + 1], 128)[:, :1]
            term = term_ref[at, :]
            for ref in got_refs:
                term = term + ref[at, :].astype(F32)
            value = base_ref[whole, :] + (term * scale_ref[whole, :] - norm_ref[whole, :] * mean)
            high = value.astype(BF16)
            split_ref[whole, :share] = high
            split_ref[whole, share:] = (value - high.astype(F32)).astype(BF16)
    for first in range(0, total, 512):
        found = dot_nn(matrix_ref[first : first + 512, :], split_ref[...])
        out_ref[first : first + 512, :] = found[:, :share] + found[:, share:]


def local(
    features,
    out_grad,
    bin_order,
    key_lists,
    list_counts,
    attn_gain,
    query_weight,
    key_weight,
    value_weight,
    out_weight,
    ffn_gain,
    ffn_in,
    ffn_out,
):
    rows, width = features.shape
    block_count, slots = key_lists.shape
    block = rows // block_count
    share = query_weight.shape[1]
    hidden = ffn_in.shape[1]
    region = lax.axis_index("elem")
    regions = lax.axis_size("elem")
    group = lax.axis_index("head")
    head_groups = lax.axis_size("head")
    half_count = block_count // head_groups
    mine_rows = rows // head_groups
    forward = [(i, (i + 1) % regions) for i in range(regions)]
    backward = [(target, source) for source, target in forward]
    sibling = [(i, i ^ 1) for i in range(regions)]

    def exchanged(pieces):
        return [
            lax.ppermute(piece, "head", [(i, (i + k) % head_groups) for i in range(head_groups)])
            for k, piece in enumerate(pieces, 1)
        ]

    positions = bin_order.reshape(1, rows)
    gain_one = attn_gain.reshape(1, width)
    gain_two = ffn_gain.reshape(1, width)

    normed = call(prep_kernel, shaped((rows, width), BF16), [VMEM] * 3, vmem=60)(positions, features, gain_one)
    low = lax.ppermute(normed, "elem", forward)
    high = lax.ppermute(normed, "elem", backward)
    meta = pl.pallas_call(
        functools.partial(plan_kernel, head_groups),
        out_shape=shaped((block_count, META_COLS), jnp.int32),
        in_specs=[SMEM] * 3,
        out_specs=SMEM,
    )(jnp.stack([region, jnp.int32(regions), group, group]), key_lists, list_counts)

    ordered, grad_sorted = call(
        sort_kernel, (shaped((rows, width), BF16), shaped((rows, width), BF16)), [VMEM] * 3
    )(positions, features, out_grad)

    projections = (query_weight, key_weight, value_weight)
    if head_groups == 2:

        def my_piece(weight, core, dim):
            size = weight.shape[dim] // 2
            return lax.dynamic_slice_in_dim(weight, core * size, size, dim)

        core, normed = lax.optimization_barrier((region % 2, normed))
        mix = my_piece(out_weight, core, 0).T
        pack = jnp.concatenate([*[my_piece(w, core, 1) for w in projections], mix], axis=1)
        core, pack = lax.optimization_barrier((core, pack))
        (pack_a,) = exchanged([pack])
        hidden_pack = jnp.concatenate([my_piece(ffn_in, core, 1), my_piece(ffn_out, core, 0)], axis=0)
        (hidden_a,) = exchanged([hidden_pack])
        pack_a, meta, ordered, grad_sorted, hidden_pack = lax.optimization_barrier(
            (pack_a, meta, ordered, grad_sorted, hidden_pack)
        )
        pack_b = lax.ppermute(pack_a, "elem", sibling)
    else:

        def pieces(weight, dim):
            size = weight.shape[dim] * head_groups // 4
            whole = lax.all_gather(weight, "head", axis=dim, tiled=True)
            return jnp.split(whole, (2 * size, 3 * size), axis=dim)

        split = [pieces(w, 1) for w in projections]
        mixing = pieces(out_weight, 0)
        projections = tuple(parts[0] for parts in split)
        pack_a, pack_b = (
            jnp.concatenate([*[parts[i] for parts in split], mixing[i].T], axis=1) for i in (1, 2)
        )
        out_weight = mixing[0]
        ffn_in, *up_parts = pieces(ffn_in, 1)
        ffn_out, *down_parts = pieces(ffn_out, 0)
        hidden_a, hidden_b = (jnp.concatenate(parts, axis=0) for parts in zip(up_parts, down_parts))

    heads_width = head_groups * share
    key_value = (*projections[1:], pack_a, pack_b)
    pairs = heads_width // PAIR
    pair_tile = (pairs, PAIR, 2 * block)
    keep = pltpu.VMEM((slots, pairs, block, 2 * block), F32)
    stats = shaped((half_count, 2 * heads_width), F32)
    keys, values, keys_t, queries, query_t, part_acc, part_peaks, part_sums = call(
        own_kernel,
        (
            shaped((rows, heads_width), BF16),
            shaped((rows, heads_width), BF16),
            shaped((block_count, heads_width, block), BF16),
            shaped((mine_rows, heads_width), BF16),
            shaped((half_count,) + pair_tile, BF16),
            shaped((half_count,) + pair_tile, F32),
            stats,
            stats,
        ),
        [SMEM] + [VMEM] * 6,
        scratch=(
            keep,
            pltpu.VMEM((block_count, heads_width, block), BF16),
        ),
        vmem=26,
    )(meta, normed, *projections, pack_a, pack_b)
    halo_keys, halo_values, attended, attended_t, log_total = call(
        halo_kernel,
        (
            shaped((2 * rows, heads_width), BF16),
            shaped((2 * rows, heads_width), BF16),
            shaped((mine_rows, heads_width), BF16),
            shaped((half_count, heads_width, block), BF16),
            stats,
        ),
        [SMEM] + [VMEM] * 10,
        scratch=(
            keep,
            pltpu.VMEM((2 * block_count, heads_width, block), BF16),
            pltpu.VMEM(pair_tile, F32),
        ),
        vmem=30,
    )(meta, low, high, *key_value, query_t, part_acc, part_peaks, part_sums)

    square = shaped((mine_rows, width), F32)
    narrow = shaped((mine_rows, width), BF16)
    if head_groups == 2:
        attended, hidden_a = lax.optimization_barrier((attended, hidden_a))
        hidden_b = lax.ppermute(hidden_a, "elem", sibling)
    hidden_in, grad_rows, norm_two, part_total, part_back = call(
        ffn_kernel,
        (square, narrow, narrow, square, square),
        [SMEM] + [VMEM] * 9,
    )(meta, ordered, grad_sorted, attended, gain_two, out_weight, pack_a, pack_b, ffn_in, ffn_out)
    others = head_groups - 1
    mixed_grad, out_own, hidden_own, *sends = call(
        rest_kernel,
        (
            narrow,
            shaped((mine_rows, share), BF16),
            shaped((mine_rows, share), F32),
            *[shaped((mine_rows, 2 * share), BF16)] * others,
        ),
        [SMEM] + [VMEM] * 11,
        scratch=(pltpu.VMEM((mine_rows, width), F32), pltpu.VMEM((mine_rows, width), F32)),
    )(
        meta,
        hidden_in,
        grad_rows,
        norm_two,
        part_total,
        part_back,
        gain_two,
        out_weight,
        pack_a,
        pack_b,
        hidden_a,
        hidden_b,
    )
    both_got = exchanged(sends)

    rows_pair = pltpu.VMEM((2, pairs, 2 * block, PAIR), BF16)
    half = rows // 2

    def side_back(side, grads, more, *extra):
        return call(
            functools.partial(side_back_kernel, side),
            (*[shaped((size, width), BF16) for size in grads], *more, shaped((half_count,) + pair_tile, F32)),
            [SMEM] + [VMEM] * (10 + len(extra)),
            scratch=(
                pltpu.VMEM((rows, heads_width), F32),
                pltpu.VMEM((rows, heads_width), F32),
                pltpu.VMEM((block_count, heads_width, block), BF16),
                rows_pair,
            ),
            vmem=24,
        )(meta, halo_keys, halo_values, queries, query_t, mixed_grad, log_total, *key_value, *extra)

    grad_low, grad_t, deltas, part_grad = side_back(
        0, (rows,), (shaped((half_count,) + pair_tile, BF16), stats), attended_t
    )
    from_right = lax.ppermute(grad_low, "elem", backward)
    grad_high_a, grad_high_b, part_grad = side_back(1, (half, half), (), grad_t, deltas, part_grad)
    from_left = [lax.ppermute(grad, "elem", forward) for grad in (grad_high_a, grad_high_b)]
    part_grad, both_got = lax.optimization_barrier((part_grad, both_got))
    grad_own = call(
        own_back_kernel,
        shaped((rows, width), F32),
        [SMEM] + [VMEM] * 15,
        scratch=(
            pltpu.VMEM((rows, heads_width), F32),
            pltpu.VMEM((rows, heads_width), F32),
            rows_pair,
            pltpu.VMEM(pair_tile, F32),
            pltpu.VMEM((mine_rows, heads_width), BF16),
        ),
        vmem=30,
    )(
        meta,
        keys,
        values,
        keys_t,
        queries,
        query_t,
        mixed_grad,
        grad_t,
        deltas,
        log_total,
        part_grad,
        *projections,
        pack_a,
        pack_b,
    )
    tail = 2 * (half // 128) * (128 // min(share, 128))
    terms, got = [], []
    for i in range(2):
        term, dots, *sends = call(
            functools.partial(term_kernel, i * half),
            (
                shaped((half, share), F32),
                shaped((half // 128, 128), F32),
                *[shaped((half + tail, share), BF16)] * others,
            ),
            [SMEM] + [VMEM] * 4,
        )(meta, grad_own, from_right, from_left[i], normed)
        terms += [term, dots]
        got += exchanged(sends)
    columns = shaped((rows, share), F32)
    output, *prepared = call(
        output_kernel,
        (shaped((rows, share), BF16), shaped((rows, rows), BF16), columns, columns, columns),
        [SMEM] + [VMEM] * (4 + head_groups),
        scratch=(pltpu.VMEM((rows, share), BF16),),
    )(meta, positions, ordered, gain_one, hidden_own, out_own, *both_got)
    input_grad = call(
        final_kernel,
        columns,
        [VMEM] * (8 + 2 * others),
        scratch=(pltpu.VMEM((rows, 2 * share), BF16),),
    )(*prepared, *terms, *got)
    return (output, input_grad)


def solution(mesh):
    in_specs = (
        P("elem", None),
        P("elem", None),
        P("elem"),
        P("elem", None),
        P("elem"),
        P(),
        P(None, "head"),
        P(None, "head"),
        P(None, "head"),
        P("head", None),
        P(),
        P(None, "head"),
        P("head", None),
    )
    out_specs = (P("elem", "head"), P("elem", "head"))
    return jax.shard_map(local, mesh=mesh, in_specs=in_specs, out_specs=out_specs, check_vma=False)
```

```python
import functools

import jax
import jax.numpy as jnp
from jax import lax
from jax.experimental import pallas as pl
from jax.experimental.pallas import tpu as pltpu
from jax.sharding import PartitionSpec as P

HD = 64
PAIR = 2 * HD
EPSILON = 1e-05
F32 = jnp.float32
BF16 = jnp.bfloat16
VMEM = pl.BlockSpec(memory_space=pltpu.VMEM)
SMEM = pl.BlockSpec(memory_space=pltpu.SMEM)
COUNT_COL = 12
BLOCK_COL = 13
GROUP_COL = 14
OWN_COL = 15
LOW_COL = 16
META_COLS = 128
COST = 1000


def dot_nn(a, b):
    return lax.dot_general(a, b, (((1,), (0,)), ((), ())), preferred_element_type=F32)


def dot_nt(a, b):
    return lax.dot_general(a, b, (((1,), (1,)), ((), ())), preferred_element_type=F32)


def row_scale(values):
    return lax.rsqrt(jnp.mean(values * values, axis=-1, keepdims=True) + EPSILON)


def call(kernel, out_shape, in_specs, scratch=(), vmem=16):
    out_specs = jax.tree.map(lambda _: VMEM, out_shape)
    return pl.pallas_call(
        kernel,
        out_shape=out_shape,
        in_specs=in_specs,
        out_specs=out_specs,
        scratch_shapes=list(scratch),
        compiler_params=pltpu.CompilerParams(vmem_limit_bytes=vmem << 20),
        cost_estimate=pl.CostEstimate(flops=COST, bytes_accessed=COST, transcendentals=0),
    )


def shaped(shape, dtype):
    return jax.ShapeDtypeStruct(shape, dtype)


def column_of(row, size):
    return jnp.broadcast_to(row, (size, size)).T


def sort_matrix(pos_ref, first, size, total):
    lanes = lax.broadcasted_iota(jnp.int32, (128, total), 1).astype(F32)
    parts = []
    for start in range(first, first + size, 128):
        column = column_of(places(pos_ref, start, 128).astype(F32), 128)
        wide = jnp.concatenate([column] * (total // 128), axis=1)
        parts.append(jnp.where(wide == lanes, 1.0, 0.0).astype(BF16))
    return jnp.concatenate(parts, axis=0)


def places(pos_ref, start, size):
    return lax.rem(pos_ref[:, start : start + size], pos_ref.shape[1])


def plan_kernel(head_groups, where_ref, lists_ref, counts_ref, meta_ref):
    blocks, slots = lists_ref.shape
    region, regions, group, heads = where_ref[0], where_ref[1], where_ref[2], head_groups
    counts = [counts_ref[i] for i in range(blocks)]
    for i in range(blocks):
        rank = jnp.int32(0)
        for j in range(blocks):
            if j != i:
                ahead = counts[j] >= counts[i] if j < i else counts[j] > counts[i]
                rank = rank + jnp.where(ahead, 1, 0)
        turn = rank // heads
        side = rank % heads
        side = jnp.where(turn % 2 == 1, heads - 1 - side, side)
        from_me = group - side
        from_me = jnp.where(from_me < 0, from_me + heads, from_me)
        row = from_me * (blocks // heads) + turn
        meta_ref[row, COUNT_COL] = counts[i]
        meta_ref[row, BLOCK_COL] = jnp.int32(i)
        meta_ref[row, GROUP_COL] = group
        entries = []
        own_total = low_total = jnp.int32(0)
        for s in range(slots):
            key = lists_ref[i, s]
            away = key // blocks - region + 1
            away = jnp.where(away < 0, away + regions, away)
            away = jnp.where(away >= regions, away - regions, away)
            entries.append((key % blocks + jnp.where(away == 2, blocks, 0), away))
            live = s < counts[i]
            own_total = own_total + jnp.where((away == 1) & live, 1, 0)
            low_total = low_total + jnp.where((away == 0) & live, 1, 0)
        meta_ref[row, OWN_COL] = own_total
        meta_ref[row, LOW_COL] = low_total
        own_next, low_next, high_next = jnp.int32(0), own_total, own_total + low_total
        for s in range(slots):
            index, away = entries[s]
            to = jnp.where(away == 1, own_next, jnp.where(away == 0, low_next, high_next))

            @pl.when(s < counts[i])
            def _(index=index, to=to):
                meta_ref[row, to] = index

            own_next = own_next + jnp.where(away == 1, 1, 0)
            low_next = low_next + jnp.where(away == 0, 1, 0)
            high_next = high_next + jnp.where(away == 2, 1, 0)


def prep_kernel(pos_ref, rows_ref, gain_ref, normed_ref):
    total = rows_ref.shape[0]
    for first in range(0, total, 512):
        picked = dot_nn(sort_matrix(pos_ref, first, 512, total), rows_ref[...])
        normed_ref[first : first + 512, :] = (picked * row_scale(picked) * gain_ref[...]).astype(BF16)


def sort_kernel(pos_ref, rows_ref, grads_ref, sorted_rows_ref, sorted_grads_ref):
    total = rows_ref.shape[0]
    for first in range(0, total, 512):
        matrix = sort_matrix(pos_ref, first, 512, total)
        sorted_rows_ref[first : first + 512, :] = dot_nn(matrix, rows_ref[...]).astype(BF16)
        sorted_grads_ref[first : first + 512, :] = dot_nn(matrix, grads_ref[...]).astype(BF16)


def chunk(values, who, share):
    out = values[:, :share]
    for start in range(share, values.shape[1], share):
        out = jnp.where(who == start // share, values[:, start : start + share], out)
    return out


def below(group, steps, count):
    who = group + steps
    return jnp.where(who >= count, who - count, who)


def both_heads(rows):
    lane = lax.broadcasted_iota(jnp.int32, rows.shape, 1)
    zero = jnp.zeros_like(rows)
    return jnp.concatenate([jnp.where(lane < HD, rows, zero), jnp.where(lane < HD, zero, rows)], axis=0)


def both_heads_t(rows):
    flipped = rows.T
    row = lax.broadcasted_iota(jnp.int32, flipped.shape, 0)
    zero = jnp.zeros_like(flipped)
    return jnp.concatenate([jnp.where(row < HD, flipped, zero), jnp.where(row < HD, zero, flipped)], axis=1)


def own_heads(wide):
    half = wide.shape[1] // 2
    return jnp.concatenate([wide[:HD, :half], wide[HD:, half:]], axis=0)


def groups_of_eight(tile, op):
    out = tile[:8]
    for start in range(8, tile.shape[0], 8):
        out = op(out, tile[start : start + 8])
    return out


def packed(packs, which):
    size = packs[0].shape[1] // 4
    return jnp.concatenate([ref[:, which * size : (which + 1) * size] for ref in packs], axis=1)


def joined(mine_ref, packs, which):
    return jnp.concatenate([mine_ref[...], packed(packs, which)], axis=1)


def project_keys(rows_ref, wk, wv, keys_ref, values_ref, values_t_ref, base):
    for start in range(0, rows_ref.shape[0], 512):
        at = slice(base + start, base + start + 512)
        here = rows_ref[start : start + 512, :]
        keys_ref[at, :] = dot_nn(here, wk).astype(BF16)
        found = dot_nn(here, wv).astype(BF16)
        values_ref[at, :] = found
        for part in range(4):
            values_t_ref[(base + start) // 128 + part] = found[part * 128 : part * 128 + 128, :].T


def block_rows(ref, indices, cols):
    return jnp.concatenate(
        [ref[pl.ds(pl.multiple_of(index * 128, 128), 128), cols] for index in indices], axis=0
    )


def block_cols(ref, indices, cols):
    return jnp.concatenate([ref[index, cols, :] for index in indices], axis=1)


def by_two(count, step, carried):
    carried = lax.fori_loop(0, count // 2, lambda i, c: step(2 * i, 2, c), carried)
    return lax.fori_loop(0, count % 2, lambda i, c: step(count - 1, 1, c), carried)


def attend(meta_ref, b, first, count, keys_ref, values_t_ref, query_t_ref, keep_ref, acc_ref, old):
    pairs = query_t_ref.shape[0]
    wide = query_t_ref.shape[2]

    def peak_step(slot, size, peaks):
        indices = [meta_ref[b, first + slot + j] for j in range(size)]
        tiles = [
            dot_nn(block_rows(keys_ref, indices, slice(p * PAIR, (p + 1) * PAIR)), query_t_ref[p])
            for p in range(pairs)
        ]
        out = []
        for p in range(pairs):
            for j in range(size):
                keep_ref[slot + j, p] = tiles[p][j * 128 : (j + 1) * 128]
            out.append(jnp.maximum(peaks[p], groups_of_eight(tiles[p], jnp.maximum)))
        return tuple(out)

    if old is None:
        start = (jnp.full((8, wide), -3.0e38, F32),) * pairs
    else:
        start = tuple(jnp.broadcast_to(peak, (8, wide)) for peak, _ in old)
    peaks = by_two(count, peak_step, start)
    peaks = tuple(jnp.max(peak, axis=0, keepdims=True) for peak in peaks)
    totals = []
    for p in range(pairs):
        if old is None:
            acc_ref[p] = jnp.zeros(acc_ref.shape[1:], F32)
            totals.append(jnp.zeros((1, wide), F32))
        else:
            shrink = jnp.exp(old[p][0] - peaks[p])
            acc_ref[p] = acc_ref[p] * shrink
            totals.append(old[p][1] * shrink)

    def sum_step(slot, size, sums):
        indices = [meta_ref[b, first + slot + j] for j in range(size)]
        out = []
        for p in range(pairs):
            cols = slice(p * PAIR, (p + 1) * PAIR)
            tile = jnp.concatenate([jnp.exp(keep_ref[slot + j, p] - peaks[p]) for j in range(size)], axis=0)
            out.append(sums[p] + groups_of_eight(tile, jnp.add))
            acc_ref[p] += dot_nn(block_cols(values_t_ref, indices, cols), tile.astype(BF16))
        return tuple(out)

    sums = by_two(count, sum_step, (jnp.zeros((8, wide), F32),) * pairs)
    return [
        (peaks[p], totals[p] + jnp.sum(sums[p], axis=0, keepdims=True)) for p in range(pairs)
    ]


def own_kernel(
    meta_ref,
    own_ref,
    wq_ref,
    wk_ref,
    wv_ref,
    pack_a,
    pack_b,
    keys_ref,
    values_ref,
    keys_t_ref,
    queries_ref,
    query_t_ref,
    acc_ref,
    peaks_ref,
    sums_ref,
    keep_ref,
    values_t_ref,
):
    block = 128
    pairs = queries_ref.shape[1] // PAIR
    packs = (pack_a, pack_b)
    project_keys(own_ref, joined(wk_ref, packs, 1), joined(wv_ref, packs, 2), keys_ref, values_ref, values_t_ref, 0)
    wq = joined(wq_ref, packs, 0)
    for kb in range(keys_t_ref.shape[0]):
        keys_t_ref[kb] = keys_ref[kb * block : (kb + 1) * block, :].T

    @pl.loop(0, queries_ref.shape[0] // block)
    def _(b):
        first = pl.multiple_of(meta_ref[b, BLOCK_COL] * block, block)
        query = dot_nn(own_ref[pl.ds(first, block), :], wq).astype(BF16)
        query = (query.astype(F32) * (HD ** (-0.5))).astype(BF16)
        queries_ref[pl.ds(pl.multiple_of(b * block, block), block), :] = query
        for p in range(pairs):
            query_t_ref[b, p] = both_heads_t(query[:, p * PAIR : (p + 1) * PAIR])
        found = attend(
            meta_ref,
            b,
            0,
            meta_ref[b, OWN_COL],
            keys_ref,
            values_t_ref,
            query_t_ref.at[b],
            keep_ref,
            acc_ref.at[b],
            None,
        )
        for p in range(pairs):
            at = slice(p * 2 * block, (p + 1) * 2 * block)
            peaks_ref[pl.ds(b, 1), at] = found[p][0]
            sums_ref[pl.ds(b, 1), at] = found[p][1]


def halo_kernel(
    meta_ref,
    low_ref,
    high_ref,
    wk_ref,
    wv_ref,
    pack_a,
    pack_b,
    query_t_ref,
    old_acc_ref,
    peaks_ref,
    sums_ref,
    keys_ref,
    values_ref,
    attended_ref,
    attended_t_ref,
    log_total_ref,
    keep_ref,
    values_t_ref,
    acc_ref,
):
    block = 128
    pairs = query_t_ref.shape[1]
    wk = joined(wk_ref, (pack_a, pack_b), 1)
    wv = joined(wv_ref, (pack_a, pack_b), 2)
    project_keys(low_ref, wk, wv, keys_ref, values_ref, values_t_ref, 0)
    project_keys(high_ref, wk, wv, keys_ref, values_ref, values_t_ref, low_ref.shape[0])

    @pl.loop(0, query_t_ref.shape[0])
    def _(b):
        here = pl.ds(pl.multiple_of(b * block, block), block)
        old = []
        for p in range(pairs):
            at = slice(p * 2 * block, (p + 1) * 2 * block)
            acc_ref[p] = old_acc_ref[b, p]
            old.append((peaks_ref[pl.ds(b, 1), at], sums_ref[pl.ds(b, 1), at]))
        own = meta_ref[b, OWN_COL]
        found = attend(
            meta_ref,
            b,
            own,
            meta_ref[b, COUNT_COL] - own,
            keys_ref,
            values_t_ref,
            query_t_ref.at[b],
            keep_ref,
            acc_ref,
            old,
        )
        for p in range(pairs):
            peak, total = found[p]
            log_total_ref[pl.ds(b, 1), p * 2 * block : (p + 1) * 2 * block] = peak + jnp.log(total)
            rows = own_heads(acc_ref[p] * (1.0 / total)).astype(BF16)
            attended_t_ref[b, p * PAIR : (p + 1) * PAIR, :] = rows
            attended_ref[here, p * PAIR : (p + 1) * PAIR] = rows.T


GELU_A = 0.044715
GELU_B = 0.7978845608028654


def ffn_chunks(norm_ref, grad_ref, chunks):
    def products(at):
        up, down = chunks[at]
        return dot_nn(norm_ref[...], up), dot_nt(grad_ref[...], down)

    totals = None
    coming = products(0)
    for at, (up, down) in enumerate(chunks):
        pre, grad_act = coming
        if at + 1 < len(chunks):
            coming = products(at + 1)
        square = pre * pre
        inner = jnp.tanh(pre * (GELU_B + (GELU_A * GELU_B) * square))
        gate = 0.5 + 0.5 * inner
        active = (pre * gate).astype(BF16)
        slope = gate + pre * (1.0 - inner * inner) * (0.5 * GELU_B + (1.5 * GELU_A * GELU_B) * square)
        grad_pre = (grad_act * slope).astype(BF16)
        found = dot_nn(active, down), dot_nt(grad_pre, up)
        totals = found if totals is None else (totals[0] + found[0], totals[1] + found[1])
    return totals


def ffn_kernel(
    meta_ref,
    ordered_ref,
    grad_ref,
    attended_ref,
    gain_ref,
    wo_ref,
    pack_a,
    pack_b,
    in_ref,
    out_ref,
    hidden_ref,
    grad_rows,
    norm_ref,
    total_ref,
    back_ref,
):
    block = 128
    size = attended_ref.shape[0]
    for b in range(size // block):
        first = pl.multiple_of(meta_ref[b, BLOCK_COL] * block, block)
        hidden_ref[b * block : (b + 1) * block, :] = ordered_ref[pl.ds(first, block), :].astype(F32)
        grad_rows[b * block : (b + 1) * block, :] = grad_ref[pl.ds(first, block), :]
    share = wo_ref.shape[0]
    hidden_in = hidden_ref[...] + dot_nn(attended_ref[:, :share], wo_ref[...])
    hidden_in = hidden_in + dot_nt(attended_ref[:, share:], packed((pack_a, pack_b), 3))
    hidden_ref[...] = hidden_in
    norm_ref[...] = (hidden_in * row_scale(hidden_in) * gain_ref[...]).astype(BF16)
    cuts = [slice(start, start + 512) for start in range(0, in_ref.shape[1], 512)]
    total_ref[...], back_ref[...] = ffn_chunks(
        norm_ref, grad_rows, [(in_ref[:, at], out_ref[at, :]) for at in cuts]
    )


def rest_kernel(
    meta_ref,
    hidden_ref,
    grad_rows,
    norm_ref,
    old_total_ref,
    old_back_ref,
    gain_ref,
    wo_ref,
    pack_a,
    pack_b,
    hidden_a,
    hidden_b,
    mixed_grad_ref,
    out_own_ref,
    hidden_own_ref,
    *refs,
):
    heads = len(refs) + 1
    width = norm_ref.shape[1]
    forward, backward = ffn_chunks(
        norm_ref, grad_rows, [(ref[:width, :], ref[width:, :]) for ref in (hidden_a, hidden_b)]
    )
    hidden_in = hidden_ref[...]
    result = (hidden_in + (old_total_ref[...] + forward)).astype(BF16)
    group = meta_ref[0, GROUP_COL]
    share = out_own_ref.shape[1]
    out_own_ref[...] = chunk(result, group, share)
    scale = row_scale(hidden_in)
    second_norm = hidden_in * scale
    scaled = (old_back_ref[...] + backward) * gain_ref[...]
    hidden_grad = grad_rows[...].astype(F32) + scale * (
        scaled - second_norm * jnp.mean(scaled * second_norm, axis=-1, keepdims=True)
    )
    hidden_own_ref[...] = chunk(hidden_grad, group, share)
    for k in range(1, heads):
        who = below(group, k, heads)
        refs[k - 1][:, :share] = chunk(result, who, share)
        refs[k - 1][:, share:] = chunk(hidden_grad, who, share).astype(BF16)
    narrow = hidden_grad.astype(BF16)
    half = wo_ref.shape[0]
    mixed_grad_ref[:, :half] = dot_nt(narrow, wo_ref[...]).astype(BF16)
    mixed_grad_ref[:, half:] = dot_nn(narrow, packed((pack_a, pack_b), 3)).astype(BF16)


def back_operands(queries_ref, mixed_grad_ref, attended_t_ref, grad_t_ref, deltas_ref):
    block = 128
    pairs = queries_ref.shape[1] // PAIR

    @pl.loop(0, queries_ref.shape[0] // block)
    def _(b):
        here = pl.ds(pl.multiple_of(b * block, block), block)
        for p in range(pairs):
            cols = slice(p * PAIR, (p + 1) * PAIR)
            grad_t = both_heads_t(mixed_grad_ref[here, cols])
            grad_t_ref[b, p] = grad_t
            attended = attended_t_ref[b, cols, :].astype(F32)
            product = grad_t.astype(F32) * jnp.concatenate([attended, attended], axis=1)
            deltas_ref[pl.ds(b, 1), p * 2 * block : (p + 1) * 2 * block] = jnp.sum(product, axis=0, keepdims=True)


def scores_back(
    meta_ref,
    b,
    first,
    count,
    base,
    keys_ref,
    values_ref,
    keys_t_ref,
    operands,
    grad_keys,
    grad_values,
    rows_ref,
    acc_ref,
):
    queries_ref, query_t_ref, mixed_grad_ref, grad_t_ref, deltas_ref, log_total_ref = operands
    block = 128
    pairs = queries_ref.shape[1] // PAIR
    here = pl.ds(pl.multiple_of(b * block, block), block)
    deltas = []
    logs = []
    for p in range(pairs):
        cols = slice(p * PAIR, (p + 1) * PAIR)
        wide = slice(p * 2 * block, (p + 1) * 2 * block)
        rows_ref[0, p] = both_heads(queries_ref[here, cols])
        rows_ref[1, p] = both_heads(mixed_grad_ref[here, cols])
        deltas.append(deltas_ref[pl.ds(b, 1), wide])
        logs.append(log_total_ref[pl.ds(b, 1), wide])

    def step(slot, size, carried):
        indices = [meta_ref[b, first + slot + j] for j in range(size)]
        here = [index - base for index in indices]
        cuts = [slice(p * PAIR, (p + 1) * PAIR) for p in range(pairs)]

        def products(p):
            scores = dot_nn(block_rows(keys_ref, indices, cuts[p]), query_t_ref[b, p])
            return scores, dot_nn(block_rows(values_ref, indices, cuts[p]), grad_t_ref[b, p])

        coming = products(0)
        for p, cols in enumerate(cuts):
            scores, prob_grad = coming
            if p + 1 < pairs:
                coming = products(p + 1)
            probs = jnp.exp(scores - logs[p])
            score_grad = (probs * (prob_grad - deltas[p])).astype(BF16)
            to_values = dot_nn(probs.astype(BF16), rows_ref[1, p])
            to_keys = dot_nn(score_grad, rows_ref[0, p])
            acc_ref[p] += dot_nn(block_cols(keys_t_ref, here, cols), score_grad)
            for j in range(size):
                at = pl.ds(pl.multiple_of(here[j] * block, block), block)
                grad_values[at, cols] += to_values[j * block : (j + 1) * block]
                grad_keys[at, cols] += to_keys[j * block : (j + 1) * block]
        return carried

    by_two(count, step, 0)


def clear_back(grad_keys, grad_values):
    @pl.loop(0, grad_keys.shape[0] // 128)
    def _(kb):
        at = pl.ds(pl.multiple_of(kb * 128, 128), 128)
        grad_keys[at, :] = jnp.zeros((128, grad_keys.shape[1]), F32)
        grad_values[at, :] = jnp.zeros((128, grad_keys.shape[1]), F32)


def project_back(grad_keys, grad_values, wk, wv, start, size):
    at = slice(start, start + size)
    keys_part = dot_nt(grad_keys[at, :].astype(BF16), wk)
    return keys_part + dot_nt(grad_values[at, :].astype(BF16), wv)


def side_back_kernel(
    side,
    meta_ref,
    keys_ref,
    values_ref,
    queries_ref,
    query_t_ref,
    mixed_grad_ref,
    log_total_ref,
    wk_ref,
    wv_ref,
    pack_a,
    pack_b,
    *refs,
):
    acc_ref, grad_keys, grad_values, keys_t_ref, rows_ref = refs[-5:]
    if side == 0:
        attended_t_ref, *grads, grad_t_ref, deltas_ref = refs[:-5]
        back_operands(queries_ref, mixed_grad_ref, attended_t_ref, grad_t_ref, deltas_ref)
    else:
        grad_t_ref, deltas_ref, old_acc_ref, *grads = refs[:-5]
    operands = queries_ref, query_t_ref, mixed_grad_ref, grad_t_ref, deltas_ref, log_total_ref
    base = side * keys_t_ref.shape[0]
    clear_back(grad_keys, grad_values)

    @pl.loop(0, keys_t_ref.shape[0])
    def _(kb):
        keys_t_ref[kb] = keys_ref[pl.ds(pl.multiple_of((kb + base) * 128, 128), 128), :].T

    @pl.loop(0, queries_ref.shape[0] // 128)
    def _(b):
        own, low = meta_ref[b, OWN_COL], meta_ref[b, LOW_COL]
        acc_ref[b] = jnp.zeros(acc_ref.shape[1:], F32) if side == 0 else old_acc_ref[b]
        scores_back(
            meta_ref,
            b,
            own if side == 0 else own + low,
            low if side == 0 else meta_ref[b, COUNT_COL] - own - low,
            base,
            keys_ref,
            values_ref,
            keys_t_ref,
            operands,
            grad_keys,
            grad_values,
            rows_ref,
            acc_ref.at[b],
        )

    packs = (pack_a, pack_b)
    weights = joined(wk_ref, packs, 1), joined(wv_ref, packs, 2)
    start = 0
    for ref in grads:
        for part in range(0, ref.shape[0], 512):
            ref[part : part + 512, :] = project_back(
                grad_keys, grad_values, *weights, start + part, 512
            ).astype(BF16)
        start += ref.shape[0]


def own_back_kernel(
    meta_ref,
    keys_ref,
    values_ref,
    keys_t_ref,
    queries_ref,
    query_t_ref,
    mixed_grad_ref,
    grad_t_ref,
    deltas_ref,
    log_total_ref,
    old_acc_ref,
    wq_ref,
    wk_ref,
    wv_ref,
    pack_a,
    pack_b,
    own_ref,
    grad_keys,
    grad_values,
    rows_ref,
    acc_ref,
    query_grad,
):
    operands = queries_ref, query_t_ref, mixed_grad_ref, grad_t_ref, deltas_ref, log_total_ref
    block = 128
    rows = own_ref.shape[0]
    pairs = queries_ref.shape[1] // PAIR
    blocks = queries_ref.shape[0] // block
    clear_back(grad_keys, grad_values)

    @pl.loop(0, blocks)
    def _(b):
        acc_ref[...] = old_acc_ref[b]
        scores_back(
            meta_ref,
            b,
            0,
            meta_ref[b, OWN_COL],
            0,
            keys_ref,
            values_ref,
            keys_t_ref,
            operands,
            grad_keys,
            grad_values,
            rows_ref,
            acc_ref,
        )
        for p in range(pairs):
            found = own_heads(acc_ref[p]) * (HD ** (-0.5))
            query_grad[pl.ds(pl.multiple_of(b * block, block), block), p * PAIR : (p + 1) * PAIR] = found.T.astype(BF16)

    packs = (pack_a, pack_b)
    weights = joined(wk_ref, packs, 1), joined(wv_ref, packs, 2)
    for start in range(0, rows, 512):
        own_ref[start : start + 512, :] = project_back(grad_keys, grad_values, *weights, start, 512)
    parts = dot_nt(query_grad[...], joined(wq_ref, packs, 0))
    for b in range(blocks):
        first = pl.multiple_of(meta_ref[b, BLOCK_COL] * block, block)
        own_ref[pl.ds(first, block), :] += parts[b * block : (b + 1) * block]


def term_kernel(offset, meta_ref, own_ref, low_ref, high_ref, normed_ref, term_ref, dots_ref, *send_refs):
    rows, share = term_ref.shape
    heads = len(send_refs) + 1
    group = meta_ref[0, GROUP_COL]
    dot_rows = []
    for start in range(0, rows, 128):
        at = slice(start, start + 128)
        whole = slice(offset + start, offset + start + 128)
        term = own_ref[whole, :] + low_ref[whole, :].astype(F32) + high_ref[at, :].astype(F32)
        dots = jnp.sum(term * normed_ref[whole, :].astype(F32), axis=-1, keepdims=True)
        dot_rows.append(jnp.broadcast_to(dots, (128, 128)).T[:1])
        term_ref[at, :] = chunk(term, group, share)
        for k in range(1, heads):
            send_refs[k - 1][at, :] = chunk(term, below(group, k, heads), share).astype(BF16)
    dots = jnp.concatenate(dot_rows, axis=0)
    dots_ref[...] = dots
    high = dots.astype(BF16)
    low = (dots - high.astype(F32)).astype(BF16)
    wide = min(share, 128)
    tail = jnp.concatenate(
        [half[:, start : start + wide] for half in (high, low) for start in range(0, 128, wide)], axis=0
    )
    if share > wide:
        tail = jnp.concatenate([tail] * (share // wide), axis=1)
    for ref in send_refs:
        ref[rows:, :] = tail


def dots_of(tail):
    wide = min(tail.shape[1], 128)
    count = 128 // wide
    size = tail.shape[0] // (2 * count)
    parts = [tail[i * size : (i + 1) * size, :wide].astype(F32) for i in range(2 * count)]
    sums = [parts[i] + parts[count + i] for i in range(count)]
    return sums[0] if count == 1 else jnp.concatenate(sums, axis=1)


def back_matrix(pos_ref, first, size, total):
    place = lax.broadcasted_iota(jnp.int32, (size, total), 0) + first
    return jnp.where(jnp.broadcast_to(places(pos_ref, 0, total), (size, total)) == place, 1.0, 0.0).astype(BF16)


def place_blocks(meta_ref, refs, all_ref, first_col):
    block = 128
    share = all_ref.shape[1]
    blocks = refs[0].shape[0] // block
    for k, ref in enumerate(refs):
        cols = slice(0, share) if k == 0 else slice(first_col, first_col + share)
        for b in range(blocks):
            first = pl.multiple_of(meta_ref[k * blocks + b, BLOCK_COL] * block, block)
            all_ref[pl.ds(first, block), :] = ref[b * block : (b + 1) * block, cols].astype(all_ref.dtype)


def output_kernel(meta_ref, pos_ref, ordered_ref, gain_ref, hidden_own_ref, *refs):
    out_ref, matrix_ref, base_ref, scale_ref, norm_ref, all_ref = refs[-6:]
    own_ref, *got_refs = refs[:-6]
    place_blocks(meta_ref, [own_ref, *got_refs], all_ref, 0)
    total, share = all_ref.shape
    place_blocks(meta_ref, [hidden_own_ref, *got_refs], base_ref, share)
    for first in range(0, total, 512):
        matrix = back_matrix(pos_ref, first, 512, total)
        matrix_ref[first : first + 512, :] = matrix
        out_ref[first : first + 512, :] = dot_nn(matrix, all_ref[...]).astype(BF16)
    group = meta_ref[0, GROUP_COL]
    gain = chunk(gain_ref[...], group, share)
    for start in range(0, total, 128):
        at = slice(start, start + 128)
        ordered = ordered_ref[at, :].astype(F32)
        scale = row_scale(ordered)
        scale_ref[at, :] = scale * gain
        norm_ref[at, :] = chunk(ordered, group, share) * (scale * scale)


def final_kernel(matrix_ref, base_ref, scale_ref, norm_ref, term_a, dots_a, term_b, dots_b, *refs):
    out_ref, split_ref = refs[-2:]
    total, share = out_ref.shape
    half = total // 2
    others = (len(refs) - 2) // 2
    for i, (term_ref, dots_ref) in enumerate(((term_a, dots_a), (term_b, dots_b))):
        got_refs = refs[i * others : (i + 1) * others]
        dots = dots_ref[...]
        for ref in got_refs:
            dots = dots + dots_of(ref[half:, :])
        dots = dots * (1.0 / (share * (others + 1)))
        for start in range(0, half, 128):
            at = slice(start, start + 128)
            whole = slice(i * half + start, i * half + start + 128)
            mean = column_of(dots[start // 128 : start // 128 + 1], 128)[:, :1]
            term = term_ref[at, :]
            for ref in got_refs:
                term = term + ref[at, :].astype(F32)
            value = base_ref[whole, :] + (term * scale_ref[whole, :] - norm_ref[whole, :] * mean)
            high = value.astype(BF16)
            split_ref[whole, :share] = high
            split_ref[whole, share:] = (value - high.astype(F32)).astype(BF16)
    for first in range(0, total, 512):
        found = dot_nn(matrix_ref[first : first + 512, :], split_ref[...])
        out_ref[first : first + 512, :] = found[:, :share] + found[:, share:]


def local(
    features,
    out_grad,
    bin_order,
    key_lists,
    list_counts,
    attn_gain,
    query_weight,
    key_weight,
    value_weight,
    out_weight,
    ffn_gain,
    ffn_in,
    ffn_out,
):
    rows, width = features.shape
    block_count, slots = key_lists.shape
    block = rows // block_count
    share = query_weight.shape[1]
    hidden = ffn_in.shape[1]
    region = lax.axis_index("elem")
    regions = lax.axis_size("elem")
    group = lax.axis_index("head")
    head_groups = lax.axis_size("head")
    half_count = block_count // head_groups
    mine_rows = rows // head_groups
    forward = [(i, (i + 1) % regions) for i in range(regions)]
    backward = [(target, source) for source, target in forward]
    sibling = [(i, i ^ 1) for i in range(regions)]

    def exchanged(pieces):
        return [
            lax.ppermute(piece, "head", [(i, (i + k) % head_groups) for i in range(head_groups)])
            for k, piece in enumerate(pieces, 1)
        ]

    positions = bin_order.reshape(1, rows)
    gain_one = attn_gain.reshape(1, width)
    gain_two = ffn_gain.reshape(1, width)

    normed = call(prep_kernel, shaped((rows, width), BF16), [VMEM] * 3, vmem=60)(positions, features, gain_one)
    low = lax.ppermute(normed, "elem", forward)
    high = lax.ppermute(normed, "elem", backward)
    meta = pl.pallas_call(
        functools.partial(plan_kernel, head_groups),
        out_shape=shaped((block_count, META_COLS), jnp.int32),
        in_specs=[SMEM] * 3,
        out_specs=SMEM,
    )(jnp.stack([region, jnp.int32(regions), group, group]), key_lists, list_counts)

    ordered, grad_sorted = call(
        sort_kernel, (shaped((rows, width), BF16), shaped((rows, width), BF16)), [VMEM] * 3
    )(positions, features, out_grad)

    projections = (query_weight, key_weight, value_weight)
    if head_groups == 2:

        def my_piece(weight, core, dim):
            size = weight.shape[dim] // 2
            return lax.dynamic_slice_in_dim(weight, core * size, size, dim)

        core, normed = lax.optimization_barrier((region % 2, normed))
        mix = my_piece(out_weight, core, 0).T
        pack = jnp.concatenate([*[my_piece(w, core, 1) for w in projections], mix], axis=1)
        core, pack = lax.optimization_barrier((core, pack))
        (pack_a,) = exchanged([pack])
        hidden_pack = jnp.concatenate([my_piece(ffn_in, core, 1), my_piece(ffn_out, core, 0)], axis=0)
        (hidden_a,) = exchanged([hidden_pack])
        pack_a, meta, ordered, grad_sorted, hidden_pack = lax.optimization_barrier(
            (pack_a, meta, ordered, grad_sorted, hidden_pack)
        )
        pack_b = lax.ppermute(pack_a, "elem", sibling)
    else:

        def pieces(weight, dim):
            size = weight.shape[dim] * head_groups // 4
            whole = lax.all_gather(weight, "head", axis=dim, tiled=True)
            return jnp.split(whole, (2 * size, 3 * size), axis=dim)

        split = [pieces(w, 1) for w in projections]
        mixing = pieces(out_weight, 0)
        projections = tuple(parts[0] for parts in split)
        pack_a, pack_b = (
            jnp.concatenate([*[parts[i] for parts in split], mixing[i].T], axis=1) for i in (1, 2)
        )
        out_weight = mixing[0]
        ffn_in, *up_parts = pieces(ffn_in, 1)
        ffn_out, *down_parts = pieces(ffn_out, 0)
        hidden_a, hidden_b = (jnp.concatenate(parts, axis=0) for parts in zip(up_parts, down_parts))

    heads_width = head_groups * share
    key_value = (*projections[1:], pack_a, pack_b)
    pairs = heads_width // PAIR
    pair_tile = (pairs, PAIR, 2 * block)
    keep = pltpu.VMEM((slots, pairs, block, 2 * block), F32)
    stats = shaped((half_count, 2 * heads_width), F32)
    keys, values, keys_t, queries, query_t, part_acc, part_peaks, part_sums = call(
        own_kernel,
        (
            shaped((rows, heads_width), BF16),
            shaped((rows, heads_width), BF16),
            shaped((block_count, heads_width, block), BF16),
            shaped((mine_rows, heads_width), BF16),
            shaped((half_count,) + pair_tile, BF16),
            shaped((half_count,) + pair_tile, F32),
            stats,
            stats,
        ),
        [SMEM] + [VMEM] * 6,
        scratch=(
            keep,
            pltpu.VMEM((block_count, heads_width, block), BF16),
        ),
        vmem=26,
    )(meta, normed, *projections, pack_a, pack_b)
    halo_keys, halo_values, attended, attended_t, log_total = call(
        halo_kernel,
        (
            shaped((2 * rows, heads_width), BF16),
            shaped((2 * rows, heads_width), BF16),
            shaped((mine_rows, heads_width), BF16),
            shaped((half_count, heads_width, block), BF16),
            stats,
        ),
        [SMEM] + [VMEM] * 10,
        scratch=(
            keep,
            pltpu.VMEM((2 * block_count, heads_width, block), BF16),
            pltpu.VMEM(pair_tile, F32),
        ),
        vmem=30,
    )(meta, low, high, *key_value, query_t, part_acc, part_peaks, part_sums)

    square = shaped((mine_rows, width), F32)
    narrow = shaped((mine_rows, width), BF16)
    if head_groups == 2:
        attended, hidden_a = lax.optimization_barrier((attended, hidden_a))
        hidden_b = lax.ppermute(hidden_a, "elem", sibling)
    hidden_in, grad_rows, norm_two, part_total, part_back = call(
        ffn_kernel,
        (square, narrow, narrow, square, square),
        [SMEM] + [VMEM] * 9,
    )(meta, ordered, grad_sorted, attended, gain_two, out_weight, pack_a, pack_b, ffn_in, ffn_out)
    others = head_groups - 1
    mixed_grad, out_own, hidden_own, *sends = call(
        rest_kernel,
        (
            narrow,
            shaped((mine_rows, share), BF16),
            shaped((mine_rows, share), F32),
            *[shaped((mine_rows, 2 * share), BF16)] * others,
        ),
        [SMEM] + [VMEM] * 11,
    )(
        meta,
        hidden_in,
        grad_rows,
        norm_two,
        part_total,
        part_back,
        gain_two,
        out_weight,
        pack_a,
        pack_b,
        hidden_a,
        hidden_b,
    )
    both_got = exchanged(sends)

    rows_pair = pltpu.VMEM((2, pairs, 2 * block, PAIR), BF16)
    half = rows // 2

    def side_back(side, grads, more, *extra):
        return call(
            functools.partial(side_back_kernel, side),
            (*[shaped((size, width), BF16) for size in grads], *more, shaped((half_count,) + pair_tile, F32)),
            [SMEM] + [VMEM] * (10 + len(extra)),
            scratch=(
                pltpu.VMEM((rows, heads_width), F32),
                pltpu.VMEM((rows, heads_width), F32),
                pltpu.VMEM((block_count, heads_width, block), BF16),
                rows_pair,
            ),
            vmem=24,
        )(meta, halo_keys, halo_values, queries, query_t, mixed_grad, log_total, *key_value, *extra)

    grad_low, grad_t, deltas, part_grad = side_back(
        0, (rows,), (shaped((half_count,) + pair_tile, BF16), stats), attended_t
    )
    from_right = lax.ppermute(grad_low, "elem", backward)
    grad_high_a, grad_high_b, part_grad = side_back(1, (half, half), (), grad_t, deltas, part_grad)
    from_left = [lax.ppermute(grad, "elem", forward) for grad in (grad_high_a, grad_high_b)]
    part_grad, both_got = lax.optimization_barrier((part_grad, both_got))
    grad_own = call(
        own_back_kernel,
        shaped((rows, width), F32),
        [SMEM] + [VMEM] * 15,
        scratch=(
            pltpu.VMEM((rows, heads_width), F32),
            pltpu.VMEM((rows, heads_width), F32),
            rows_pair,
            pltpu.VMEM(pair_tile, F32),
            pltpu.VMEM((mine_rows, heads_width), BF16),
        ),
        vmem=30,
    )(
        meta,
        keys,
        values,
        keys_t,
        queries,
        query_t,
        mixed_grad,
        grad_t,
        deltas,
        log_total,
        part_grad,
        *projections,
        pack_a,
        pack_b,
    )
    tail = 2 * (half // 128) * (128 // min(share, 128))
    terms, got = [], []
    for i in range(2):
        term, dots, *sends = call(
            functools.partial(term_kernel, i * half),
            (
                shaped((half, share), F32),
                shaped((half // 128, 128), F32),
                *[shaped((half + tail, share), BF16)] * others,
            ),
            [SMEM] + [VMEM] * 4,
        )(meta, grad_own, from_right, from_left[i], normed)
        terms += [term, dots]
        got += exchanged(sends)
    columns = shaped((rows, share), F32)
    output, *prepared = call(
        output_kernel,
        (shaped((rows, share), BF16), shaped((rows, rows), BF16), columns, columns, columns),
        [SMEM] + [VMEM] * (4 + head_groups),
        scratch=(pltpu.VMEM((rows, share), BF16),),
    )(meta, positions, ordered, gain_one, hidden_own, out_own, *both_got)
    input_grad = call(
        final_kernel,
        columns,
        [VMEM] * (8 + 2 * others),
        scratch=(pltpu.VMEM((rows, 2 * share), BF16),),
    )(*prepared, *terms, *got)
    return (output, input_grad)


def solution(mesh):
    in_specs = (
        P("elem", None),
        P("elem", None),
        P("elem"),
        P("elem", None),
        P("elem"),
        P(),
        P(None, "head"),
        P(None, "head"),
        P(None, "head"),
        P("head", None),
        P(),
        P(None, "head"),
        P("head", None),
    )
    out_specs = (P("elem", "head"), P("elem", "head"))
    return jax.shard_map(local, mesh=mesh, in_specs=in_specs, out_specs=out_specs, check_vma=False)
```

```python
import functools

import jax
import jax.numpy as jnp
from jax import lax
from jax.experimental import pallas as pl
from jax.experimental.pallas import tpu as pltpu
from jax.sharding import PartitionSpec as P

HD = 64
PAIR = 2 * HD
EPSILON = 1e-05
F32 = jnp.float32
BF16 = jnp.bfloat16
VMEM = pl.BlockSpec(memory_space=pltpu.VMEM)
SMEM = pl.BlockSpec(memory_space=pltpu.SMEM)
COUNT_COL = 12
BLOCK_COL = 13
GROUP_COL = 14
OWN_COL = 15
LOW_COL = 16
META_COLS = 128
COST = 1000


def dot_nn(a, b):
    return lax.dot_general(a, b, (((1,), (0,)), ((), ())), preferred_element_type=F32)


def dot_nt(a, b):
    return lax.dot_general(a, b, (((1,), (1,)), ((), ())), preferred_element_type=F32)


def row_scale(values):
    return lax.rsqrt(jnp.mean(values * values, axis=-1, keepdims=True) + EPSILON)


def call(kernel, out_shape, in_specs, scratch=(), vmem=16):
    out_specs = jax.tree.map(lambda _: VMEM, out_shape)
    return pl.pallas_call(
        kernel,
        out_shape=out_shape,
        in_specs=in_specs,
        out_specs=out_specs,
        scratch_shapes=list(scratch),
        compiler_params=pltpu.CompilerParams(vmem_limit_bytes=vmem << 20),
        cost_estimate=pl.CostEstimate(flops=COST, bytes_accessed=COST, transcendentals=0),
    )


def shaped(shape, dtype):
    return jax.ShapeDtypeStruct(shape, dtype)


def column_of(row, size):
    return jnp.broadcast_to(row, (size, size)).T


def sort_matrix(pos_ref, first, size, total):
    lanes = lax.broadcasted_iota(jnp.int32, (128, total), 1).astype(F32)
    parts = []
    for start in range(first, first + size, 128):
        column = column_of(places(pos_ref, start, 128).astype(F32), 128)
        wide = jnp.concatenate([column] * (total // 128), axis=1)
        parts.append(jnp.where(wide == lanes, 1.0, 0.0).astype(BF16))
    return jnp.concatenate(parts, axis=0)


def places(pos_ref, start, size):
    return lax.rem(pos_ref[:, start : start + size], pos_ref.shape[1])


def plan_kernel(head_groups, where_ref, lists_ref, counts_ref, meta_ref):
    blocks, slots = lists_ref.shape
    region, regions, group, heads = where_ref[0], where_ref[1], where_ref[2], head_groups
    counts = [counts_ref[i] for i in range(blocks)]
    for i in range(blocks):
        rank = jnp.int32(0)
        for j in range(blocks):
            if j != i:
                ahead = counts[j] >= counts[i] if j < i else counts[j] > counts[i]
                rank = rank + jnp.where(ahead, 1, 0)
        turn = rank // heads
        side = rank % heads
        side = jnp.where(turn % 2 == 1, heads - 1 - side, side)
        from_me = group - side
        from_me = jnp.where(from_me < 0, from_me + heads, from_me)
        row = from_me * (blocks // heads) + turn
        meta_ref[row, COUNT_COL] = counts[i]
        meta_ref[row, BLOCK_COL] = jnp.int32(i)
        meta_ref[row, GROUP_COL] = group
        entries = []
        own_total = low_total = jnp.int32(0)
        for s in range(slots):
            key = lists_ref[i, s]
            away = key // blocks - region + 1
            away = jnp.where(away < 0, away + regions, away)
            away = jnp.where(away >= regions, away - regions, away)
            entries.append((key % blocks + jnp.where(away == 2, blocks, 0), away))
            live = s < counts[i]
            own_total = own_total + jnp.where((away == 1) & live, 1, 0)
            low_total = low_total + jnp.where((away == 0) & live, 1, 0)
        meta_ref[row, OWN_COL] = own_total
        meta_ref[row, LOW_COL] = low_total
        own_next, low_next, high_next = jnp.int32(0), own_total, own_total + low_total
        for s in range(slots):
            index, away = entries[s]
            to = jnp.where(away == 1, own_next, jnp.where(away == 0, low_next, high_next))

            @pl.when(s < counts[i])
            def _(index=index, to=to):
                meta_ref[row, to] = index

            own_next = own_next + jnp.where(away == 1, 1, 0)
            low_next = low_next + jnp.where(away == 0, 1, 0)
            high_next = high_next + jnp.where(away == 2, 1, 0)


def prep_kernel(pos_ref, rows_ref, gain_ref, normed_ref):
    total = rows_ref.shape[0]
    for first in range(0, total, 512):
        picked = dot_nn(sort_matrix(pos_ref, first, 512, total), rows_ref[...])
        normed_ref[first : first + 512, :] = (picked * row_scale(picked) * gain_ref[...]).astype(BF16)


def sort_kernel(pos_ref, rows_ref, grads_ref, sorted_rows_ref, sorted_grads_ref):
    total = rows_ref.shape[0]
    for first in range(0, total, 512):
        matrix = sort_matrix(pos_ref, first, 512, total)
        sorted_rows_ref[first : first + 512, :] = dot_nn(matrix, rows_ref[...]).astype(BF16)
        sorted_grads_ref[first : first + 512, :] = dot_nn(matrix, grads_ref[...]).astype(BF16)


def chunk(values, who, share):
    out = values[:, :share]
    for start in range(share, values.shape[1], share):
        out = jnp.where(who == start // share, values[:, start : start + share], out)
    return out


def below(group, steps, count):
    who = group + steps
    return jnp.where(who >= count, who - count, who)


def both_heads(rows):
    lane = lax.broadcasted_iota(jnp.int32, rows.shape, 1)
    zero = jnp.zeros_like(rows)
    return jnp.concatenate([jnp.where(lane < HD, rows, zero), jnp.where(lane < HD, zero, rows)], axis=0)


def both_heads_t(rows):
    flipped = rows.T
    row = lax.broadcasted_iota(jnp.int32, flipped.shape, 0)
    zero = jnp.zeros_like(flipped)
    return jnp.concatenate([jnp.where(row < HD, flipped, zero), jnp.where(row < HD, zero, flipped)], axis=1)


def own_heads(wide):
    half = wide.shape[1] // 2
    return jnp.concatenate([wide[:HD, :half], wide[HD:, half:]], axis=0)


def groups_of_eight(tile, op):
    out = tile[:8]
    for start in range(8, tile.shape[0], 8):
        out = op(out, tile[start : start + 8])
    return out


def packed(packs, which):
    size = packs[0].shape[1] // 4
    return jnp.concatenate([ref[:, which * size : (which + 1) * size] for ref in packs], axis=1)


def joined(mine_ref, packs, which):
    return jnp.concatenate([mine_ref[...], packed(packs, which)], axis=1)


def project_keys(rows_ref, wk, wv, keys_ref, values_ref, values_t_ref, base):
    for start in range(0, rows_ref.shape[0], 512):
        at = slice(base + start, base + start + 512)
        here = rows_ref[start : start + 512, :]
        keys_ref[at, :] = dot_nn(here, wk).astype(BF16)
        found = dot_nn(here, wv).astype(BF16)
        values_ref[at, :] = found
        for part in range(4):
            values_t_ref[(base + start) // 128 + part] = found[part * 128 : part * 128 + 128, :].T


def block_rows(ref, indices, cols):
    return jnp.concatenate(
        [ref[pl.ds(pl.multiple_of(index * 128, 128), 128), cols] for index in indices], axis=0
    )


def block_cols(ref, indices, cols):
    return jnp.concatenate([ref[index, cols, :] for index in indices], axis=1)


def by_two(count, step, carried):
    carried = lax.fori_loop(0, count // 2, lambda i, c: step(2 * i, 2, c), carried)
    return lax.fori_loop(0, count % 2, lambda i, c: step(count - 1, 1, c), carried)


def attend(meta_ref, b, first, count, keys_ref, values_t_ref, query_t_ref, keep_ref, acc_ref, old):
    pairs = query_t_ref.shape[0]
    wide = query_t_ref.shape[2]

    def peak_step(slot, size, peaks):
        indices = [meta_ref[b, first + slot + j] for j in range(size)]
        tiles = [
            dot_nn(block_rows(keys_ref, indices, slice(p * PAIR, (p + 1) * PAIR)), query_t_ref[p])
            for p in range(pairs)
        ]
        out = []
        for p in range(pairs):
            for j in range(size):
                keep_ref[slot + j, p] = tiles[p][j * 128 : (j + 1) * 128]
            out.append(jnp.maximum(peaks[p], groups_of_eight(tiles[p], jnp.maximum)))
        return tuple(out)

    if old is None:
        start = (jnp.full((8, wide), -3.0e38, F32),) * pairs
    else:
        start = tuple(jnp.broadcast_to(peak, (8, wide)) for peak, _ in old)
    peaks = by_two(count, peak_step, start)
    peaks = tuple(jnp.max(peak, axis=0, keepdims=True) for peak in peaks)
    totals = []
    for p in range(pairs):
        if old is None:
            acc_ref[p] = jnp.zeros(acc_ref.shape[1:], F32)
            totals.append(jnp.zeros((1, wide), F32))
        else:
            shrink = jnp.exp(old[p][0] - peaks[p])
            acc_ref[p] = acc_ref[p] * shrink
            totals.append(old[p][1] * shrink)

    def sum_step(slot, size, sums):
        indices = [meta_ref[b, first + slot + j] for j in range(size)]
        out = []
        for p in range(pairs):
            cols = slice(p * PAIR, (p + 1) * PAIR)
            tile = jnp.concatenate([jnp.exp(keep_ref[slot + j, p] - peaks[p]) for j in range(size)], axis=0)
            out.append(sums[p] + groups_of_eight(tile, jnp.add))
            acc_ref[p] += dot_nn(block_cols(values_t_ref, indices, cols), tile.astype(BF16))
        return tuple(out)

    sums = by_two(count, sum_step, (jnp.zeros((8, wide), F32),) * pairs)
    return [
        (peaks[p], totals[p] + jnp.sum(sums[p], axis=0, keepdims=True)) for p in range(pairs)
    ]


def own_kernel(
    meta_ref,
    own_ref,
    wq_ref,
    wk_ref,
    wv_ref,
    pack_a,
    pack_b,
    keys_ref,
    values_ref,
    keys_t_ref,
    queries_ref,
    query_t_ref,
    acc_ref,
    peaks_ref,
    sums_ref,
    keep_ref,
    values_t_ref,
):
    block = 128
    pairs = queries_ref.shape[1] // PAIR
    packs = (pack_a, pack_b)
    project_keys(own_ref, joined(wk_ref, packs, 1), joined(wv_ref, packs, 2), keys_ref, values_ref, values_t_ref, 0)
    wq = joined(wq_ref, packs, 0)
    for kb in range(keys_t_ref.shape[0]):
        keys_t_ref[kb] = keys_ref[kb * block : (kb + 1) * block, :].T

    @pl.loop(0, queries_ref.shape[0] // block)
    def _(b):
        first = pl.multiple_of(meta_ref[b, BLOCK_COL] * block, block)
        query = dot_nn(own_ref[pl.ds(first, block), :], wq).astype(BF16)
        query = (query.astype(F32) * (HD ** (-0.5))).astype(BF16)
        queries_ref[pl.ds(pl.multiple_of(b * block, block), block), :] = query
        for p in range(pairs):
            query_t_ref[b, p] = both_heads_t(query[:, p * PAIR : (p + 1) * PAIR])
        found = attend(
            meta_ref,
            b,
            0,
            meta_ref[b, OWN_COL],
            keys_ref,
            values_t_ref,
            query_t_ref.at[b],
            keep_ref,
            acc_ref.at[b],
            None,
        )
        for p in range(pairs):
            at = slice(p * 2 * block, (p + 1) * 2 * block)
            peaks_ref[pl.ds(b, 1), at] = found[p][0]
            sums_ref[pl.ds(b, 1), at] = found[p][1]


def halo_kernel(
    meta_ref,
    low_ref,
    high_ref,
    wk_ref,
    wv_ref,
    pack_a,
    pack_b,
    query_t_ref,
    old_acc_ref,
    peaks_ref,
    sums_ref,
    keys_ref,
    values_ref,
    attended_ref,
    attended_t_ref,
    log_total_ref,
    keep_ref,
    values_t_ref,
    acc_ref,
):
    block = 128
    pairs = query_t_ref.shape[1]
    wk = joined(wk_ref, (pack_a, pack_b), 1)
    wv = joined(wv_ref, (pack_a, pack_b), 2)
    project_keys(low_ref, wk, wv, keys_ref, values_ref, values_t_ref, 0)
    project_keys(high_ref, wk, wv, keys_ref, values_ref, values_t_ref, low_ref.shape[0])

    @pl.loop(0, query_t_ref.shape[0])
    def _(b):
        here = pl.ds(pl.multiple_of(b * block, block), block)
        old = []
        for p in range(pairs):
            at = slice(p * 2 * block, (p + 1) * 2 * block)
            acc_ref[p] = old_acc_ref[b, p]
            old.append((peaks_ref[pl.ds(b, 1), at], sums_ref[pl.ds(b, 1), at]))
        own = meta_ref[b, OWN_COL]
        found = attend(
            meta_ref,
            b,
            own,
            meta_ref[b, COUNT_COL] - own,
            keys_ref,
            values_t_ref,
            query_t_ref.at[b],
            keep_ref,
            acc_ref,
            old,
        )
        for p in range(pairs):
            peak, total = found[p]
            log_total_ref[pl.ds(b, 1), p * 2 * block : (p + 1) * 2 * block] = peak + jnp.log(total)
            rows = own_heads(acc_ref[p] * (1.0 / total)).astype(BF16)
            attended_t_ref[b, p * PAIR : (p + 1) * PAIR, :] = rows
            attended_ref[here, p * PAIR : (p + 1) * PAIR] = rows.T


GELU_A = 0.044715
GELU_B = 0.7978845608028654


def ffn_chunks(norm_ref, grad_ref, chunks):
    def products(at):
        up, down = chunks[at]
        return dot_nn(norm_ref[...], up), dot_nt(grad_ref[...], down)

    totals = None
    coming = products(0)
    for at, (up, down) in enumerate(chunks):
        pre, grad_act = coming
        if at + 1 < len(chunks):
            coming = products(at + 1)
        square = pre * pre
        inner = jnp.tanh(pre * (GELU_B + (GELU_A * GELU_B) * square))
        gate = 0.5 + 0.5 * inner
        active = (pre * gate).astype(BF16)
        slope = gate + pre * (1.0 - inner * inner) * (0.5 * GELU_B + (1.5 * GELU_A * GELU_B) * square)
        grad_pre = (grad_act * slope).astype(BF16)
        found = dot_nn(active, down), dot_nt(grad_pre, up)
        totals = found if totals is None else (totals[0] + found[0], totals[1] + found[1])
    return totals


def ffn_kernel(
    meta_ref,
    ordered_ref,
    grad_ref,
    attended_ref,
    gain_ref,
    wo_ref,
    pack_a,
    pack_b,
    in_ref,
    out_ref,
    hidden_ref,
    grad_rows,
    norm_ref,
    total_ref,
    back_ref,
):
    block = 128
    size = attended_ref.shape[0]
    for b in range(size // block):
        first = pl.multiple_of(meta_ref[b, BLOCK_COL] * block, block)
        hidden_ref[b * block : (b + 1) * block, :] = ordered_ref[pl.ds(first, block), :].astype(F32)
        grad_rows[b * block : (b + 1) * block, :] = grad_ref[pl.ds(first, block), :]
    share = wo_ref.shape[0]
    hidden_in = hidden_ref[...] + dot_nn(attended_ref[:, :share], wo_ref[...])
    hidden_in = hidden_in + dot_nt(attended_ref[:, share:], packed((pack_a, pack_b), 3))
    hidden_ref[...] = hidden_in
    norm_ref[...] = (hidden_in * row_scale(hidden_in) * gain_ref[...]).astype(BF16)
    cuts = [slice(start, start + 512) for start in range(0, in_ref.shape[1], 512)]
    total_ref[...], back_ref[...] = ffn_chunks(
        norm_ref, grad_rows, [(in_ref[:, at], out_ref[at, :]) for at in cuts]
    )


def rest_kernel(
    meta_ref,
    hidden_ref,
    grad_rows,
    norm_ref,
    old_total_ref,
    old_back_ref,
    gain_ref,
    wo_ref,
    pack_a,
    pack_b,
    hidden_a,
    hidden_b,
    mixed_grad_ref,
    out_own_ref,
    hidden_own_ref,
    *refs,
):
    heads = len(refs) + 1
    width = norm_ref.shape[1]
    forward, backward = ffn_chunks(
        norm_ref, grad_rows, [(ref[:width, :], ref[width:, :]) for ref in (hidden_a, hidden_b)]
    )
    hidden_in = hidden_ref[...]
    result = (hidden_in + (old_total_ref[...] + forward)).astype(BF16)
    group = meta_ref[0, GROUP_COL]
    share = out_own_ref.shape[1]
    out_own_ref[...] = chunk(result, group, share)
    scale = row_scale(hidden_in)
    second_norm = hidden_in * scale
    scaled = (old_back_ref[...] + backward) * gain_ref[...]
    hidden_grad = grad_rows[...].astype(F32) + scale * (
        scaled - second_norm * jnp.mean(scaled * second_norm, axis=-1, keepdims=True)
    )
    hidden_own_ref[...] = chunk(hidden_grad, group, share)
    for k in range(1, heads):
        who = below(group, k, heads)
        refs[k - 1][:, :share] = chunk(result, who, share)
        refs[k - 1][:, share:] = chunk(hidden_grad, who, share).astype(BF16)
    narrow = hidden_grad.astype(BF16)
    half = wo_ref.shape[0]
    mixed_grad_ref[:, :half] = dot_nt(narrow, wo_ref[...]).astype(BF16)
    mixed_grad_ref[:, half:] = dot_nn(narrow, packed((pack_a, pack_b), 3)).astype(BF16)


def back_operands(queries_ref, mixed_grad_ref, attended_t_ref, grad_t_ref, deltas_ref):
    block = 128
    pairs = queries_ref.shape[1] // PAIR

    @pl.loop(0, queries_ref.shape[0] // block)
    def _(b):
        here = pl.ds(pl.multiple_of(b * block, block), block)
        for p in range(pairs):
            cols = slice(p * PAIR, (p + 1) * PAIR)
            grad_t = both_heads_t(mixed_grad_ref[here, cols])
            grad_t_ref[b, p] = grad_t
            attended = attended_t_ref[b, cols, :].astype(F32)
            product = grad_t.astype(F32) * jnp.concatenate([attended, attended], axis=1)
            deltas_ref[pl.ds(b, 1), p * 2 * block : (p + 1) * 2 * block] = jnp.sum(product, axis=0, keepdims=True)


def scores_back(
    meta_ref,
    b,
    first,
    count,
    base,
    keys_ref,
    values_ref,
    keys_t_ref,
    operands,
    grad_keys,
    grad_values,
    rows_ref,
    acc_ref,
):
    queries_ref, query_t_ref, mixed_grad_ref, grad_t_ref, deltas_ref, log_total_ref = operands
    block = 128
    pairs = queries_ref.shape[1] // PAIR
    here = pl.ds(pl.multiple_of(b * block, block), block)
    deltas = []
    logs = []
    for p in range(pairs):
        cols = slice(p * PAIR, (p + 1) * PAIR)
        wide = slice(p * 2 * block, (p + 1) * 2 * block)
        rows_ref[0, p] = both_heads(queries_ref[here, cols])
        rows_ref[1, p] = both_heads(mixed_grad_ref[here, cols])
        deltas.append(deltas_ref[pl.ds(b, 1), wide])
        logs.append(log_total_ref[pl.ds(b, 1), wide])

    def step(slot, size, carried):
        indices = [meta_ref[b, first + slot + j] for j in range(size)]
        here = [index - base for index in indices]
        cuts = [slice(p * PAIR, (p + 1) * PAIR) for p in range(pairs)]

        def products(p):
            scores = dot_nn(block_rows(keys_ref, indices, cuts[p]), query_t_ref[b, p])
            return scores, dot_nn(block_rows(values_ref, indices, cuts[p]), grad_t_ref[b, p])

        coming = products(0)
        for p, cols in enumerate(cuts):
            scores, prob_grad = coming
            if p + 1 < pairs:
                coming = products(p + 1)
            probs = jnp.exp(scores - logs[p])
            score_grad = (probs * (prob_grad - deltas[p])).astype(BF16)
            to_values = dot_nn(probs.astype(BF16), rows_ref[1, p])
            to_keys = dot_nn(score_grad, rows_ref[0, p])
            acc_ref[p] += dot_nn(block_cols(keys_t_ref, here, cols), score_grad)
            for j in range(size):
                at = pl.ds(pl.multiple_of(here[j] * block, block), block)
                grad_values[at, cols] += to_values[j * block : (j + 1) * block]
                grad_keys[at, cols] += to_keys[j * block : (j + 1) * block]
        return carried

    by_two(count, step, 0)


def clear_back(grad_keys, grad_values):
    @pl.loop(0, grad_keys.shape[0] // 128)
    def _(kb):
        at = pl.ds(pl.multiple_of(kb * 128, 128), 128)
        grad_keys[at, :] = jnp.zeros((128, grad_keys.shape[1]), F32)
        grad_values[at, :] = jnp.zeros((128, grad_keys.shape[1]), F32)


def project_back(grad_keys, grad_values, wk, wv, start, size):
    at = slice(start, start + size)
    grads = jnp.concatenate([grad_keys[at, :].astype(BF16), grad_values[at, :].astype(BF16)], axis=1)
    return dot_nt(grads, jnp.concatenate([wk, wv], axis=1))


def side_back_kernel(
    side,
    meta_ref,
    keys_ref,
    values_ref,
    queries_ref,
    query_t_ref,
    mixed_grad_ref,
    log_total_ref,
    wk_ref,
    wv_ref,
    pack_a,
    pack_b,
    *refs,
):
    acc_ref, grad_keys, grad_values, keys_t_ref, rows_ref = refs[-5:]
    if side == 0:
        attended_t_ref, *grads, grad_t_ref, deltas_ref = refs[:-5]
        back_operands(queries_ref, mixed_grad_ref, attended_t_ref, grad_t_ref, deltas_ref)
    else:
        grad_t_ref, deltas_ref, old_acc_ref, *grads = refs[:-5]
    operands = queries_ref, query_t_ref, mixed_grad_ref, grad_t_ref, deltas_ref, log_total_ref
    base = side * keys_t_ref.shape[0]
    clear_back(grad_keys, grad_values)

    @pl.loop(0, keys_t_ref.shape[0])
    def _(kb):
        keys_t_ref[kb] = keys_ref[pl.ds(pl.multiple_of((kb + base) * 128, 128), 128), :].T

    @pl.loop(0, queries_ref.shape[0] // 128)
    def _(b):
        own, low = meta_ref[b, OWN_COL], meta_ref[b, LOW_COL]
        acc_ref[b] = jnp.zeros(acc_ref.shape[1:], F32) if side == 0 else old_acc_ref[b]
        scores_back(
            meta_ref,
            b,
            own if side == 0 else own + low,
            low if side == 0 else meta_ref[b, COUNT_COL] - own - low,
            base,
            keys_ref,
            values_ref,
            keys_t_ref,
            operands,
            grad_keys,
            grad_values,
            rows_ref,
            acc_ref.at[b],
        )

    packs = (pack_a, pack_b)
    weights = joined(wk_ref, packs, 1), joined(wv_ref, packs, 2)
    start = 0
    for ref in grads:
        for part in range(0, ref.shape[0], 512):
            ref[part : part + 512, :] = project_back(
                grad_keys, grad_values, *weights, start + part, 512
            ).astype(BF16)
        start += ref.shape[0]


def own_back_kernel(
    meta_ref,
    keys_ref,
    values_ref,
    keys_t_ref,
    queries_ref,
    query_t_ref,
    mixed_grad_ref,
    grad_t_ref,
    deltas_ref,
    log_total_ref,
    old_acc_ref,
    wq_ref,
    wk_ref,
    wv_ref,
    pack_a,
    pack_b,
    own_ref,
    grad_keys,
    grad_values,
    rows_ref,
    acc_ref,
    query_grad,
):
    operands = queries_ref, query_t_ref, mixed_grad_ref, grad_t_ref, deltas_ref, log_total_ref
    block = 128
    rows = own_ref.shape[0]
    pairs = queries_ref.shape[1] // PAIR
    blocks = queries_ref.shape[0] // block
    clear_back(grad_keys, grad_values)

    @pl.loop(0, blocks)
    def _(b):
        acc_ref[...] = old_acc_ref[b]
        scores_back(
            meta_ref,
            b,
            0,
            meta_ref[b, OWN_COL],
            0,
            keys_ref,
            values_ref,
            keys_t_ref,
            operands,
            grad_keys,
            grad_values,
            rows_ref,
            acc_ref,
        )
        for p in range(pairs):
            found = own_heads(acc_ref[p]) * (HD ** (-0.5))
            query_grad[pl.ds(pl.multiple_of(b * block, block), block), p * PAIR : (p + 1) * PAIR] = found.T.astype(BF16)

    packs = (pack_a, pack_b)
    weights = joined(wk_ref, packs, 1), joined(wv_ref, packs, 2)
    for start in range(0, rows, 512):
        own_ref[start : start + 512, :] = project_back(grad_keys, grad_values, *weights, start, 512)
    parts = dot_nt(query_grad[...], joined(wq_ref, packs, 0))
    for b in range(blocks):
        first = pl.multiple_of(meta_ref[b, BLOCK_COL] * block, block)
        own_ref[pl.ds(first, block), :] += parts[b * block : (b + 1) * block]


def term_kernel(offset, meta_ref, own_ref, low_ref, high_ref, normed_ref, term_ref, dots_ref, *send_refs):
    rows, share = term_ref.shape
    heads = len(send_refs) + 1
    group = meta_ref[0, GROUP_COL]
    dot_rows = []
    for start in range(0, rows, 128):
        at = slice(start, start + 128)
        whole = slice(offset + start, offset + start + 128)
        term = own_ref[whole, :] + low_ref[whole, :].astype(F32) + high_ref[at, :].astype(F32)
        dots = jnp.sum(term * normed_ref[whole, :].astype(F32), axis=-1, keepdims=True)
        dot_rows.append(jnp.broadcast_to(dots, (128, 128)).T[:1])
        term_ref[at, :] = chunk(term, group, share)
        for k in range(1, heads):
            send_refs[k - 1][at, :] = chunk(term, below(group, k, heads), share).astype(BF16)
    dots = jnp.concatenate(dot_rows, axis=0)
    dots_ref[...] = dots
    high = dots.astype(BF16)
    low = (dots - high.astype(F32)).astype(BF16)
    wide = min(share, 128)
    tail = jnp.concatenate(
        [half[:, start : start + wide] for half in (high, low) for start in range(0, 128, wide)], axis=0
    )
    if share > wide:
        tail = jnp.concatenate([tail] * (share // wide), axis=1)
    for ref in send_refs:
        ref[rows:, :] = tail


def dots_of(tail):
    wide = min(tail.shape[1], 128)
    count = 128 // wide
    size = tail.shape[0] // (2 * count)
    parts = [tail[i * size : (i + 1) * size, :wide].astype(F32) for i in range(2 * count)]
    sums = [parts[i] + parts[count + i] for i in range(count)]
    return sums[0] if count == 1 else jnp.concatenate(sums, axis=1)


def back_matrix(pos_ref, first, size, total):
    place = lax.broadcasted_iota(jnp.int32, (size, total), 0) + first
    return jnp.where(jnp.broadcast_to(places(pos_ref, 0, total), (size, total)) == place, 1.0, 0.0).astype(BF16)


def place_blocks(meta_ref, refs, all_ref, first_col):
    block = 128
    share = all_ref.shape[1]
    blocks = refs[0].shape[0] // block
    for k, ref in enumerate(refs):
        cols = slice(0, share) if k == 0 else slice(first_col, first_col + share)
        for b in range(blocks):
            first = pl.multiple_of(meta_ref[k * blocks + b, BLOCK_COL] * block, block)
            all_ref[pl.ds(first, block), :] = ref[b * block : (b + 1) * block, cols].astype(all_ref.dtype)


def output_kernel(meta_ref, pos_ref, ordered_ref, gain_ref, hidden_own_ref, *refs):
    out_ref, matrix_ref, base_ref, scale_ref, norm_ref, all_ref = refs[-6:]
    own_ref, *got_refs = refs[:-6]
    place_blocks(meta_ref, [own_ref, *got_refs], all_ref, 0)
    total, share = all_ref.shape
    place_blocks(meta_ref, [hidden_own_ref, *got_refs], base_ref, share)
    for first in range(0, total, 512):
        matrix = back_matrix(pos_ref, first, 512, total)
        matrix_ref[first : first + 512, :] = matrix
        out_ref[first : first + 512, :] = dot_nn(matrix, all_ref[...]).astype(BF16)
    group = meta_ref[0, GROUP_COL]
    gain = chunk(gain_ref[...], group, share)
    for start in range(0, total, 128):
        at = slice(start, start + 128)
        ordered = ordered_ref[at, :].astype(F32)
        scale = row_scale(ordered)
        scale_ref[at, :] = scale * gain
        norm_ref[at, :] = chunk(ordered, group, share) * (scale * scale)


def final_kernel(matrix_ref, base_ref, scale_ref, norm_ref, term_a, dots_a, term_b, dots_b, *refs):
    out_ref, split_ref = refs[-2:]
    total, share = out_ref.shape
    half = total // 2
    others = (len(refs) - 2) // 2
    for i, (term_ref, dots_ref) in enumerate(((term_a, dots_a), (term_b, dots_b))):
        got_refs = refs[i * others : (i + 1) * others]
        dots = dots_ref[...]
        for ref in got_refs:
            dots = dots + dots_of(ref[half:, :])
        dots = dots * (1.0 / (share * (others + 1)))
        for start in range(0, half, 128):
            at = slice(start, start + 128)
            whole = slice(i * half + start, i * half + start + 128)
            mean = column_of(dots[start // 128 : start // 128 + 1], 128)[:, :1]
            term = term_ref[at, :]
            for ref in got_refs:
                term = term + ref[at, :].astype(F32)
            value = base_ref[whole, :] + (term * scale_ref[whole, :] - norm_ref[whole, :] * mean)
            high = value.astype(BF16)
            split_ref[whole, :share] = high
            split_ref[whole, share:] = (value - high.astype(F32)).astype(BF16)
    for first in range(0, total, 512):
        found = dot_nn(matrix_ref[first : first + 512, :], split_ref[...])
        out_ref[first : first + 512, :] = found[:, :share] + found[:, share:]


def local(
    features,
    out_grad,
    bin_order,
    key_lists,
    list_counts,
    attn_gain,
    query_weight,
    key_weight,
    value_weight,
    out_weight,
    ffn_gain,
    ffn_in,
    ffn_out,
):
    rows, width = features.shape
    block_count, slots = key_lists.shape
    block = rows // block_count
    share = query_weight.shape[1]
    hidden = ffn_in.shape[1]
    region = lax.axis_index("elem")
    regions = lax.axis_size("elem")
    group = lax.axis_index("head")
    head_groups = lax.axis_size("head")
    half_count = block_count // head_groups
    mine_rows = rows // head_groups
    forward = [(i, (i + 1) % regions) for i in range(regions)]
    backward = [(target, source) for source, target in forward]
    sibling = [(i, i ^ 1) for i in range(regions)]

    def exchanged(pieces):
        return [
            lax.ppermute(piece, "head", [(i, (i + k) % head_groups) for i in range(head_groups)])
            for k, piece in enumerate(pieces, 1)
        ]

    positions = bin_order.reshape(1, rows)
    gain_one = attn_gain.reshape(1, width)
    gain_two = ffn_gain.reshape(1, width)

    normed = call(prep_kernel, shaped((rows, width), BF16), [VMEM] * 3, vmem=60)(positions, features, gain_one)
    low = lax.ppermute(normed, "elem", forward)
    high = lax.ppermute(normed, "elem", backward)
    meta = pl.pallas_call(
        functools.partial(plan_kernel, head_groups),
        out_shape=shaped((block_count, META_COLS), jnp.int32),
        in_specs=[SMEM] * 3,
        out_specs=SMEM,
    )(jnp.stack([region, jnp.int32(regions), group, group]), key_lists, list_counts)

    ordered, grad_sorted = call(
        sort_kernel, (shaped((rows, width), BF16), shaped((rows, width), BF16)), [VMEM] * 3
    )(positions, features, out_grad)

    projections = (query_weight, key_weight, value_weight)
    if head_groups == 2:

        def my_piece(weight, core, dim):
            size = weight.shape[dim] // 2
            return lax.dynamic_slice_in_dim(weight, core * size, size, dim)

        core, normed = lax.optimization_barrier((region % 2, normed))
        mix = my_piece(out_weight, core, 0).T
        pack = jnp.concatenate([*[my_piece(w, core, 1) for w in projections], mix], axis=1)
        core, pack = lax.optimization_barrier((core, pack))
        (pack_a,) = exchanged([pack])
        hidden_pack = jnp.concatenate([my_piece(ffn_in, core, 1), my_piece(ffn_out, core, 0)], axis=0)
        (hidden_a,) = exchanged([hidden_pack])
        pack_a, meta, ordered, grad_sorted, hidden_pack = lax.optimization_barrier(
            (pack_a, meta, ordered, grad_sorted, hidden_pack)
        )
        pack_b = lax.ppermute(pack_a, "elem", sibling)
    else:

        def pieces(weight, dim):
            size = weight.shape[dim] * head_groups // 4
            whole = lax.all_gather(weight, "head", axis=dim, tiled=True)
            return jnp.split(whole, (2 * size, 3 * size), axis=dim)

        split = [pieces(w, 1) for w in projections]
        mixing = pieces(out_weight, 0)
        projections = tuple(parts[0] for parts in split)
        pack_a, pack_b = (
            jnp.concatenate([*[parts[i] for parts in split], mixing[i].T], axis=1) for i in (1, 2)
        )
        out_weight = mixing[0]
        ffn_in, *up_parts = pieces(ffn_in, 1)
        ffn_out, *down_parts = pieces(ffn_out, 0)
        hidden_a, hidden_b = (jnp.concatenate(parts, axis=0) for parts in zip(up_parts, down_parts))

    heads_width = head_groups * share
    key_value = (*projections[1:], pack_a, pack_b)
    pairs = heads_width // PAIR
    pair_tile = (pairs, PAIR, 2 * block)
    keep = pltpu.VMEM((slots, pairs, block, 2 * block), F32)
    stats = shaped((half_count, 2 * heads_width), F32)
    keys, values, keys_t, queries, query_t, part_acc, part_peaks, part_sums = call(
        own_kernel,
        (
            shaped((rows, heads_width), BF16),
            shaped((rows, heads_width), BF16),
            shaped((block_count, heads_width, block), BF16),
            shaped((mine_rows, heads_width), BF16),
            shaped((half_count,) + pair_tile, BF16),
            shaped((half_count,) + pair_tile, F32),
            stats,
            stats,
        ),
        [SMEM] + [VMEM] * 6,
        scratch=(
            keep,
            pltpu.VMEM((block_count, heads_width, block), BF16),
        ),
        vmem=26,
    )(meta, normed, *projections, pack_a, pack_b)
    halo_keys, halo_values, attended, attended_t, log_total = call(
        halo_kernel,
        (
            shaped((2 * rows, heads_width), BF16),
            shaped((2 * rows, heads_width), BF16),
            shaped((mine_rows, heads_width), BF16),
            shaped((half_count, heads_width, block), BF16),
            stats,
        ),
        [SMEM] + [VMEM] * 10,
        scratch=(
            keep,
            pltpu.VMEM((2 * block_count, heads_width, block), BF16),
            pltpu.VMEM(pair_tile, F32),
        ),
        vmem=30,
    )(meta, low, high, *key_value, query_t, part_acc, part_peaks, part_sums)

    square = shaped((mine_rows, width), F32)
    narrow = shaped((mine_rows, width), BF16)
    if head_groups == 2:
        attended, hidden_a = lax.optimization_barrier((attended, hidden_a))
        hidden_b = lax.ppermute(hidden_a, "elem", sibling)
    hidden_in, grad_rows, norm_two, part_total, part_back = call(
        ffn_kernel,
        (square, narrow, narrow, square, square),
        [SMEM] + [VMEM] * 9,
    )(meta, ordered, grad_sorted, attended, gain_two, out_weight, pack_a, pack_b, ffn_in, ffn_out)
    others = head_groups - 1
    mixed_grad, out_own, hidden_own, *sends = call(
        rest_kernel,
        (
            narrow,
            shaped((mine_rows, share), BF16),
            shaped((mine_rows, share), F32),
            *[shaped((mine_rows, 2 * share), BF16)] * others,
        ),
        [SMEM] + [VMEM] * 11,
    )(
        meta,
        hidden_in,
        grad_rows,
        norm_two,
        part_total,
        part_back,
        gain_two,
        out_weight,
        pack_a,
        pack_b,
        hidden_a,
        hidden_b,
    )
    both_got = exchanged(sends)

    rows_pair = pltpu.VMEM((2, pairs, 2 * block, PAIR), BF16)
    half = rows // 2

    def side_back(side, grads, more, *extra):
        return call(
            functools.partial(side_back_kernel, side),
            (*[shaped((size, width), BF16) for size in grads], *more, shaped((half_count,) + pair_tile, F32)),
            [SMEM] + [VMEM] * (10 + len(extra)),
            scratch=(
                pltpu.VMEM((rows, heads_width), F32),
                pltpu.VMEM((rows, heads_width), F32),
                pltpu.VMEM((block_count, heads_width, block), BF16),
                rows_pair,
            ),
            vmem=24,
        )(meta, halo_keys, halo_values, queries, query_t, mixed_grad, log_total, *key_value, *extra)

    grad_low, grad_t, deltas, part_grad = side_back(
        0, (rows,), (shaped((half_count,) + pair_tile, BF16), stats), attended_t
    )
    from_right = lax.ppermute(grad_low, "elem", backward)
    grad_high_a, grad_high_b, part_grad = side_back(1, (half, half), (), grad_t, deltas, part_grad)
    from_left = [lax.ppermute(grad, "elem", forward) for grad in (grad_high_a, grad_high_b)]
    part_grad, both_got = lax.optimization_barrier((part_grad, both_got))
    grad_own = call(
        own_back_kernel,
        shaped((rows, width), F32),
        [SMEM] + [VMEM] * 15,
        scratch=(
            pltpu.VMEM((rows, heads_width), F32),
            pltpu.VMEM((rows, heads_width), F32),
            rows_pair,
            pltpu.VMEM(pair_tile, F32),
            pltpu.VMEM((mine_rows, heads_width), BF16),
        ),
        vmem=30,
    )(
        meta,
        keys,
        values,
        keys_t,
        queries,
        query_t,
        mixed_grad,
        grad_t,
        deltas,
        log_total,
        part_grad,
        *projections,
        pack_a,
        pack_b,
    )
    tail = 2 * (half // 128) * (128 // min(share, 128))
    terms, got = [], []
    for i in range(2):
        term, dots, *sends = call(
            functools.partial(term_kernel, i * half),
            (
                shaped((half, share), F32),
                shaped((half // 128, 128), F32),
                *[shaped((half + tail, share), BF16)] * others,
            ),
            [SMEM] + [VMEM] * 4,
        )(meta, grad_own, from_right, from_left[i], normed)
        terms += [term, dots]
        got += exchanged(sends)
    columns = shaped((rows, share), F32)
    output, *prepared = call(
        output_kernel,
        (shaped((rows, share), BF16), shaped((rows, rows), BF16), columns, columns, columns),
        [SMEM] + [VMEM] * (4 + head_groups),
        scratch=(pltpu.VMEM((rows, share), BF16),),
    )(meta, positions, ordered, gain_one, hidden_own, out_own, *both_got)
    input_grad = call(
        final_kernel,
        columns,
        [VMEM] * (8 + 2 * others),
        scratch=(pltpu.VMEM((rows, 2 * share), BF16),),
    )(*prepared, *terms, *got)
    return (output, input_grad)


def solution(mesh):
    in_specs = (
        P("elem", None),
        P("elem", None),
        P("elem"),
        P("elem", None),
        P("elem"),
        P(),
        P(None, "head"),
        P(None, "head"),
        P(None, "head"),
        P("head", None),
        P(),
        P(None, "head"),
        P("head", None),
    )
    out_specs = (P("elem", "head"), P("elem", "head"))
    return jax.shard_map(local, mesh=mesh, in_specs=in_specs, out_specs=out_specs, check_vma=False)
```
